32 devices in a mesh: dp: 4 (over z), group: 8 (over y, x, core).
Axes of the slice: x: 2, y: 2, z: 4, core: 2. Of those that a mesh axis runs over, the one named last changes fastest.
Arguments:
- tokens: bfloat16 [128, 160, 768], P(('dp', 'group')), may hold values from -6 to 6
- cotangent: bfloat16 [128, 160, 768], P(('dp', 'group')), may hold values from -6 to 6
- counts: int32 [128], P(('dp', 'group')), may hold values from 96 to 160, as said below
- first_gain: float32 [768], replicated, may hold values from 0.5 to 1.5
- first_shift: float32 [768], replicated, may hold values from -1.75 to 1.75
- joined_weight: bfloat16 [768, 2304], replicated, may hold values from -0.21875 to 0.21875
- joined_bias: float32 [2, 768], replicated, may hold values from -1.75 to 1.75
- merge_weight: bfloat16 [768, 768], replicated, may hold values from -0.75 to 0.75
- merge_bias: float32 [768], replicated, may hold values from -1.75 to 1.75
- second_gain: float32 [768], replicated, may hold values from 0.5 to 1.5
- second_shift: float32 [768], replicated, may hold values from -1.75 to 1.75
- up_weight: bfloat16 [768, 3072], replicated, may hold values from -0.21875 to 0.21875
- up_bias: float32 [3072], replicated, may hold values from -1.75 to 1.75
- down_weight: bfloat16 [3072, 768], replicated, may hold values from -0.109375 to 0.109375
- down_bias: float32 [768], replicated, may hold values from -1.75 to 1.75
Outputs:
- result: bfloat16 [128, 160, 768], P(('dp', 'group'))
- token_grad: bfloat16 [128, 160, 768], P(('dp', 'group'))
- first_gain_grad: float32 [768], replicated
- first_shift_grad: float32 [768], replicated
- joined_weight_grad: float32 [768, 2304], replicated
- joined_bias_grad: float32 [2, 768], replicated
- merge_weight_grad: float32 [768, 768], replicated
- merge_bias_grad: float32 [768], replicated
- second_gain_grad: float32 [768], replicated
- second_shift_grad: float32 [768], replicated
- up_weight_grad: float32 [768, 3072], replicated
- up_bias_grad: float32 [3072], replicated
- down_weight_grad: float32 [3072, 768], replicated
- down_bias_grad: float32 [768], replicated
The draws below stay inside these ranges and needn't reach their ends.
Inputs may be any that keep to these rules, and one draw needn't show every extreme that they name: `counts`: item j of a device is owned by the device with index j // 1 along dp and the same index along group; the items owned by one device hold 512 visible patches together.
All inputs are finite; a program needn't handle non-finite values.
Results may differ from the reference program's by a relative error of at most 0.012.
Values may be sent and summed in bfloat16 or wider, within the bound.
No kernel may reach another device: no remote copies, remote signals or barrier semaphores. Data moves between devices by JAX's collectives and lax.ppermute only.
A program may use at most 256 MiB of HBM per device.

```python
import jax
import jax.numpy as jnp
from jax import lax

D = 768
HEADS = 12
HEAD_DIM = 64
FF = 3072
VIS_MEAN = 128
VIS_SPREAD = 32
ITEM_PEER = 1
VIS_MOST = 160
ITEM_DEV = 4
ITEMS = 128
N_DP = 4
N_GROUP = 8


def draw_counts(key, part):
    delta_key = jax.random.fold_in(key, 12)
    deltas = jax.random.randint(delta_key, (N_GROUP, N_DP, N_DP // 2, ITEM_PEER), -VIS_SPREAD, VIS_SPREAD + 1)
    deltas = deltas.at[:, :, 0, 0].set(VIS_SPREAD)
    paired = jnp.stack([deltas, -deltas], axis=3).reshape(N_GROUP, N_DP, N_DP, ITEM_PEER)
    received = (VIS_MEAN + paired).astype(jnp.int32)
    table = jnp.transpose(received, (2, 0, 1, 3)).reshape(N_DP, N_GROUP, N_DP * ITEM_PEER)
    return table.reshape(-1).astype(jnp.int32)


def block_scale(stream_key, shape, cuts, low, high):
    def one(position, blocks):
        heights = jax.random.uniform(jax.random.fold_in(jax.random.fold_in(stream_key, 6), position), (blocks,), jnp.float32, low / len(cuts), high / len(cuts))
        return jnp.repeat(jnp.exp(heights), shape[position] // blocks).reshape((-1,) + (1,) * (len(shape) - position - 1))

    loudness = one(*cuts[0])
    for cut in cuts[1:]:
        loudness = loudness * one(*cut)
    return loudness


def scatter_about(own_key, shape, scale, limit, split=(), held_as=jnp.bfloat16):
    drawn = scale * jax.random.normal(own_key, shape, jnp.float32)
    if split:
        drawn = drawn * block_scale(own_key, shape, split, -0.22, 0.18)
    return jnp.clip(drawn, -limit, limit).astype(held_as)


def setup_inputs(seed: int = 0) -> dict:
    streams_of = jax.random.split(jax.random.key(seed), 16)
    return {
        "tokens": scatter_about(streams_of[0], (ITEMS, VIS_MOST, D), 1.0, 6.0, ((0, 32),)),
        "cotangent": scatter_about(streams_of[1], (ITEMS, VIS_MOST, D), 1.0, 6.0, ((0, 32),)),
        "counts": draw_counts(jax.random.fold_in(streams_of[15], 71), 0),
        "first_gain": jnp.clip(1.0 + 0.1 * jax.random.normal(streams_of[3], (D,), jnp.float32), 0.5, 1.5),
        "first_shift": scatter_about(streams_of[4], (D,), 0.3, 1.75, (), jnp.float32),
        "joined_weight": scatter_about(streams_of[5], (D, 3 * D), D ** -0.5, 0.21875),
        "joined_bias": scatter_about(streams_of[6], (2, D), 0.3, 1.75, (), jnp.float32),
        "merge_weight": scatter_about(streams_of[7], (D, D), HEAD_DIM ** -0.5, 0.75),
        "merge_bias": scatter_about(streams_of[8], (D,), 0.3, 1.75, (), jnp.float32),
        "second_gain": jnp.clip(1.0 + 0.1 * jax.random.normal(streams_of[9], (D,), jnp.float32), 0.5, 1.5),
        "second_shift": scatter_about(streams_of[10], (D,), 0.3, 1.75, (), jnp.float32),
        "up_weight": scatter_about(streams_of[11], (D, FF), D ** -0.5, 0.21875),
        "up_bias": scatter_about(streams_of[12], (FF,), 0.3, 1.75, (), jnp.float32),
        "down_weight": scatter_about(streams_of[13], (FF, D), FF ** -0.5, 0.109375),
        "down_bias": scatter_about(streams_of[14], (D,), 0.3, 1.75, (), jnp.float32),
    }


EPS = 1e-06
NEG = -1e+30

@jax.custom_vjp
def low(v):
    return lax.optimization_barrier(v.astype(jnp.bfloat16)).astype(jnp.float32)

@jax.custom_vjp
def low_back(v):
    return v

def low_keep(v):
    return (low(v), None)

def low_pass(kept, grad):
    return (grad,)

def back_keep(v):
    return (v, None)

def back_low(kept, grad):
    return (low(grad),)
low.defvjp(low_keep, low_pass)
low_back.defvjp(back_keep, back_low)

def norm_rows(matrix, gain_row, shift_row):
    row_mean = lax.optimization_barrier(jnp.mean(matrix, axis=-1, keepdims=True))
    centred = matrix - row_mean
    variance = lax.optimization_barrier(jnp.mean(centred * centred, axis=-1, keepdims=True))
    return centred * lax.rsqrt(variance + EPS) * gain_row + shift_row

def forward(weights, inputs, visible):
    first_gain, first_shift, joined_weight, joined_bias, merge_weight, merge_bias, second_gain, second_shift, up_weight, up_bias, down_weight, down_bias = weights
    exact = lax.Precision.HIGHEST
    item_count, slot_count, features = inputs.shape
    factor = HEAD_DIM ** (-0.5)
    normed = low(norm_rows(inputs, first_gain, first_shift))
    bias_full = jnp.concatenate([joined_bias[0], jnp.zeros((features,), jnp.float32), joined_bias[1]])
    joined = jnp.einsum('ild,de->ile', normed, joined_weight, precision=exact) + bias_full
    joined = low(low_back(joined)).reshape(item_count, slot_count, 3, HEADS, HEAD_DIM)
    queries = joined[:, :, 0]
    key_rows = joined[:, :, 1]
    values = joined[:, :, 2]
    scores = low_back(jnp.einsum('iqhd,ikhd->ihqk', queries, key_rows, precision=exact) * factor)
    scores = jnp.where(visible[:, None, None, :] > 0.5, scores, NEG)
    probs = low(jax.nn.softmax(scores, axis=-1))
    mixture = jnp.einsum('ihqk,ikhd->iqhd', probs, values, precision=exact)
    mixture = low(low_back(mixture.reshape(item_count, slot_count, features)))
    branch = low_back(jnp.einsum('ild,de->ile', mixture, merge_weight, precision=exact) + merge_bias)
    middle = inputs + branch
    second = low(norm_rows(middle, second_gain, second_shift))
    hidden = low_back(jnp.einsum('ild,df->ilf', second, up_weight, precision=exact) + up_bias)
    active = low(jax.nn.gelu(hidden, approximate=False))
    outer = low_back(jnp.einsum('ilf,fd->ild', active, down_weight, precision=exact) + down_bias)
    return (middle + outer) * visible[..., None]

def reference(tokens, cotangent, counts, first_gain, first_shift, joined_weight, joined_bias, merge_weight, merge_bias, second_gain, second_shift, up_weight, up_bias, down_weight, down_bias):
    weights = tuple((arr.astype(jnp.float32) for arr in (first_gain, first_shift, joined_weight, joined_bias, merge_weight, merge_bias, second_gain, second_shift, up_weight, up_bias, down_weight, down_bias)))
    blocks = ITEMS // ITEM_DEV
    slots = jnp.arange(VIS_MOST, dtype=jnp.int32)
    visible = (slots[None, :] < counts[:, None]).astype(jnp.float32)
    stacked_tokens = tokens.astype(jnp.float32).reshape(blocks, ITEM_DEV, VIS_MOST, D)
    stacked_cot = cotangent.astype(jnp.float32).reshape(blocks, ITEM_DEV, VIS_MOST, D)
    stacked_visible = visible.reshape(blocks, ITEM_DEV, VIS_MOST)

    def advance(totals, pieces):
        block_tokens, block_cot, block_visible = pieces
        outputs, pullback = jax.vjp(lambda params, inputs: forward(params, inputs, block_visible), weights, block_tokens)
        grad_params, grad_inputs = pullback(block_cot)
        totals = tuple((left + right for left, right in zip(totals, grad_params)))
        return (totals, (outputs.astype(jnp.bfloat16), grad_inputs.astype(jnp.bfloat16)))
    starting = tuple((jnp.zeros_like(arr) for arr in weights))
    totals, (outputs, grad_tokens) = lax.scan(advance, starting, (stacked_tokens, stacked_cot, stacked_visible))
    return (outputs.reshape(ITEMS, VIS_MOST, D), grad_tokens.reshape(ITEMS, VIS_MOST, D), totals[0], totals[1], totals[2], totals[3], totals[4], totals[5], totals[6], totals[7], totals[8], totals[9], totals[10], totals[11])
```

```python
import math

import jax
import jax.numpy as jnp
from jax import lax
from jax.experimental import pallas as pl
from jax.experimental.pallas import tpu as pltpu
from jax.sharding import PartitionSpec as P

D = 768
HEADS = 12
HEAD_DIM = 64
FF = 3072
PAIRS = HEADS // 2
LANES = 2 * HEAD_DIM
EPS = 1e-06
NEG = -1e30
BF = jnp.bfloat16
F32 = jnp.float32
FACTOR = HEAD_DIM ** (-0.5)
BLOCKS = 16
BROWS = D // BLOCKS


def dot(a, b):
    return jnp.dot(a, b, preferred_element_type=F32)


def dot_t(a, b):
    return lax.dot_general(a, b, (((1,), (1,)), ((), ())), preferred_element_type=F32)


def t_dot(a, b):
    return lax.dot_general(a, b, (((0,), (0,)), ((), ())), preferred_element_type=F32)


def stats(x):
    centred = x - jnp.mean(x, axis=-1, keepdims=True)
    rstd = lax.rsqrt(jnp.mean(centred * centred, axis=-1, keepdims=True) + EPS)
    return centred * rstd, rstd


def params(limit=56):
    return pltpu.CompilerParams(vmem_limit_bytes=limit * 1024 * 1024)


def cost(flops, nbytes, trans=0):
    return pl.CostEstimate(flops=int(flops), bytes_accessed=int(nbytes), transcendentals=int(trans))


def full(shape):
    return pl.BlockSpec(shape, lambda *_: (0,) * len(shape))


def head_masks(rows):
    lane = lax.broadcasted_iota(jnp.int32, (rows, LANES), 1)
    return lane < HEAD_DIM


def stack_heads(pair, low):
    zero = jnp.zeros_like(pair)
    return jnp.concatenate([jnp.where(low, pair, zero), jnp.where(low, zero, pair)], axis=0)


def first_body(
    slots,
    counts_ref,
    tok_ref,
    cot_ref,
    g1_ref,
    s1_ref,
    wj_ref,
    jb_ref,
    wm_ref,
    mb_ref,
    g2_ref,
    s2_ref,
    normed_ref,
    joined_ref,
    probs_ref,
    mix_ref,
    middle_ref,
    second_ref,
    gout_ref,
):
    step = pl.program_id(0)
    rows = tok_ref.shape[0]
    items = rows // slots
    x = tok_ref[...].astype(F32)
    xhat, _ = stats(x)
    normed = (xhat * g1_ref[...] + s1_ref[...]).astype(BF)
    normed_ref[...] = normed
    for third in range(3):
        cols = slice(third * D, (third + 1) * D)
        part = dot(normed, wj_ref[:, cols])
        if third == 0:
            part = part + jb_ref[0:1, :]
        if third == 2:
            part = part + jb_ref[1:2, :]
        joined_ref[:, cols] = part.astype(BF)
    low = head_masks(slots)
    key_slot = lax.broadcasted_iota(jnp.int32, (2 * slots, slots), 1)
    row_slot = lax.broadcasted_iota(jnp.int32, (slots, D), 0)

    def one(item, carry):
        count = counts_ref[step * items + item]
        here = pl.ds(pl.multiple_of(item * slots, 16), slots)
        seen = row_slot < count
        cot = cot_ref[here, :]
        gout_ref[here, :] = jnp.where(seen, cot, jnp.zeros_like(cot))
        allowed = key_slot < count
        for pair in range(PAIRS):
            cols = slice(pair * LANES, (pair + 1) * LANES)
            q = stack_heads(joined_ref[here, cols], low)
            k = joined_ref[here, D + pair * LANES : D + (pair + 1) * LANES]
            v = joined_ref[here, 2 * D + pair * LANES : 2 * D + (pair + 1) * LANES]
            scores = jnp.where(allowed, dot_t(q, k) * FACTOR, NEG)
            raised = jnp.exp(scores - jnp.max(scores, axis=-1, keepdims=True))
            soft = (raised / jnp.sum(raised, axis=-1, keepdims=True)).astype(BF)
            probs_ref[item, pair] = soft
            mixed = dot(soft, v)
            mix_ref[here, cols] = jnp.where(low, mixed[:slots], mixed[slots:]).astype(BF)
        return carry

    lax.fori_loop(0, items, one, 0)
    middle = x + dot(mix_ref[...], wm_ref[...]) + mb_ref[...]
    middle_ref[...] = middle
    xhat, _ = stats(middle)
    second_ref[...] = (xhat * g2_ref[...] + s2_ref[...]).astype(BF)


def first_call(group, slots, counts, tok, cot, g1, s1, wj, jb, wm, mb, g2, s2):
    total = tok.shape[0]
    rows = group * slots
    steps = total // rows
    row = lambda width: pl.BlockSpec((rows, width), lambda i, c: (i, 0))
    out = lambda width, dt: jax.ShapeDtypeStruct((total, width), dt)
    return pl.pallas_call(
        lambda *refs: first_body(slots, *refs),
        grid_spec=pltpu.PrefetchScalarGridSpec(
            num_scalar_prefetch=1,
            grid=(steps,),
            in_specs=[row(D), row(D)]
            + [full(a.shape) for a in (g1, s1, wj, jb, wm, mb, g2, s2)],
            out_specs=[
                row(D),
                row(3 * D),
                pl.BlockSpec((group, PAIRS, 2 * slots, slots), lambda i, c: (i, 0, 0, 0)),
                row(D),
                row(D),
                row(D),
                row(D),
            ],
        ),
        out_shape=[
            out(D, BF),
            out(3 * D, BF),
            jax.ShapeDtypeStruct((total // slots, PAIRS, 2 * slots, slots), BF),
            out(D, BF),
            out(D, F32),
            out(D, BF),
            out(D, BF),
        ],
        compiler_params=params(),
        cost_estimate=cost(2 * total * D * D * 4 * 2, 20e6),
        name="attn_fwd",
    )(counts, tok, cot, g1, s1, wj, jb, wm, mb, g2, s2)


def put_blocks(ref, which, mask, value):
    for k in range(BLOCKS):
        ref[which, k ^ mask] = value[k * BROWS : (k + 1) * BROWS, :].astype(BF)


def quarter_body(chunk, ids_ref, sec_ref, gout_ref, up_ref, ub_ref, down_ref, *rest):
    act_ref, gh_ref, grad_ref = rest[-3:]
    rows = sec_ref.shape[0]
    chunk = rows // chunk
    for part in range(rows // chunk):
        here = slice(part * chunk, (part + 1) * chunk)
        hidden = dot(sec_ref[here, :], up_ref[...]) + ub_ref[...]
        grad_act = dot_t(gout_ref[here, :], down_ref[...])
        cdf = 0.5 + 0.5 * lax.erf(hidden * (0.5**0.5))
        act_ref[0, here, :] = (hidden * cdf).astype(BF)
        slope = cdf + hidden * (jnp.exp(-0.5 * hidden * hidden) * ((2 * math.pi) ** -0.5))
        gh_ref[0, here, :] = (grad_act * slope).astype(BF)
    put_blocks(grad_ref, 0, ids_ref[0], t_dot(act_ref[0], gout_ref[...]))
    put_blocks(grad_ref, 1, ids_ref[1], t_dot(sec_ref[...], gh_ref[0]))


def quarter_call(call, ids, second, gout, up, ub, down, kept):
    total = second.shape[0]
    quarter = lambda ids: ids[4 + call]
    in_specs = [
        full((total, D)),
        full((total, D)),
        pl.BlockSpec((D, D), lambda i, ids: (0, quarter(ids))),
        pl.BlockSpec((1, D), lambda i, ids: (0, quarter(ids))),
        pl.BlockSpec((D, D), lambda i, ids: (quarter(ids), 0)),
    ]
    args = [ids, second, gout, up, ub, down]
    aliases = {}
    if kept is not None:
        in_specs += [pl.BlockSpec(memory_space=pl.ANY)] * 2
        args += list(kept)
        aliases = {6: 0, 7: 1}
    slab = pl.BlockSpec((1, total, D), lambda i, ids: (call, 0, 0))
    return pl.pallas_call(
        lambda *refs: quarter_body(2, *refs),
        grid_spec=pltpu.PrefetchScalarGridSpec(
            num_scalar_prefetch=1,
            grid=(1,),
            in_specs=in_specs,
            out_specs=[slab, slab, full((2, BLOCKS, BROWS, D))],
        ),
        out_shape=[
            jax.ShapeDtypeStruct((4, total, D), BF),
            jax.ShapeDtypeStruct((4, total, D), BF),
            jax.ShapeDtypeStruct((2, BLOCKS, BROWS, D), BF),
        ],
        input_output_aliases=aliases,
        compiler_params=params(),
        cost_estimate=cost(8 * total * D * D * 2, 12e6),
        name=f"mlp_{call}",
    )(*args)


def middle_body(
    slots,
    counts_ref,
    ids_ref,
    act_ref,
    gh_ref,
    down_ref,
    up_ref,
    mid_ref,
    gout_ref,
    db_ref,
    g2_ref,
    wm_ref,
    result_ref,
    gmid_ref,
    branch_ref,
    gmix_ref,
    small_ref,
    outer_ref,
    g_ref,
):
    step = pl.program_id(0)
    rows = mid_ref.shape[0]
    items = rows // slots
    outer = dot(act_ref[0], down_ref[...])
    g = dot_t(gh_ref[0], up_ref[...])
    sums = jnp.sum(gh_ref[0].astype(F32), axis=0, keepdims=True)
    small_ref[pl.ds(ids_ref[4 + step], 1), :] = sums

    @pl.when(step == 0)
    def _():
        outer_ref[...] = outer
        g_ref[...] = g

    @pl.when(step > 0)
    def _():
        outer_ref[...] += outer
        g_ref[...] += g

    @pl.when(step == 3)
    def _():
        row_slot = lax.broadcasted_iota(jnp.int32, (slots, D), 0)

        def one(item, sums):
            here = pl.ds(pl.multiple_of(item * slots, 16), slots)
            seen = row_slot < counts_ref[item]
            middle = mid_ref[here, :]
            total = middle + outer_ref[here, :] + db_ref[...]
            result_ref[here, :] = jnp.where(seen, total, 0.0).astype(BF)
            gout = gout_ref[here, :].astype(F32)
            xhat, rstd = stats(middle)
            g = g_ref[here, :]
            e = g * g2_ref[...]
            mean_e = jnp.mean(e, axis=-1, keepdims=True)
            mean_x = jnp.mean(e * xhat, axis=-1, keepdims=True)
            grad = gout + rstd * (e - mean_e - xhat * mean_x)
            gmid_ref[here, :] = grad
            branch = grad.astype(BF)
            branch_ref[here, :] = branch
            row = lambda a: jnp.sum(a, axis=0, keepdims=True)
            return (
                sums[0] + row(gout),
                sums[1] + row(g * xhat),
                sums[2] + row(g),
                sums[3] + row(branch.astype(F32)),
            )

        zero = jnp.zeros((1, D), F32)
        sums = lax.fori_loop(0, items, one, (zero,) * 4)
        for k in range(4):
            small_ref[4 + k : 5 + k, :] = sums[k]
        gmix_ref[...] = dot_t(branch_ref[...], wm_ref[...]).astype(BF)


def middle_call(slots, counts, ids, act, gh, down, up, mid, gout, db, g2, wm):
    total = mid.shape[0]
    whole = full((total, D))
    return pl.pallas_call(
        lambda *refs: middle_body(slots, *refs),
        grid_spec=pltpu.PrefetchScalarGridSpec(
            num_scalar_prefetch=2,
            grid=(4,),
            in_specs=[
                pl.BlockSpec((1, total, D), lambda i, c, ids: (i, 0, 0)),
                pl.BlockSpec((1, total, D), lambda i, c, ids: (i, 0, 0)),
                pl.BlockSpec((D, D), lambda i, c, ids: (ids[4 + i], 0)),
                pl.BlockSpec((D, D), lambda i, c, ids: (0, ids[4 + i])),
                whole,
                whole,
                full((1, D)),
                full((1, D)),
                full((D, D)),
            ],
            out_specs=[whole, whole, whole, whole, full((8, D))],
            scratch_shapes=[pltpu.VMEM((total, D), F32), pltpu.VMEM((total, D), F32)],
        ),
        out_shape=[
            jax.ShapeDtypeStruct((total, D), BF),
            jax.ShapeDtypeStruct((total, D), F32),
            jax.ShapeDtypeStruct((total, D), BF),
            jax.ShapeDtypeStruct((total, D), BF),
            jax.ShapeDtypeStruct((8, D), F32),
        ],
        compiler_params=params(),
        cost_estimate=cost(2 * total * D * D * 9, 25e6),
        name="mlp_back",
    )(counts, ids, act, gh, down, up, mid, gout, db, g2, wm)


def attn_back_body(joined_ref, probs_ref, gmix_ref, grad_ref):
    slots = joined_ref.shape[0]
    low = head_masks(slots)
    for pair in range(PAIRS):
        cols = slice(pair * LANES, (pair + 1) * LANES)
        q = stack_heads(joined_ref[:, cols], low)
        k = joined_ref[:, D + pair * LANES : D + (pair + 1) * LANES]
        v = joined_ref[:, 2 * D + pair * LANES : 2 * D + (pair + 1) * LANES]
        out = stack_heads(gmix_ref[:, cols], low)
        low_soft = probs_ref[0, pair]
        soft = low_soft.astype(F32)
        grad_probs = dot_t(out, v)
        mean = jnp.sum(soft * grad_probs, axis=-1, keepdims=True)
        scores = (soft * (grad_probs - mean)).astype(BF)
        gq = dot(scores, k) * FACTOR
        grad_ref[:, cols] = jnp.where(low, gq[:slots], gq[slots:]).astype(BF)
        grad_ref[:, D + pair * LANES : D + (pair + 1) * LANES] = (
            t_dot(scores, q) * FACTOR
        ).astype(BF)
        grad_ref[:, 2 * D + pair * LANES : 2 * D + (pair + 1) * LANES] = t_dot(
            low_soft, out
        ).astype(BF)


def attn_back_call(slots, joined, probs, gmix):
    total = joined.shape[0]
    row = lambda width: pl.BlockSpec((slots, width), lambda i: (i, 0))
    return pl.pallas_call(
        attn_back_body,
        grid=(total // slots,),
        in_specs=[
            row(3 * D),
            pl.BlockSpec((1, PAIRS, 2 * slots, slots), lambda i: (i, 0, 0, 0)),
            row(D),
        ],
        out_specs=row(3 * D),
        out_shape=jax.ShapeDtypeStruct((total, 3 * D), BF),
        compiler_params=params(),
        cost_estimate=cost(total * slots * 256 * 6 * 8, 12e6),
        name="attn_bwd",
    )(joined, probs, gmix)


def attn_grad_body(ids_ref, normed_ref, mix_ref, grad_ref, branch_ref, out_ref):
    half = BLOCKS // 2

    def put(which, base, mask, value):
        for k in range(half):
            out_ref[which, (base + k) ^ mask] = value[k * BROWS : (k + 1) * BROWS, :].astype(BF)

    normed = normed_ref[...]
    put(0, 0, ids_ref[0], t_dot(normed, grad_ref[:, :D]))
    put(0, half, ids_ref[0], t_dot(normed, grad_ref[:, D : 2 * D]))
    put(1, 0, ids_ref[1], t_dot(normed, grad_ref[:, 2 * D :]))
    put(1, half, ids_ref[1], t_dot(mix_ref[...], branch_ref[...]))


def attn_grad_call(call, ids, normed, mix, grad, branch):
    total = normed.shape[0]
    half = pl.BlockSpec((total, D // 2), lambda i, ids: (0, ids[8 + call]))
    return pl.pallas_call(
        attn_grad_body,
        grid_spec=pltpu.PrefetchScalarGridSpec(
            num_scalar_prefetch=1,
            grid=(1,),
            in_specs=[half, half, full((total, 3 * D)), full((total, D))],
            out_specs=full((2, BLOCKS, BROWS, D)),
        ),
        out_shape=jax.ShapeDtypeStruct((2, BLOCKS, BROWS, D), BF),
        compiler_params=params(),
        cost_estimate=cost(2 * total * D * D * 2, 8e6),
        name=f"attn_grad_{call}",
    )(ids, normed, mix, grad, branch)


def last_body(slots, grad_ref, wj_ref, tok_ref, gmid_ref, g1_ref, out_ref, small_ref, g_ref):
    rows = tok_ref.shape[0]
    items = rows // slots
    g_ref[...] = dot_t(grad_ref[...], wj_ref[...])

    def one(item, sums):
        here = pl.ds(pl.multiple_of(item * slots, 16), slots)
        xhat, rstd = stats(tok_ref[here, :].astype(F32))
        g = g_ref[here, :]
        e = g * g1_ref[...]
        mean_e = jnp.mean(e, axis=-1, keepdims=True)
        mean_x = jnp.mean(e * xhat, axis=-1, keepdims=True)
        out_ref[here, :] = (gmid_ref[here, :] + rstd * (e - mean_e - xhat * mean_x)).astype(BF)
        row = lambda a: jnp.sum(a, axis=0, keepdims=True)
        return (
            sums[0] + row(grad_ref[here, :D].astype(F32)),
            sums[1] + row(grad_ref[here, 2 * D :].astype(F32)),
            sums[2] + row(g * xhat),
            sums[3] + row(g),
        )

    zero = jnp.zeros((1, D), F32)
    sums = lax.fori_loop(0, items, one, (zero,) * 4)
    for k in range(4):
        small_ref[k : k + 1, :] = sums[k]
    small_ref[4:8, :] = jnp.zeros((4, D), F32)


def last_call(slots, grad, wj, tok, gmid, g1):
    total = tok.shape[0]
    return pl.pallas_call(
        lambda *refs: last_body(slots, *refs),
        grid=(1,),
        in_specs=[full(a.shape) for a in (grad, wj, tok, gmid, g1)],
        out_specs=[full((total, D)), full((8, D))],
        out_shape=[
            jax.ShapeDtypeStruct((total, D), BF),
            jax.ShapeDtypeStruct((8, D), F32),
        ],
        scratch_shapes=[pltpu.VMEM((total, D), F32)],
        compiler_params=params(),
        cost_estimate=cost(2 * total * D * D * 3, 12e6),
        name="first_back",
    )(grad, wj, tok, gmid, g1)


def finish_mlp_body(groups, ids_ref, in_ref, *rest):
    for ab, out_ref in enumerate(rest[-2:]):
        mask = ids_ref[ab] & (groups - 1)
        for k in range(groups):
            out_ref[k * BROWS : (k + 1) * BROWS, :] = in_ref[ab, k ^ mask].astype(F32)


def finish_attn_body(ids_ref, in_ref, *rest):
    joined_ref, merge_ref = rest[-2:]
    half = BLOCKS // 2
    for ab in range(2):
        mask = ids_ref[ab] & (BLOCKS - 1)
        for i in range(BLOCKS):
            block = in_ref[ab, i ^ mask].astype(F32)
            third, k = 2 * ab + i // half, i % half
            rows = slice(k * BROWS, (k + 1) * BROWS)
            if third < 3:
                joined_ref[rows, third * D : (third + 1) * D] = block
            else:
                merge_ref[rows, :] = block


def finish_call(kind, which, ids, blocks, kept):
    groups = 8 if kind < 2 else BLOCKS
    steps = BLOCKS // groups
    top = lambda ids: ids[3] ^ which

    def place(ab):
        def index(i, ids):
            at = ((ids[ab] & (BLOCKS - 1)) // groups) ^ i
            if ab == 0:
                return ((2 * kind + top(ids)) * steps + at, 0)
            return (at, 2 * kind + top(ids))

        return index

    in_specs = [pl.BlockSpec((2, groups, BROWS, D), lambda i, ids: (0, i, 0, 0))]
    args = [ids, blocks]
    aliases = {}
    if kept is not None:
        in_specs += [pl.BlockSpec(memory_space=pl.ANY)] * 2
        args += list(kept)
        aliases = {2: 0, 3: 1}
    if kind < 2:
        body = lambda *refs: finish_mlp_body(groups, *refs)
        out_specs = [pl.BlockSpec((groups * BROWS, D), place(ab)) for ab in range(2)]
        shapes = [(FF, D), (D, FF)]
    else:
        body = finish_attn_body
        out_specs = [
            pl.BlockSpec((D // 2, 3 * D), lambda i, ids: (top(ids), 0)),
            pl.BlockSpec((D // 2, D), lambda i, ids: (top(ids), 0)),
        ]
        shapes = [(D, 3 * D), (D, D)]
    return pl.pallas_call(
        body,
        grid_spec=pltpu.PrefetchScalarGridSpec(
            num_scalar_prefetch=1, grid=(steps,), in_specs=in_specs, out_specs=out_specs
        ),
        out_shape=[jax.ShapeDtypeStruct(s, F32) for s in shapes],
        input_output_aliases=aliases,
        compiler_params=params(32),
        cost_estimate=cost(0, 7e6),
        name=f"finish_{kind}_{which}",
    )(*args)


def stage_lists(sizes):
    bits = {axis: [(axis, b) for b in range(size.bit_length() - 1)] for axis, size in sizes.items()}
    dp, group = bits["dp"], bits["group"]
    if len(dp) == 2 and len(group) == 3:
        order = group + dp
    else:
        order = [dp[0], group[0], group[-1]] + dp[1:] + group[1:-1]
    return order[0], order[1:3], order[3:]


def swap(value, stage, sizes):
    axis, bit = stage
    return lax.ppermute(value, axis, [(i, i ^ (1 << bit)) for i in range(sizes[axis])])


def add(a, b):
    return (a.astype(F32) + b.astype(F32)).astype(BF)


def bit_of(stage):
    return (lax.axis_index(stage[0]) >> stage[1]) & 1


def reduce_chunk(keep, send, plan, sizes):
    first, pair, rest = plan
    got = swap(send, first, sizes)
    halves = []
    for ab in range(2):
        stages = pair if ab == 0 else pair[::-1]
        mine, theirs = keep[ab], got[ab]
        for stage in stages:
            n = mine.shape[0] // 2
            out = add(mine[n:], theirs[n:])
            mine = add(mine[:n], theirs[:n])
            theirs = swap(out, stage, sizes)
        halves.append(add(mine, theirs))
    mine = jnp.stack(halves)
    for at, stage in enumerate(rest):
        if at < 2:
            n = mine.shape[1] // 2
            mine = add(mine[:, :n], swap(mine[:, n:], stage, sizes))
        else:
            n = mine.shape[2] // 2
            high = bit_of(stage) == 1
            out = jnp.where(high, mine[:, :, :n], mine[:, :, n:])
            mine = jnp.where(high, mine[:, :, n:], mine[:, :, :n])
            mine = add(mine, swap(out, stage, sizes))
    return mine


def gather_chunk(mine, plan, sizes):
    first, pair, rest = plan
    for at in reversed(range(len(rest))):
        got = swap(mine, rest[at], sizes)
        if at < 2:
            mine = jnp.concatenate([mine, got], axis=1)
        else:
            high = bit_of(rest[at]) == 1
            mine = jnp.concatenate(
                [jnp.where(high, got, mine), jnp.where(high, mine, got)], axis=2
            )
    halves = []
    for ab in range(2):
        stages = pair if ab == 0 else pair[::-1]
        own = mine[ab]
        for stage in reversed(stages):
            own = jnp.concatenate([own, swap(own, stage, sizes)], axis=0)
        halves.append(own)
    own = jnp.stack(halves)
    return own, swap(own, first, sizes)


def solution(mesh):
    sizes = dict(mesh.shape)
    plan = stage_lists(sizes)

    def shards(
        tokens,
        cotangent,
        counts,
        first_gain,
        first_shift,
        joined_weight,
        joined_bias,
        merge_weight,
        merge_bias,
        second_gain,
        second_shift,
        up_weight,
        up_bias,
        down_weight,
        down_bias,
    ):
        items, slots, features = tokens.shape
        total = items * slots
        row = lambda a: a.reshape(1, -1)
        tok = tokens.reshape(total, features)
        cot = cotangent.reshape(total, features)
        counts = counts.astype(jnp.int32)
        first, pair, rest = plan
        masks = []
        for two in (pair, pair[::-1]):
            mask = bit_of(first)
            for stage in list(two) + list(rest[:2]):
                mask = 2 * mask + bit_of(stage)
            masks.append(mask)
        core = bit_of(first)
        other = 1 - core
        ids = jnp.stack(
            [masks[0], masks[1], core, core, other, core, 2 + other, 2 + core, other, core]
        ).astype(jnp.int32)
        low_ids = ids.at[0].set(ids[0] & (BLOCKS - 1)).at[1].set(ids[1] & (BLOCKS - 1))

        normed, joined, probs, mix, middle, second, gout = first_call(
            4,
            slots,
            counts,
            tok,
            cot,
            row(first_gain),
            row(first_shift),
            joined_weight,
            joined_bias,
            merge_weight,
            row(merge_bias),
            row(second_gain),
            row(second_shift),
        )
        kept = None
        pieces = []
        for call in range(4):
            act, gh, grad = quarter_call(
                call, low_ids, second, gout, up_weight, row(up_bias), down_weight, kept
            )
            kept = (act, gh)
            pieces.append(grad)
        result, gmid, branch, gmix, small_a = middle_call(
            slots,
            counts,
            low_ids,
            act,
            gh,
            down_weight,
            up_weight,
            middle,
            gout,
            row(down_bias),
            row(second_gain),
            merge_weight,
        )
        grad_joined = attn_back_call(slots, joined, probs, gmix)
        for call in range(2):
            pieces.append(attn_grad_call(call, low_ids, normed, mix, grad_joined, branch))
        token_grad, small_b = last_call(
            slots, grad_joined, joined_weight, tok, gmid, row(first_gain)
        )
        small = lax.psum(jnp.concatenate([small_a, small_b], axis=0), ("dp", "group"))
        outs = []
        for chunk in range(3):
            mine = reduce_chunk(pieces[2 * chunk + 1], pieces[2 * chunk], plan, sizes)
            outs.append(gather_chunk(mine, plan, sizes))
        mlp = None
        for chunk in range(2):
            for which in range(2):
                mlp = finish_call(chunk, which, ids, outs[chunk][which], mlp)
        attn = None
        for which in range(2):
            attn = finish_call(2, which, ids, outs[2][which], attn)
        down_grad, up_grad = mlp
        joined_grad, merge_grad = attn
        return (
            result.reshape(tokens.shape),
            token_grad.reshape(tokens.shape),
            small[10],
            small[11],
            joined_grad,
            small[8:10],
            merge_grad,
            small[7],
            small[5],
            small[6],
            up_grad,
            small[:4].reshape(FF),
            down_grad,
            small[4],
        )

    spread = P(("dp", "group"), None, None)
    return jax.shard_map(
        shards,
        mesh=mesh,
        in_specs=(spread, spread, P(("dp", "group"))) + (P(),) * 12,
        out_specs=(spread, spread) + (P(),) * 12,
        check_vma=False,
    )
```

```python
import math

import jax
import jax.numpy as jnp
from jax import lax
from jax.experimental import pallas as pl
from jax.experimental.pallas import tpu as pltpu
from jax.sharding import PartitionSpec as P

D = 768
HEADS = 12
HEAD_DIM = 64
FF = 3072
PAIRS = HEADS // 2
LANES = 2 * HEAD_DIM
EPS = 1e-06
NEG = -1e30
BF = jnp.bfloat16
F32 = jnp.float32
FACTOR = HEAD_DIM ** (-0.5)
BLOCKS = 16
BROWS = D // BLOCKS


def dot(a, b):
    return jnp.dot(a, b, preferred_element_type=F32)


def dot_t(a, b):
    return lax.dot_general(a, b, (((1,), (1,)), ((), ())), preferred_element_type=F32)


def t_dot(a, b):
    return lax.dot_general(a, b, (((0,), (0,)), ((), ())), preferred_element_type=F32)


def vectors(g1, s1, jb, mb, g2, s2, db):
    row = lax.broadcasted_iota(jnp.int32, (8, D), 0)
    total = jnp.zeros((8, D), F32)
    for at, vector in enumerate((g1, s1, jb[0], jb[1], mb, g2, s2, db)):
        total = jnp.where(row == at, vector[None, :], total)
    return total


def stats(x):
    centred = x - jnp.mean(x, axis=-1, keepdims=True)
    rstd = lax.rsqrt(jnp.mean(centred * centred, axis=-1, keepdims=True) + EPS)
    return centred * rstd, rstd


def params(limit=56):
    return pltpu.CompilerParams(vmem_limit_bytes=limit * 1024 * 1024)


def cost(flops, nbytes, trans=0):
    return pl.CostEstimate(flops=int(10 * flops), bytes_accessed=int(10 * nbytes), transcendentals=int(trans))


def full(shape):
    return pl.BlockSpec(shape, lambda *_: (0,) * len(shape))


def head_masks(rows):
    lane = lax.broadcasted_iota(jnp.int32, (rows, LANES), 1)
    return lane < HEAD_DIM


def stack_heads(pair, low):
    zero = jnp.zeros_like(pair)
    return jnp.concatenate([jnp.where(low, pair, zero), jnp.where(low, zero, pair)], axis=0)


def first_body(
    slots,
    counts_ref,
    tok_ref,
    cot_ref,
    vec_ref,
    wj_ref,
    wm_ref,
    normed_ref,
    joined_ref,
    probs_ref,
    mix_ref,
    middle_ref,
    second_ref,
    gout_ref,
):
    step = pl.program_id(0)
    rows = tok_ref.shape[0]
    items = rows // slots
    x = tok_ref[...].astype(F32)
    xhat, _ = stats(x)
    normed = (xhat * vec_ref[0:1, :] + vec_ref[1:2, :]).astype(BF)
    normed_ref[...] = normed
    for third in range(3):
        cols = slice(third * D, (third + 1) * D)
        part = dot(normed, wj_ref[:, cols])
        if third == 0:
            part = part + vec_ref[2:3, :]
        if third == 2:
            part = part + vec_ref[3:4, :]
        joined_ref[:, cols] = part.astype(BF)
    low = head_masks(slots)
    key_slot = lax.broadcasted_iota(jnp.int32, (2 * slots, slots), 1)
    row_slot = lax.broadcasted_iota(jnp.int32, (slots, D), 0)

    def one(item, carry):
        count = counts_ref[step * items + item]
        here = pl.ds(pl.multiple_of(item * slots, 16), slots)
        seen = row_slot < count
        cot = cot_ref[here, :]
        gout_ref[here, :] = jnp.where(seen, cot, jnp.zeros_like(cot))
        allowed = key_slot < count
        for pair in range(PAIRS):
            cols = slice(pair * LANES, (pair + 1) * LANES)
            q = stack_heads(joined_ref[here, cols], low)
            k = joined_ref[here, D + pair * LANES : D + (pair + 1) * LANES]
            v = joined_ref[here, 2 * D + pair * LANES : 2 * D + (pair + 1) * LANES]
            scores = jnp.where(allowed, dot_t(q, k) * FACTOR, NEG)
            raised = jnp.exp(scores - jnp.max(scores, axis=-1, keepdims=True))
            soft = (raised / jnp.sum(raised, axis=-1, keepdims=True)).astype(BF)
            probs_ref[item, pair] = soft
            mixed = dot(soft, v)
            mix_ref[here, cols] = jnp.where(low, mixed[:slots], mixed[slots:]).astype(BF)
        return carry

    lax.fori_loop(0, items, one, 0)
    middle = x + dot(mix_ref[...], wm_ref[...]) + vec_ref[4:5, :]
    middle_ref[...] = middle
    xhat, _ = stats(middle)
    second_ref[...] = (xhat * vec_ref[5:6, :] + vec_ref[6:7, :]).astype(BF)


def first_call(group, slots, counts, tok, cot, vec, wj, wm):
    total = tok.shape[0]
    rows = group * slots
    steps = total // rows
    row = lambda width: pl.BlockSpec((rows, width), lambda i, c: (i, 0))
    out = lambda width, dt: jax.ShapeDtypeStruct((total, width), dt)
    return pl.pallas_call(
        lambda *refs: first_body(slots, *refs),
        grid_spec=pltpu.PrefetchScalarGridSpec(
            num_scalar_prefetch=1,
            grid=(steps,),
            in_specs=[row(D), row(D)]
            + [full(a.shape) for a in (vec, wj, wm)],
            out_specs=[
                row(D),
                row(3 * D),
                pl.BlockSpec((group, PAIRS, 2 * slots, slots), lambda i, c: (i, 0, 0, 0)),
                row(D),
                row(D),
                row(D),
                row(D),
            ],
        ),
        out_shape=[
            out(D, BF),
            out(3 * D, BF),
            jax.ShapeDtypeStruct((total // slots, PAIRS, 2 * slots, slots), BF),
            out(D, BF),
            out(D, F32),
            out(D, BF),
            out(D, BF),
        ],
        compiler_params=params(),
        cost_estimate=cost(2 * total * D * D * 4 * 2, 20e6),
        name="attn_fwd",
    )(counts, tok, cot, vec, wj, wm)


def put_blocks(ref, which, mask, value):
    for k in range(BLOCKS):
        ref[which, k ^ mask] = value[k * BROWS : (k + 1) * BROWS, :].astype(BF)


def quarter_body(chunk, ids_ref, sec_ref, gout_ref, up_ref, ub_ref, down_ref, *rest):
    act_ref, gh_ref, grad_ref = rest[-3:]
    rows = sec_ref.shape[0]
    chunk = rows // chunk
    for part in range(rows // chunk):
        here = slice(part * chunk, (part + 1) * chunk)
        hidden = dot(sec_ref[here, :], up_ref[...]) + ub_ref[...]
        grad_act = dot_t(gout_ref[here, :], down_ref[...])
        cdf = 0.5 + 0.5 * lax.erf(hidden * (0.5**0.5))
        act_ref[0, here, :] = (hidden * cdf).astype(BF)
        slope = cdf + hidden * (jnp.exp(-0.5 * hidden * hidden) * ((2 * math.pi) ** -0.5))
        gh_ref[0, here, :] = (grad_act * slope).astype(BF)
    put_blocks(grad_ref, 0, ids_ref[0], t_dot(act_ref[0], gout_ref[...]))
    put_blocks(grad_ref, 1, ids_ref[1], t_dot(sec_ref[...], gh_ref[0]))


def quarter_call(call, ids, second, gout, up, ub, down, kept):
    total = second.shape[0]
    quarter = lambda ids: ids[4 + call]
    in_specs = [
        full((total, D)),
        full((total, D)),
        pl.BlockSpec((D, D), lambda i, ids: (0, quarter(ids))),
        pl.BlockSpec((1, D), lambda i, ids: (0, quarter(ids))),
        pl.BlockSpec((D, D), lambda i, ids: (quarter(ids), 0)),
    ]
    args = [ids, second, gout, up, ub, down]
    aliases = {}
    if kept is not None:
        in_specs += [pl.BlockSpec(memory_space=pl.ANY)] * 2
        args += list(kept)
        aliases = {6: 0, 7: 1}
    slab = pl.BlockSpec((1, total, D), lambda i, ids: (call, 0, 0))
    return pl.pallas_call(
        lambda *refs: quarter_body(2, *refs),
        grid_spec=pltpu.PrefetchScalarGridSpec(
            num_scalar_prefetch=1,
            grid=(1,),
            in_specs=in_specs,
            out_specs=[slab, slab, full((2, BLOCKS, BROWS, D))],
        ),
        out_shape=[
            jax.ShapeDtypeStruct((4, total, D), BF),
            jax.ShapeDtypeStruct((4, total, D), BF),
            jax.ShapeDtypeStruct((2, BLOCKS, BROWS, D), BF),
        ],
        input_output_aliases=aliases,
        compiler_params=params(),
        cost_estimate=cost(8 * total * D * D * 2, 12e6),
        name=f"mlp_{call}",
    )(*args)


def middle_body(
    slots,
    counts_ref,
    ids_ref,
    act_ref,
    gh_ref,
    down_ref,
    up_ref,
    mid_ref,
    gout_ref,
    vec_ref,
    wm_ref,
    result_ref,
    gmid_ref,
    branch_ref,
    gmix_ref,
    small_ref,
    outer_ref,
    g_ref,
):
    step = pl.program_id(0)
    rows = mid_ref.shape[0]
    items = rows // slots
    outer = dot(act_ref[0], down_ref[...])
    g = dot_t(gh_ref[0], up_ref[...])
    sums = jnp.sum(gh_ref[0].astype(F32), axis=0, keepdims=True)
    small_ref[pl.ds(ids_ref[4 + step], 1), :] = sums

    @pl.when(step == 0)
    def _():
        outer_ref[...] = outer
        g_ref[...] = g

    @pl.when(step > 0)
    def _():
        outer_ref[...] += outer
        g_ref[...] += g

    @pl.when(step == 3)
    def _():
        row_slot = lax.broadcasted_iota(jnp.int32, (slots, D), 0)

        def one(item, sums):
            here = pl.ds(pl.multiple_of(item * slots, 16), slots)
            seen = row_slot < counts_ref[item]
            middle = mid_ref[here, :]
            total = middle + outer_ref[here, :] + vec_ref[7:8, :]
            result_ref[here, :] = jnp.where(seen, total, 0.0).astype(BF)
            gout = gout_ref[here, :].astype(F32)
            xhat, rstd = stats(middle)
            g = g_ref[here, :]
            e = g * vec_ref[5:6, :]
            mean_e = jnp.mean(e, axis=-1, keepdims=True)
            mean_x = jnp.mean(e * xhat, axis=-1, keepdims=True)
            grad = gout + rstd * (e - mean_e - xhat * mean_x)
            gmid_ref[here, :] = grad
            branch = grad.astype(BF)
            branch_ref[here, :] = branch
            row = lambda a: jnp.sum(a, axis=0, keepdims=True)
            return (
                sums[0] + row(gout),
                sums[1] + row(g * xhat),
                sums[2] + row(g),
                sums[3] + row(branch.astype(F32)),
            )

        zero = jnp.zeros((1, D), F32)
        sums = lax.fori_loop(0, items, one, (zero,) * 4)
        for k in range(4):
            small_ref[4 + k : 5 + k, :] = sums[k]
        gmix_ref[...] = dot_t(branch_ref[...], wm_ref[...]).astype(BF)


def middle_call(slots, counts, ids, act, gh, down, up, mid, gout, vec, wm):
    total = mid.shape[0]
    whole = full((total, D))
    return pl.pallas_call(
        lambda *refs: middle_body(slots, *refs),
        grid_spec=pltpu.PrefetchScalarGridSpec(
            num_scalar_prefetch=2,
            grid=(4,),
            in_specs=[
                pl.BlockSpec((1, total, D), lambda i, c, ids: (i, 0, 0)),
                pl.BlockSpec((1, total, D), lambda i, c, ids: (i, 0, 0)),
                pl.BlockSpec((D, D), lambda i, c, ids: (ids[4 + i], 0)),
                pl.BlockSpec((D, D), lambda i, c, ids: (0, ids[4 + i])),
                whole,
                whole,
                full((8, D)),
                full((D, D)),
            ],
            out_specs=[whole, whole, whole, whole, full((8, D))],
            scratch_shapes=[pltpu.VMEM((total, D), F32), pltpu.VMEM((total, D), F32)],
        ),
        out_shape=[
            jax.ShapeDtypeStruct((total, D), BF),
            jax.ShapeDtypeStruct((total, D), F32),
            jax.ShapeDtypeStruct((total, D), BF),
            jax.ShapeDtypeStruct((total, D), BF),
            jax.ShapeDtypeStruct((8, D), F32),
        ],
        compiler_params=params(),
        cost_estimate=cost(2 * total * D * D * 9, 25e6),
        name="mlp_back",
    )(counts, ids, act, gh, down, up, mid, gout, vec, wm)


def attn_back_body(joined_ref, probs_ref, gmix_ref, grad_ref):
    slots = joined_ref.shape[0]
    low = head_masks(slots)
    for pair in range(PAIRS):
        cols = slice(pair * LANES, (pair + 1) * LANES)
        q = stack_heads(joined_ref[:, cols], low)
        k = joined_ref[:, D + pair * LANES : D + (pair + 1) * LANES]
        v = joined_ref[:, 2 * D + pair * LANES : 2 * D + (pair + 1) * LANES]
        out = stack_heads(gmix_ref[:, cols], low)
        low_soft = probs_ref[0, pair]
        soft = low_soft.astype(F32)
        grad_probs = dot_t(out, v)
        mean = jnp.sum(soft * grad_probs, axis=-1, keepdims=True)
        scores = (soft * (grad_probs - mean)).astype(BF)
        gq = dot(scores, k) * FACTOR
        grad_ref[:, cols] = jnp.where(low, gq[:slots], gq[slots:]).astype(BF)
        grad_ref[:, D + pair * LANES : D + (pair + 1) * LANES] = (
            t_dot(scores, q) * FACTOR
        ).astype(BF)
        grad_ref[:, 2 * D + pair * LANES : 2 * D + (pair + 1) * LANES] = t_dot(
            low_soft, out
        ).astype(BF)


def attn_back_call(slots, joined, probs, gmix):
    total = joined.shape[0]
    row = lambda width: pl.BlockSpec((slots, width), lambda i: (i, 0))
    return pl.pallas_call(
        attn_back_body,
        grid=(total // slots,),
        in_specs=[
            row(3 * D),
            pl.BlockSpec((1, PAIRS, 2 * slots, slots), lambda i: (i, 0, 0, 0)),
            row(D),
        ],
        out_specs=row(3 * D),
        out_shape=jax.ShapeDtypeStruct((total, 3 * D), BF),
        compiler_params=params(),
        cost_estimate=cost(total * slots * 256 * 6 * 8, 12e6),
        name="attn_bwd",
    )(joined, probs, gmix)


def attn_grad_body(ids_ref, normed_ref, mix_ref, grad_ref, branch_ref, out_ref):
    half = BLOCKS // 2

    def put(which, base, mask, value):
        for k in range(half):
            out_ref[which, (base + k) ^ mask] = value[k * BROWS : (k + 1) * BROWS, :].astype(BF)

    normed = normed_ref[...]
    put(0, 0, ids_ref[0], t_dot(normed, grad_ref[:, :D]))
    put(0, half, ids_ref[0], t_dot(normed, grad_ref[:, D : 2 * D]))
    put(1, 0, ids_ref[1], t_dot(normed, grad_ref[:, 2 * D :]))
    put(1, half, ids_ref[1], t_dot(mix_ref[...], branch_ref[...]))


def attn_grad_call(call, ids, normed, mix, grad, branch):
    total = normed.shape[0]
    half = pl.BlockSpec((total, D // 2), lambda i, ids: (0, ids[8 + call]))
    return pl.pallas_call(
        attn_grad_body,
        grid_spec=pltpu.PrefetchScalarGridSpec(
            num_scalar_prefetch=1,
            grid=(1,),
            in_specs=[half, half, full((total, 3 * D)), full((total, D))],
            out_specs=full((2, BLOCKS, BROWS, D)),
        ),
        out_shape=jax.ShapeDtypeStruct((2, BLOCKS, BROWS, D), BF),
        compiler_params=params(),
        cost_estimate=cost(2 * total * D * D * 2, 8e6),
        name=f"attn_grad_{call}",
    )(ids, normed, mix, grad, branch)


def last_body(slots, grad_ref, wj_ref, tok_ref, gmid_ref, vec_ref, out_ref, small_ref, g_ref):
    rows = tok_ref.shape[0]
    items = rows // slots
    g_ref[...] = dot_t(grad_ref[...], wj_ref[...])

    def one(item, sums):
        here = pl.ds(pl.multiple_of(item * slots, 16), slots)
        xhat, rstd = stats(tok_ref[here, :].astype(F32))
        g = g_ref[here, :]
        e = g * vec_ref[0:1, :]
        mean_e = jnp.mean(e, axis=-1, keepdims=True)
        mean_x = jnp.mean(e * xhat, axis=-1, keepdims=True)
        out_ref[here, :] = (gmid_ref[here, :] + rstd * (e - mean_e - xhat * mean_x)).astype(BF)
        row = lambda a: jnp.sum(a, axis=0, keepdims=True)
        return (
            sums[0] + row(grad_ref[here, :D].astype(F32)),
            sums[1] + row(grad_ref[here, 2 * D :].astype(F32)),
            sums[2] + row(g * xhat),
            sums[3] + row(g),
        )

    zero = jnp.zeros((1, D), F32)
    sums = lax.fori_loop(0, items, one, (zero,) * 4)
    for k in range(4):
        small_ref[k : k + 1, :] = sums[k]
    small_ref[4:8, :] = jnp.zeros((4, D), F32)


def last_call(slots, grad, wj, tok, gmid, vec):
    total = tok.shape[0]
    return pl.pallas_call(
        lambda *refs: last_body(slots, *refs),
        grid=(1,),
        in_specs=[full(a.shape) for a in (grad, wj, tok, gmid, vec)],
        out_specs=[full((total, D)), full((8, D))],
        out_shape=[
            jax.ShapeDtypeStruct((total, D), BF),
            jax.ShapeDtypeStruct((8, D), F32),
        ],
        scratch_shapes=[pltpu.VMEM((total, D), F32)],
        compiler_params=params(),
        cost_estimate=cost(2 * total * D * D * 3, 12e6),
        name="first_back",
    )(grad, wj, tok, gmid, vec)


def finish_mlp_body(groups, ab, ids_ref, in_ref, *rest):
    out_ref = rest[-1]
    mask = ids_ref[ab] & (groups - 1)
    for k in range(groups):
        out_ref[k * BROWS : (k + 1) * BROWS, :] = in_ref[0, k ^ mask].astype(F32)


def finish_mlp_call(ab, which, ids, blocks, kept):
    groups = 8
    steps = BLOCKS // groups

    def place(chunk, i, ids):
        at = (ids[ab] // groups) ^ i
        quarter = 2 * chunk + (ids[3] ^ which)
        return (quarter * steps + at, 0) if ab == 0 else (at, quarter)

    in_specs = [pl.BlockSpec((1, groups, BROWS, D), lambda chunk, i, ids: (chunk, i, 0, 0))]
    args = [ids, blocks]
    aliases = {}
    if kept is not None:
        in_specs.append(pl.BlockSpec(memory_space=pl.ANY))
        args.append(kept)
        aliases = {2: 0}
    return pl.pallas_call(
        lambda *refs: finish_mlp_body(groups, ab, *refs),
        grid_spec=pltpu.PrefetchScalarGridSpec(
            num_scalar_prefetch=1,
            grid=(2, steps),
            in_specs=in_specs,
            out_specs=pl.BlockSpec((groups * BROWS, D), place),
        ),
        out_shape=jax.ShapeDtypeStruct((FF, D) if ab == 0 else (D, FF), F32),
        input_output_aliases=aliases,
        compiler_params=params(16),
        cost_estimate=cost(0, 7e6),
        name=f"finish_mlp_{ab}_{which}",
    )(*args)


def finish_attn_body(ids_ref, a_ref, b_ref, *rest):
    joined_ref, merge_ref = rest[-2:]
    half = BLOCKS // 2
    for ab, in_ref in enumerate((a_ref, b_ref)):
        mask = ids_ref[ab]
        for i in range(BLOCKS):
            block = in_ref[i ^ mask].astype(F32)
            third, k = 2 * ab + i // half, i % half
            rows = slice(k * BROWS, (k + 1) * BROWS)
            if third < 3:
                joined_ref[rows, third * D : (third + 1) * D] = block
            else:
                merge_ref[rows, :] = block


def finish_attn_call(which, ids, a, b, kept):
    in_specs = [full((BLOCKS, BROWS, D))] * 2
    args = [ids, a, b]
    aliases = {}
    if kept is not None:
        in_specs += [pl.BlockSpec(memory_space=pl.ANY)] * 2
        args += list(kept)
        aliases = {3: 0, 4: 1}
    place = lambda i, ids: (ids[3] ^ which, 0)
    return pl.pallas_call(
        finish_attn_body,
        grid_spec=pltpu.PrefetchScalarGridSpec(
            num_scalar_prefetch=1,
            grid=(1,),
            in_specs=in_specs,
            out_specs=[pl.BlockSpec((D // 2, 3 * D), place), pl.BlockSpec((D // 2, D), place)],
        ),
        out_shape=[jax.ShapeDtypeStruct(s, F32) for s in ((D, 3 * D), (D, D))],
        input_output_aliases=aliases,
        compiler_params=params(32),
        cost_estimate=cost(0, 7e6),
        name=f"finish_attn_{which}",
    )(*args)


def stage_lists(sizes):
    bits = {axis: [(axis, b) for b in range(size.bit_length() - 1)] for axis, size in sizes.items()}
    dp, group = bits["dp"], bits["group"]
    if len(dp) == 2 and len(group) == 3:
        order = group + dp
    else:
        order = [dp[0], group[0], group[-1]] + dp[1:] + group[1:-1]
    return order[0], order[1:3], order[3:]


def add(a, b):
    return (a.astype(F32) + b.astype(F32)).astype(BF)


def bit_of(stage):
    return (lax.axis_index(stage[0]) >> stage[1]) & 1


def tie(*values):
    return lax.optimization_barrier(values)


class Sums:
    def __init__(self, sizes):
        self.sizes = sizes
        self.first, self.pair, self.rest = stage_lists(sizes)

    def swap(self, value, stage):
        axis, bit = stage
        return lax.ppermute(value, axis, [(i, i ^ (1 << bit)) for i in range(self.sizes[axis])])

    def stage(self, ab, at):
        return self.pair[at if ab == 0 else 1 - at]

    def halve(self, mine, got, axis=0):
        n = mine.shape[axis] // 2
        low = lax.slice_in_dim(mine, 0, n, axis=axis), lax.slice_in_dim(got, 0, n, axis=axis)
        high = lax.slice_in_dim(mine, n, 2 * n, axis=axis), lax.slice_in_dim(
            got, n, 2 * n, axis=axis
        )
        return add(*low), add(*high)

    def tail_down(self, at, mine):
        if at < 2:
            n = mine.shape[1] // 2
            return mine[:, :n], mine[:, n:]
        n = mine.shape[2] // 2
        high = bit_of(self.rest[at]) == 1
        low_rows, high_rows = mine[:, :, :n], mine[:, :, n:]
        return jnp.where(high, high_rows, low_rows), jnp.where(high, low_rows, high_rows)

    def tail_up(self, at, mine, got):
        if at < 2:
            return jnp.concatenate([mine, got], axis=1)
        high = bit_of(self.rest[at]) == 1
        return jnp.concatenate([jnp.where(high, got, mine), jnp.where(high, mine, got)], axis=2)


def split_small(value):
    high = lax.reduce_precision(value, 8, 7)
    return jnp.concatenate([high.astype(BF), (value - high).astype(BF)], axis=0)


def join_small(value):
    n = value.shape[0] // 2
    return value[:n].astype(F32) + value[n:].astype(F32)


def solution(mesh):
    sizes = dict(mesh.shape)
    sums = Sums(sizes)

    def shards(
        tokens,
        cotangent,
        counts,
        first_gain,
        first_shift,
        joined_weight,
        joined_bias,
        merge_weight,
        merge_bias,
        second_gain,
        second_shift,
        up_weight,
        up_bias,
        down_weight,
        down_bias,
    ):
        items, slots, features = tokens.shape
        total = items * slots
        row = lambda a: a.reshape(1, -1)
        tok = tokens.reshape(total, features)
        cot = cotangent.reshape(total, features)
        counts = counts.astype(jnp.int32)
        masks = []
        for two in (sums.pair, sums.pair[::-1]):
            mask = 0
            for stage in list(two) + list(sums.rest[:2]):
                mask = 2 * mask + bit_of(stage)
            masks.append(mask)
        core = bit_of(sums.first)
        other = 1 - core
        ids = jnp.stack(
            [masks[0], masks[1], core, core, other, core, 2 + other, 2 + core, other, core]
        ).astype(jnp.int32)

        vec = vectors(
            first_gain,
            first_shift,
            joined_bias,
            merge_bias,
            second_gain,
            second_shift,
            down_bias,
        )
        normed, joined, probs, mix, middle, second, gout = first_call(
            4,
            slots,
            counts,
            tok,
            cot,
            vec,
            joined_weight,
            merge_weight,
        )

        def quarter(call, kept, ids):
            act, gh, grad = quarter_call(
                call, ids, second, gout, up_weight, row(up_bias), down_weight, kept
            )
            return (act, gh), grad

        def start_pair(keep, send, at):
            return [sums.swap(send[ab], sums.stage(ab, at)) for ab in range(2)]

        kept, send0 = quarter(0, None, ids)
        got0 = sums.swap(send0, sums.first)
        kept, keep0 = quarter(1, kept, ids)
        keep0, out0 = zip(*[sums.halve(keep0[ab], got0[ab]) for ab in range(2)])
        got0 = start_pair(keep0, out0, 0)
        ids, out0 = tie(ids, out0)
        kept, send1 = quarter(2, kept, ids)
        got1 = sums.swap(send1, sums.first)
        kept, keep1 = quarter(3, kept, ids)
        keep1, out1 = zip(*[sums.halve(keep1[ab], got1[ab]) for ab in range(2)])
        got1 = start_pair(keep1, out1, 0)
        keep0, out0 = zip(*[sums.halve(keep0[ab], got0[ab]) for ab in range(2)])
        got0 = start_pair(keep0, out0, 1)
        ids, out0, out1 = tie(ids, out0, out1)
        result, gmid, branch, gmix, small_a = middle_call(
            slots,
            counts,
            ids,
            kept[0],
            kept[1],
            down_weight,
            up_weight,
            middle,
            gout,
            vec,
            merge_weight,
        )
        keep1, out1 = zip(*[sums.halve(keep1[ab], got1[ab]) for ab in range(2)])
        got1 = start_pair(keep1, out1, 1)
        mine0 = [add(keep0[ab], got0[ab]) for ab in range(2)]
        gmix, out1, mine0 = tie(gmix, out1, mine0)
        grad_joined = attn_back_call(slots, joined, probs, gmix)
        mine1 = [add(keep1[ab], got1[ab]) for ab in range(2)]
        mine = jnp.stack([mine0[0], mine1[0], mine0[1], mine1[1]])
        down = sums.tail_down(0, mine)
        got = sums.swap(down[1], sums.rest[0])
        ids, down = tie(ids, down)
        send2 = attn_grad_call(0, ids, normed, mix, grad_joined, branch)
        got2 = sums.swap(send2, sums.first)
        for at in range(len(sums.rest)):
            mine = add(down[0], got)
            if at + 1 < len(sums.rest):
                down = sums.tail_down(at + 1, mine)
                got = sums.swap(down[1], sums.rest[at + 1])
                if at == 0:
                    ids, down = tie(ids, down)
                    keep2 = attn_grad_call(1, ids, normed, mix, grad_joined, branch)
        keep2, out2 = zip(*[sums.halve(keep2[ab], got2[ab]) for ab in range(2)])
        got2 = start_pair(keep2, out2, 0)
        got = sums.swap(mine, sums.rest[-1])
        grad_joined, out2, mine = tie(grad_joined, out2, mine)
        token_grad, small_b = last_call(
            slots, grad_joined, joined_weight, tok, gmid, vec
        )
        for at in reversed(range(len(sums.rest))):
            mine = sums.tail_up(at, mine, got)
            if at:
                got = sums.swap(mine, sums.rest[at - 1])
        keep2, out2 = zip(*[sums.halve(keep2[ab], got2[ab]) for ab in range(2)])
        got2 = start_pair(keep2, out2, 1)
        own = [mine[:2], mine[2:]]
        got = [sums.swap(own[ab], sums.stage(ab, 1)) for ab in range(2)]
        mine2 = jnp.stack([add(keep2[ab], got2[ab]) for ab in range(2)])
        for at in range(len(sums.rest)):
            down = sums.tail_down(at, mine2)
            mine2 = add(down[0], sums.swap(down[1], sums.rest[at]))
        small = jnp.concatenate([small_a, small_b[:4]], axis=0)

        def piggy(value, small, stage):
            rows = split_small(small)
            pad = jnp.zeros((BROWS - rows.shape[0], D), BF)
            load = value.reshape(-1, D)
            out = jnp.concatenate([load, rows, pad], axis=0)
            got = sums.swap(out, stage)
            total = join_small(rows) + join_small(
                got[load.shape[0] : load.shape[0] + rows.shape[0]]
            )
            return got[: load.shape[0]].reshape(value.shape), total

        for at in reversed(range(len(sums.rest))):
            got2, small = piggy(mine2, small, sums.rest[at])
            mine2 = sums.tail_up(at, mine2, got2)
        own = [jnp.concatenate([own[ab], got[ab]], axis=1) for ab in range(2)]
        got = [sums.swap(own[ab], sums.stage(ab, 0)) for ab in range(2)]
        own2 = [mine2[0], mine2[1]]
        for at in (1, 0):
            got2, small = piggy(own2[0], small, sums.stage(0, at))
            other2 = sums.swap(own2[1], sums.stage(1, at))
            own2 = [jnp.concatenate([own2[0], got2]), jnp.concatenate([own2[1], other2])]
            if at:
                own = [jnp.concatenate([own[ab], got[ab]], axis=1) for ab in range(2)]
                got = [sums.swap(own[ab], sums.first) for ab in range(2)]
        mlp = [finish_mlp_call(ab, 0, ids, own[ab], None) for ab in range(2)]
        mlp = [finish_mlp_call(ab, 1, ids, got[ab], mlp[ab]) for ab in range(2)]
        got2, small = piggy(own2[0], small, sums.first)
        other2 = sums.swap(own2[1], sums.first)
        attn = finish_attn_call(0, ids, own2[0], own2[1], None)
        joined_grad, merge_grad = finish_attn_call(1, ids, got2, other2, attn)
        down_grad, up_grad = mlp
        return (
            result.reshape(tokens.shape),
            token_grad.reshape(tokens.shape),
            small[10],
            small[11],
            joined_grad,
            small[8:10],
            merge_grad,
            small[7],
            small[5],
            small[6],
            up_grad,
            small[:4].reshape(FF),
            down_grad,
            small[4],
        )

    spread = P(("dp", "group"), None, None)
    return jax.shard_map(
        shards,
        mesh=mesh,
        in_specs=(spread, spread, P(("dp", "group"))) + (P(),) * 12,
        out_specs=(spread, spread) + (P(),) * 12,
        check_vma=False,
    )
```

```python
import math

import jax
import jax.numpy as jnp
from jax import lax
from jax.experimental import pallas as pl
from jax.experimental.pallas import tpu as pltpu
from jax.sharding import PartitionSpec as P

D = 768
HEADS = 12
HEAD_DIM = 64
FF = 3072
PAIRS = HEADS // 2
LANES = 2 * HEAD_DIM
EPS = 1e-06
NEG = -1e30
BF = jnp.bfloat16
F32 = jnp.float32
FACTOR = HEAD_DIM ** (-0.5)
BLOCKS = 16
BROWS = D // BLOCKS
SCALE = 10


def dot(a, b):
    return jnp.dot(a, b, preferred_element_type=F32)


def dot_t(a, b):
    return lax.dot_general(a, b, (((1,), (1,)), ((), ())), preferred_element_type=F32)


def t_dot(a, b):
    return lax.dot_general(a, b, (((0,), (0,)), ((), ())), preferred_element_type=F32)


def stats(x):
    centred = x - jnp.mean(x, axis=-1, keepdims=True)
    rstd = lax.rsqrt(jnp.mean(centred * centred, axis=-1, keepdims=True) + EPS)
    return centred * rstd, rstd


def pin(value):
    return pltpu.with_memory_space_constraint(value, pltpu.HBM)


def vmem(limit):
    return pltpu.CompilerParams(vmem_limit_bytes=limit * 1024 * 1024)


def params(rows=640):
    return vmem(20 if rows <= 640 else 48)


def cost(us):
    return pl.CostEstimate(flops=int(us * SCALE * 1e9), bytes_accessed=1000, transcendentals=0)


def full(shape):
    return pl.BlockSpec(shape, lambda *_: (0,) * len(shape))


def head_masks(rows):
    lane = lax.broadcasted_iota(jnp.int32, (rows, LANES), 1)
    return lane < HEAD_DIM


def stack_heads(pair, low):
    zero = jnp.zeros_like(pair)
    return jnp.concatenate([jnp.where(low, pair, zero), jnp.where(low, zero, pair)], axis=0)


def first_body(
    slots,
    counts_ref,
    tok_hbm,
    cot_hbm,
    wj_hbm,
    wm_hbm,
    g1_ref,
    s1_ref,
    jb_ref,
    mb_ref,
    g2_ref,
    s2_ref,
    normed_ref,
    joined_ref,
    probs_ref,
    mix_ref,
    middle_ref,
    second_ref,
    gout_ref,
    tok_ref,
    cot_ref,
    wj_ref,
    wm_ref,
    sem,
):
    step = pl.program_id(0)
    rows = tok_ref.shape[0]
    items = rows // slots
    span = pl.ds(pl.multiple_of(step * rows, 16), rows)
    tok_copy = pltpu.make_async_copy(tok_hbm.at[span], tok_ref, sem.at[0])
    cot_copy = pltpu.make_async_copy(cot_hbm.at[span], cot_ref, sem.at[1])
    wm_copy = pltpu.make_async_copy(wm_hbm, wm_ref, sem.at[2])
    wj_copies = [
        pltpu.make_async_copy(
            wj_hbm.at[:, pl.ds(third * D, D)], wj_ref.at[third], sem.at[3 + third]
        )
        for third in range(3)
    ]
    tok_copy.start()

    @pl.when(step == 0)
    def _():
        for copy in wj_copies:
            copy.start()

    cot_copy.start()

    @pl.when(step == 0)
    def _():
        wm_copy.start()

    tok_copy.wait()
    x = tok_ref[...].astype(F32)
    xhat, _ = stats(x)
    normed = (xhat * g1_ref[...] + s1_ref[...]).astype(BF)
    normed_ref[...] = normed
    for third in range(3):
        cols = slice(third * D, (third + 1) * D)

        @pl.when(step == 0)
        def _():
            wj_copies[third].wait()

        part = dot(normed, wj_ref[third])
        if third == 0:
            part = part + jb_ref[0:1, :]
        if third == 2:
            part = part + jb_ref[1:2, :]
        joined_ref[:, cols] = part.astype(BF)
    cot_copy.wait()
    low = head_masks(slots)
    key_slot = lax.broadcasted_iota(jnp.int32, (2 * slots, slots), 1)
    row_slot = lax.broadcasted_iota(jnp.int32, (slots, D), 0)

    def one(item, carry):
        count = counts_ref[step * items + item]
        here = pl.ds(pl.multiple_of(item * slots, 16), slots)
        seen = row_slot < count
        cot = cot_ref[here, :]
        gout_ref[here, :] = jnp.where(seen, cot, jnp.zeros_like(cot))
        allowed = key_slot < count
        for pair in range(PAIRS):
            cols = slice(pair * LANES, (pair + 1) * LANES)
            q = stack_heads(joined_ref[here, cols] * BF(FACTOR), low)
            k = joined_ref[here, D + pair * LANES : D + (pair + 1) * LANES]
            v = joined_ref[here, 2 * D + pair * LANES : 2 * D + (pair + 1) * LANES]
            scores = jnp.where(allowed, dot_t(q, k), NEG)
            raised = jnp.exp(scores - jnp.max(scores, axis=-1, keepdims=True))
            soft = (raised * (1.0 / jnp.sum(raised, axis=-1, keepdims=True))).astype(BF)
            probs_ref[item, pair] = soft
            mixed = dot(soft, v)
            mix_ref[here, cols] = jnp.where(low, mixed[:slots], mixed[slots:]).astype(BF)
        return carry

    lax.fori_loop(0, items, one, 0)

    @pl.when(step == 0)
    def _():
        wm_copy.wait()

    middle = tok_ref[...].astype(F32) + dot(mix_ref[...], wm_ref[...]) + mb_ref[...]
    middle_ref[...] = middle
    xhat, _ = stats(middle)
    second_ref[...] = (xhat * g2_ref[...] + s2_ref[...]).astype(BF)


def first_call(group, slots, counts, tok, cot, wj, wm, g1, s1, jb, mb, g2, s2):
    total = tok.shape[0]
    rows = group * slots
    steps = total // rows
    row = lambda width: pl.BlockSpec((rows, width), lambda i, c: (i, 0))
    out = lambda width, dt: jax.ShapeDtypeStruct((total, width), dt)
    hbm = pl.BlockSpec(memory_space=pltpu.HBM)
    return pl.pallas_call(
        lambda *refs: first_body(slots, *refs),
        grid_spec=pltpu.PrefetchScalarGridSpec(
            num_scalar_prefetch=1,
            grid=(steps,),
            in_specs=[hbm] * 4 + [full(a.shape) for a in (g1, s1, jb, mb, g2, s2)],
            out_specs=[
                row(D),
                row(3 * D),
                pl.BlockSpec((group, PAIRS, 2 * slots, slots), lambda i, c: (i, 0, 0, 0)),
                row(D),
                row(D),
                row(D),
                row(D),
            ],
            scratch_shapes=[
                pltpu.VMEM((rows, D), BF),
                pltpu.VMEM((rows, D), BF),
                pltpu.VMEM((3, D, D), BF),
                pltpu.VMEM((D, D), BF),
                pltpu.SemaphoreType.DMA((6,)),
            ],
        ),
        out_shape=[
            out(D, BF),
            out(3 * D, BF),
            jax.ShapeDtypeStruct((total // slots, PAIRS, 2 * slots, slots), BF),
            out(D, BF),
            out(D, F32),
            out(D, BF),
            out(D, BF),
        ],
        compiler_params=vmem(32 if steps == 1 else 48),
        cost_estimate=cost(15),
        name="attn_fwd",
    )(*[pin(a) for a in (counts, tok, cot, wj, wm, g1, s1, jb, mb, g2, s2)])


def put_blocks(ref, which, mask, value):
    for k in range(BLOCKS):
        ref[which, k ^ mask] = value[k * BROWS : (k + 1) * BROWS, :].astype(BF)


def quarter_body(parts, ids_ref, sec_ref, gout_ref, up_ref, ub_ref, down_ref, *outs):
    grad_ref, act_ref, gh_ref = outs
    rows = sec_ref.shape[0] // parts
    for part in range(parts):
        here = slice(part * rows, (part + 1) * rows)
        hidden = dot(sec_ref[here, :], up_ref[...]) + ub_ref[...]
        grad_act = dot_t(gout_ref[here, :], down_ref[...])
        cdf = 0.5 + 0.5 * lax.erf(hidden * (0.5**0.5))
        act_ref[here, :] = (hidden * cdf).astype(BF)
        slope = cdf + hidden * (jnp.exp(-0.5 * hidden * hidden) * ((2 * math.pi) ** -0.5))
        gh_ref[here, :] = (grad_act * slope).astype(BF)
    put_blocks(grad_ref, 0, ids_ref[0], t_dot(act_ref[...], gout_ref[...]))
    put_blocks(grad_ref, 1, ids_ref[1], t_dot(sec_ref[...], gh_ref[...]))


def quarter_call(call, ids, second, gout, up, ub, down):
    total = second.shape[0]
    whole = full((total, D))
    return pl.pallas_call(
        lambda *refs: quarter_body(2, *refs),
        grid_spec=pltpu.PrefetchScalarGridSpec(
            num_scalar_prefetch=1,
            grid=(1,),
            in_specs=[
                whole,
                whole,
                pl.BlockSpec((D, D), lambda i, ids: (0, ids[4 + call])),
                pl.BlockSpec((1, D), lambda i, ids: (0, ids[4 + call])),
                pl.BlockSpec((D, D), lambda i, ids: (ids[4 + call], 0)),
            ],
            out_specs=[full((2, BLOCKS, BROWS, D)), whole, whole],
        ),
        out_shape=[
            jax.ShapeDtypeStruct((2, BLOCKS, BROWS, D), BF),
            jax.ShapeDtypeStruct((total, D), BF),
            jax.ShapeDtypeStruct((total, D), BF),
        ],
        compiler_params=params(total),
        cost_estimate=cost(4.3),
        name=f"mlp_{call}",
    )(ids, second, gout, up, ub, down)


def collect_body(chunk, ids_ref, *refs):
    acts, ghs = refs[:2], refs[2:4]
    down_ref, up_ref = refs[4:6]
    kept = refs[6:-3]
    outer_ref, g_ref, small_ref = refs[-3:]
    step = pl.program_id(0)
    for at in range(2):

        @pl.when(step == at)
        def _():
            outer = dot(acts[at][...], down_ref[...])
            g = dot_t(ghs[at][...], up_ref[...])
            if at:
                outer = outer + outer_ref[...]
                g = g + g_ref[...]
            elif chunk:
                outer = outer + kept[0][...]
                g = g + kept[1][...]
                small_ref[...] = kept[2][...]
            outer_ref[...] = outer
            g_ref[...] = g
            small_ref[pl.ds(ids_ref[4 + 2 * chunk + at], 1), :] = jnp.sum(
                ghs[at][...].astype(F32), axis=0, keepdims=True
            )


def collect_call(chunk, ids, acts, ghs, down, up, kept):
    total = acts[0].shape[0]
    whole = full((total, D))
    specs = [whole, whole, full((4, D))]
    return pl.pallas_call(
        lambda *refs: collect_body(chunk, *refs),
        grid_spec=pltpu.PrefetchScalarGridSpec(
            num_scalar_prefetch=1,
            grid=(2,),
            in_specs=[whole] * 4
            + [
                pl.BlockSpec((D, D), lambda i, ids: (ids[4 + 2 * chunk + i], 0)),
                pl.BlockSpec((D, D), lambda i, ids: (0, ids[4 + 2 * chunk + i])),
            ]
            + specs * (1 if chunk else 0),
            out_specs=specs,
        ),
        out_shape=[
            jax.ShapeDtypeStruct((total, D), F32),
            jax.ShapeDtypeStruct((total, D), F32),
            jax.ShapeDtypeStruct((4, D), F32),
        ],
        compiler_params=vmem(24 if total <= 640 else 56),
        cost_estimate=cost(4.3),
        name=f"mlp_collect_{chunk}",
    )(ids, *acts, *ghs, down, up, *(kept or ()))


def middle_body(
    slots,
    counts_ref,
    outer_ref,
    g_ref,
    mid_ref,
    gout_ref,
    db_ref,
    g2_ref,
    wm_ref,
    result_ref,
    gmid_ref,
    branch_ref,
    gmix_ref,
    small_ref,
):
    items = mid_ref.shape[0] // slots
    row_slot = lax.broadcasted_iota(jnp.int32, (slots, D), 0)

    def one(item, sums):
        here = pl.ds(pl.multiple_of(item * slots, 16), slots)
        seen = row_slot < counts_ref[item]
        middle = mid_ref[here, :]
        total = middle + outer_ref[here, :] + db_ref[...]
        result_ref[here, :] = jnp.where(seen, total, 0.0).astype(BF)
        gout = gout_ref[here, :].astype(F32)
        xhat, rstd = stats(middle)
        g = g_ref[here, :]
        e = g * g2_ref[...]
        mean_e = jnp.mean(e, axis=-1, keepdims=True)
        mean_x = jnp.mean(e * xhat, axis=-1, keepdims=True)
        grad = gout + rstd * (e - mean_e - xhat * mean_x)
        gmid_ref[here, :] = grad
        branch = grad.astype(BF)
        branch_ref[here, :] = branch
        row = lambda a: jnp.sum(a, axis=0, keepdims=True)
        return (
            sums[0] + row(gout),
            sums[1] + row(g * xhat),
            sums[2] + row(g),
            sums[3] + row(branch.astype(F32)),
        )

    zero = jnp.zeros((1, D), F32)
    sums = lax.fori_loop(0, items, one, (zero,) * 4)
    for k in range(4):
        small_ref[k : k + 1, :] = sums[k]
    gmix_ref[...] = dot_t(branch_ref[...], wm_ref[...]).astype(BF)


def middle_call(slots, counts, outer, g, mid, gout, db, g2, wm):
    total = mid.shape[0]
    whole = full((total, D))
    return pl.pallas_call(
        lambda *refs: middle_body(slots, *refs),
        grid_spec=pltpu.PrefetchScalarGridSpec(
            num_scalar_prefetch=1,
            grid=(1,),
            in_specs=[whole, whole, whole, whole, full(db.shape), full(g2.shape), full((D, D))],
            out_specs=[whole, whole, whole, whole, full((4, D))],
        ),
        out_shape=[
            jax.ShapeDtypeStruct((total, D), BF),
            jax.ShapeDtypeStruct((total, D), F32),
            jax.ShapeDtypeStruct((total, D), BF),
            jax.ShapeDtypeStruct((total, D), BF),
            jax.ShapeDtypeStruct((4, D), F32),
        ],
        compiler_params=params(total),
        cost_estimate=cost(3.6),
        name="mlp_back",
    )(counts, outer, g, mid, gout, db, g2, wm)


def attn_back_body(joined_ref, probs_ref, gmix_ref, grad_ref):
    slots = joined_ref.shape[0]
    low = head_masks(slots)
    for pair in range(PAIRS):
        cols = slice(pair * LANES, (pair + 1) * LANES)
        q = stack_heads(joined_ref[:, cols], low)
        k = joined_ref[:, D + pair * LANES : D + (pair + 1) * LANES]
        v = joined_ref[:, 2 * D + pair * LANES : 2 * D + (pair + 1) * LANES]
        out = stack_heads(gmix_ref[:, cols], low)
        low_soft = probs_ref[0, pair]
        soft = low_soft.astype(F32)
        grad_probs = dot_t(out, v)
        mean = jnp.sum(soft * grad_probs, axis=-1, keepdims=True)
        scores = (soft * (grad_probs - mean)).astype(BF)
        gq = dot(scores, k) * FACTOR
        grad_ref[:, cols] = jnp.where(low, gq[:slots], gq[slots:]).astype(BF)
        grad_ref[:, D + pair * LANES : D + (pair + 1) * LANES] = (
            t_dot(scores, q) * FACTOR
        ).astype(BF)
        grad_ref[:, 2 * D + pair * LANES : 2 * D + (pair + 1) * LANES] = t_dot(
            low_soft, out
        ).astype(BF)


def attn_back_call(call, slots, joined, probs, gmix, kept):
    total = joined.shape[0]
    steps = total // slots // 2
    row = lambda width: pl.BlockSpec((slots, width), lambda i: (call * steps + i, 0))
    in_specs = [
        row(3 * D),
        pl.BlockSpec((1, PAIRS, 2 * slots, slots), lambda i: (call * steps + i, 0, 0, 0)),
        row(D),
    ]
    args = [joined, probs, gmix]
    aliases = {}
    if kept is not None:
        in_specs.append(pl.BlockSpec(memory_space=pl.ANY))
        args.append(kept)
        aliases = {3: 0}
    return pl.pallas_call(
        lambda *refs: attn_back_body(*refs[:3], refs[-1]),
        grid=(steps,),
        in_specs=in_specs,
        out_specs=row(3 * D),
        out_shape=jax.ShapeDtypeStruct((total, 3 * D), BF),
        input_output_aliases=aliases,
        compiler_params=params(),
        cost_estimate=cost(5.5),
        name=f"attn_bwd_{call}",
    )(*args)


def attn_grad_body(ids_ref, normed_ref, mix_ref, grad_ref, branch_ref, out_ref):
    half = BLOCKS // 2

    def put(which, base, mask, value):
        for k in range(half):
            out_ref[which, (base + k) ^ mask] = value[k * BROWS : (k + 1) * BROWS, :].astype(BF)

    normed = normed_ref[...]
    put(0, 0, ids_ref[0], t_dot(normed, grad_ref[:, :D]))
    put(0, half, ids_ref[0], t_dot(normed, grad_ref[:, D : 2 * D]))
    put(1, 0, ids_ref[1], t_dot(normed, grad_ref[:, 2 * D :]))
    put(1, half, ids_ref[1], t_dot(mix_ref[...], branch_ref[...]))


def attn_grad_call(call, ids, normed, mix, grad, branch):
    total = normed.shape[0]
    half = pl.BlockSpec((total, D // 2), lambda i, ids: (0, ids[8 + call]))
    return pl.pallas_call(
        attn_grad_body,
        grid_spec=pltpu.PrefetchScalarGridSpec(
            num_scalar_prefetch=1,
            grid=(1,),
            in_specs=[half, half, full((total, 3 * D)), full((total, D))],
            out_specs=full((2, BLOCKS, BROWS, D)),
        ),
        out_shape=jax.ShapeDtypeStruct((2, BLOCKS, BROWS, D), BF),
        compiler_params=params(total),
        cost_estimate=cost(2.6),
        name=f"attn_grad_{call}",
    )(ids, normed, mix, grad, branch)


def last_body(slots, grad_ref, wj_ref, tok_ref, gmid_ref, g1_ref, out_ref, small_ref, g_ref):
    rows = tok_ref.shape[0]
    items = rows // slots
    g_ref[...] = dot_t(grad_ref[...], wj_ref[...])

    def one(item, sums):
        here = pl.ds(pl.multiple_of(item * slots, 16), slots)
        xhat, rstd = stats(tok_ref[here, :].astype(F32))
        g = g_ref[here, :]
        e = g * g1_ref[...]
        mean_e = jnp.mean(e, axis=-1, keepdims=True)
        mean_x = jnp.mean(e * xhat, axis=-1, keepdims=True)
        out_ref[here, :] = (gmid_ref[here, :] + rstd * (e - mean_e - xhat * mean_x)).astype(BF)
        row = lambda a: jnp.sum(a, axis=0, keepdims=True)
        return (
            sums[0] + row(grad_ref[here, :D].astype(F32)),
            sums[1] + row(grad_ref[here, 2 * D :].astype(F32)),
            sums[2] + row(g * xhat),
            sums[3] + row(g),
        )

    zero = jnp.zeros((1, D), F32)
    sums = lax.fori_loop(0, items, one, (zero,) * 4)
    for k in range(4):
        small_ref[k : k + 1, :] = sums[k]
    small_ref[4:8, :] = jnp.zeros((4, D), F32)


def last_call(slots, grad, wj, tok, gmid, g1):
    total = tok.shape[0]
    return pl.pallas_call(
        lambda *refs: last_body(slots, *refs),
        grid=(1,),
        in_specs=[full(a.shape) for a in (grad, wj, tok, gmid, g1)],
        out_specs=[full((total, D)), full((8, D))],
        out_shape=[
            jax.ShapeDtypeStruct((total, D), BF),
            jax.ShapeDtypeStruct((8, D), F32),
        ],
        scratch_shapes=[pltpu.VMEM((total, D), F32)],
        compiler_params=params(total),
        cost_estimate=cost(5.6),
        name="first_back",
    )(grad, wj, tok, gmid, g1)


def finish_mlp_body(groups, ids_ref, a_ref, b_ref, *rest):
    for ab, in_ref in enumerate((a_ref, b_ref)):
        mask = ids_ref[ab] & (groups - 1)
        for k in range(groups):
            rest[ab - 2][k * BROWS : (k + 1) * BROWS, :] = in_ref[k ^ mask].astype(F32)


def finish_mlp_call(chunk, which, ids, a, b, kept):
    groups = 4
    steps = BLOCKS // groups

    def place(ab):
        def index(i, ids):
            at = (ids[ab] // groups) ^ i
            quarter = 2 * chunk + (ids[3] ^ which)
            return (quarter * steps + at, 0) if ab == 0 else (at, quarter)

        return index

    in_specs = [pl.BlockSpec((groups, BROWS, D), lambda i, ids: (i, 0, 0))] * 2
    args = [ids, a, b]
    aliases = {}
    if kept is not None:
        in_specs += [pl.BlockSpec(memory_space=pl.ANY)] * 2
        args += list(kept)
        aliases = {3: 0, 4: 1}
    return pl.pallas_call(
        lambda *refs: finish_mlp_body(groups, *refs),
        grid_spec=pltpu.PrefetchScalarGridSpec(
            num_scalar_prefetch=1,
            grid=(steps,),
            in_specs=in_specs,
            out_specs=[pl.BlockSpec((groups * BROWS, D), place(ab)) for ab in range(2)],
        ),
        out_shape=[jax.ShapeDtypeStruct(shape, F32) for shape in ((FF, D), (D, FF))],
        input_output_aliases=aliases,
        compiler_params=params(),
        cost_estimate=cost(3.2),
        name=f"finish_mlp_{chunk}_{which}",
    )(*args)


def finish_attn_body(ids_ref, a_ref, b_ref, *rest):
    joined_ref, merge_ref = rest[-2:]
    half = BLOCKS // 2
    for ab, in_ref in enumerate((a_ref, b_ref)):
        mask = ids_ref[ab]
        for i in range(BLOCKS):
            block = in_ref[i ^ mask].astype(F32)
            third, k = 2 * ab + i // half, i % half
            rows = slice(k * BROWS, (k + 1) * BROWS)
            if third < 3:
                joined_ref[rows, third * D : (third + 1) * D] = block
            else:
                merge_ref[rows, :] = block


def finish_attn_call(which, ids, a, b, kept):
    in_specs = [full(a.shape), full(b.shape)]
    args = [ids, a, b]
    aliases = {}
    if kept is not None:
        in_specs += [pl.BlockSpec(memory_space=pl.ANY)] * 2
        args += list(kept)
        aliases = {3: 0, 4: 1}
    place = lambda i, ids: (ids[3] ^ which, 0)
    return pl.pallas_call(
        finish_attn_body,
        grid_spec=pltpu.PrefetchScalarGridSpec(
            num_scalar_prefetch=1,
            grid=(1,),
            in_specs=in_specs,
            out_specs=[pl.BlockSpec((D // 2, 3 * D), place), pl.BlockSpec((D // 2, D), place)],
        ),
        out_shape=[jax.ShapeDtypeStruct(s, F32) for s in ((D, 3 * D), (D, D))],
        input_output_aliases=aliases,
        compiler_params=params(),
        cost_estimate=cost(4.2),
        name=f"finish_attn_{which}",
    )(*args)


def finish_small_body(mine_ref, got_ref, *outs):
    mine = mine_ref[...].astype(F32)
    got = got_ref[0].astype(F32)
    total = mine[0:12, :] + mine[12:24, :] + (got[0:12, :] + got[12:24, :])
    for k in range(4):
        outs[0][pl.ds(k * D, D)] = total[k]
    for out, k in zip(outs[1:7], (4, 5, 6, 7, 10, 11)):
        out[...] = total[k]
    outs[7][...] = total[8:10, :]


def finish_small_call(mine, got):
    vector = lambda n: jax.ShapeDtypeStruct((n,), F32)
    shapes = [vector(FF)] + [vector(D)] * 6 + [jax.ShapeDtypeStruct((2, D), F32)]
    return pl.pallas_call(
        finish_small_body,
        grid=(1,),
        in_specs=[
            full(mine.shape),
            pl.BlockSpec((1, BROWS, D), lambda i: (got.shape[0] - 1, 0, 0)),
        ],
        out_specs=[full(s.shape) for s in shapes],
        out_shape=shapes,
        compiler_params=params(),
        cost_estimate=cost(1),
        name="finish_small",
    )(mine, got)


def stage_lists(sizes):
    bits = {axis: [(axis, b) for b in range(size.bit_length() - 1)] for axis, size in sizes.items()}
    dp, group = bits["dp"], bits["group"]
    if len(dp) == 2 and len(group) == 3:
        order = group + dp
    else:
        order = [dp[0], group[0], group[-1]] + dp[1:] + group[1:-1]
    return order[0], order[1:3], order[3:]


def add(a, b):
    return (a.astype(F32) + b.astype(F32)).astype(BF)


def bit_of(stage):
    return (lax.axis_index(stage[0]) >> stage[1]) & 1


def tie(*values):
    return lax.optimization_barrier(values)


class Chain:
    def __init__(self):
        self.last = None

    def after(self, value):
        if self.last is None:
            return value
        value, _ = tie(value, self.last)
        return value

    def run(self, step, value):
        out = step(self.after(value))
        self.last = jax.tree.leaves(out)[0]
        return out


class Chunk:
    def __init__(self, sums, chain):
        self.sums = sums
        self.chain = chain
        self.down_at = 0
        self.small = None

    def first(self, send):
        self.got = self.sums.swap(send, self.sums.first)

    def pair(self, at, keep=None):
        if keep is not None:
            self.keep = keep
        got = self.chain.after(self.got)
        both = [self.sums.halve(self.keep[ab], got[ab]) for ab in range(2)]
        self.keep = [b[0] for b in both]
        out = [b[1] for b in both]
        self.chain.last = out
        self.got = [self.sums.swap(out[ab], self.sums.stage(ab, at)) for ab in range(2)]

    def tail_down(self, small=None):
        at = self.down_at
        got = self.chain.after(self.got)
        if at == 0:
            mine = jnp.stack([add(self.keep[ab], got[ab]) for ab in range(2)])
        else:
            mine = add(self.keep, got)
        self.down_at += 1
        if at < len(self.sums.rest):
            self.keep, out = self.sums.tail_down(at, mine)
            self.chain.last = out
            self.got = self.sums.swap(out, self.sums.rest[at])
            if len(self.sums.rest) > 2 and at >= 1 and at + 1 < len(self.sums.rest):
                self.tail_down(small)
            return
        self.mine = mine
        self.chain.last = mine
        self.up_at = at
        self.small = small
        self.up(self.mine, self.sums.rest[at - 1])

    def up(self, value, stage):
        if self.small is None:
            self.got = self.sums.swap(value, stage)
            return
        self.rows = split_small(self.small)
        pad = jnp.zeros((BROWS - self.rows.shape[0], D), BF)
        block = jnp.concatenate([self.rows, pad], axis=0)[None]
        load = value.reshape((-1,) + value.shape[-2:])
        if value.shape[-2] != BROWS:
            load = load.reshape(-1, D)
            load = jnp.concatenate([load, jnp.zeros((-load.shape[0] % BROWS, D), BF)])
            load = load.reshape(-1, BROWS, D)
        self.all = self.sums.swap(jnp.concatenate([load, block], axis=0), stage)
        self.got = self.all[:-1].reshape(-1, D)[: value.size // D].reshape(value.shape)

    def small_sum(self):
        other = self.all[-1, : self.rows.shape[0]]
        self.small = join_small(self.rows) + join_small(other)

    def tail_up(self):
        at = self.up_at - 1
        got = self.chain.after(self.got)
        self.mine = self.sums.tail_up(at, self.mine, got)
        self.chain.last = self.mine
        self.up_at = at
        if self.small is not None:
            self.small_sum()
        if at:
            self.up(self.mine, self.sums.rest[at - 1])
            if at > 1:
                self.tail_up()
            return
        self.own = [self.mine[0], self.mine[1]]
        self.ups([self.sums.stage(ab, 1) for ab in range(2)])

    def ups(self, stages):
        if self.small is None:
            self.got = [self.sums.swap(self.own[ab], stages[ab]) for ab in range(2)]
            return
        self.up(self.own[0], stages[0])
        self.got = [self.got, self.sums.swap(self.own[1], stages[1])]

    def pair_up(self, at):
        got = self.chain.after(self.got)
        self.own = [jnp.concatenate([self.own[ab], got[ab]]) for ab in range(2)]
        self.chain.last = self.own
        if self.small is not None:
            self.small_sum()
        if at:
            self.ups([self.sums.stage(ab, at - 1) for ab in range(2)])
        else:
            self.ups([self.sums.first] * 2)


class Sums:
    def __init__(self, sizes):
        self.sizes = sizes
        self.first, self.pair, self.rest = stage_lists(sizes)

    def swap(self, value, stage):
        axis, bit = stage
        return lax.ppermute(value, axis, [(i, i ^ (1 << bit)) for i in range(self.sizes[axis])])

    def stage(self, ab, at):
        return self.pair[at if ab == 0 else 1 - at]

    def halve(self, mine, got, axis=0):
        n = mine.shape[axis] // 2
        low = lax.slice_in_dim(mine, 0, n, axis=axis), lax.slice_in_dim(got, 0, n, axis=axis)
        high = lax.slice_in_dim(mine, n, 2 * n, axis=axis), lax.slice_in_dim(
            got, n, 2 * n, axis=axis
        )
        return add(*low), add(*high)

    def tail_down(self, at, mine):
        if at < 2:
            n = mine.shape[1] // 2
            return mine[:, :n], mine[:, n:]
        n = mine.shape[2] // 2
        high = bit_of(self.rest[at]) == 1
        low_rows, high_rows = mine[:, :, :n], mine[:, :, n:]
        return jnp.where(high, high_rows, low_rows), jnp.where(high, low_rows, high_rows)

    def tail_up(self, at, mine, got):
        if at < 2:
            return jnp.concatenate([mine, got], axis=1)
        high = bit_of(self.rest[at]) == 1
        return jnp.concatenate([jnp.where(high, got, mine), jnp.where(high, mine, got)], axis=2)


def split_small(value):
    high = lax.reduce_precision(value, 8, 7)
    return jnp.concatenate([high.astype(BF), (value - high).astype(BF)], axis=0)


def join_small(value):
    n = value.shape[0] // 2
    return value[:n].astype(F32) + value[n:].astype(F32)


def solution(mesh):
    sizes = dict(mesh.shape)
    sums = Sums(sizes)

    def shards(
        tokens,
        cotangent,
        counts,
        first_gain,
        first_shift,
        joined_weight,
        joined_bias,
        merge_weight,
        merge_bias,
        second_gain,
        second_shift,
        up_weight,
        up_bias,
        down_weight,
        down_bias,
    ):
        items, slots, features = tokens.shape
        total = items * slots
        row = lambda a: a.reshape(1, -1)
        tok = tokens.reshape(total, features)
        cot = cotangent.reshape(total, features)
        counts = counts.astype(jnp.int32)
        masks = []
        for two in (sums.pair, sums.pair[::-1]):
            mask = 0
            for stage in list(two) + list(sums.rest[:2]):
                mask = 2 * mask + bit_of(stage)
            masks.append(mask)
        core = bit_of(sums.first)
        other = 1 - core
        ids = jnp.stack(
            [masks[0], masks[1], core, core, other, core, 2 + other, 2 + core, other, core]
        ).astype(jnp.int32)

        normed, joined, probs, mix, middle, second, gout = first_call(
            4,
            slots,
            counts,
            tok,
            cot,
            joined_weight,
            merge_weight,
            first_gain,
            first_shift,
            joined_bias,
            merge_bias,
            second_gain,
            second_shift,
        )
        chain = Chain()

        acts, ghs = [], []

        def quarter(call):
            def step(ids):
                return quarter_call(
                    call, ids, second, gout, up_weight, row(up_bias), down_weight
                )

            grad, act, gh = chain.run(step, ids)
            acts.append(act)
            ghs.append(gh)
            return grad

        def collect(chunk, kept):
            pick = slice(2 * chunk, 2 * chunk + 2)
            return chain.run(
                lambda ids: collect_call(
                    chunk, ids, acts[pick], ghs[pick], down_weight, up_weight, kept
                ),
                ids,
            )

        def finish(chunk, which, kept):
            part = chunks[chunk].got if which else chunks[chunk].own
            return chain.run(
                lambda a: finish_mlp_call(chunk, which, ids, a, part[1], kept), part[0]
            )

        chunks = [Chunk(sums, chain) for _ in range(3)]
        one, two, three = chunks
        one.first(quarter(0))
        keep = quarter(1)
        kept = collect(0, None)
        one.pair(0, keep)
        send = quarter(2)
        keep = quarter(3)
        two.first(chain.after(send))
        outer, g, small_a = collect(1, kept)
        two.pair(0, keep)
        one.pair(1)
        result, gmid, branch, gmix, small_b = chain.run(
            lambda outer: middle_call(
                slots, counts, outer, g, middle, gout, down_bias, second_gain, merge_weight
            ),
            outer,
        )
        grad_joined = chain.run(
            lambda gmix: attn_back_call(0, slots, joined, probs, gmix, None), gmix
        )
        grad_joined = chain.run(
            lambda gmix: attn_back_call(1, slots, joined, probs, gmix, grad_joined), gmix
        )
        one.tail_down()
        attn_grad = lambda call: chain.run(
            lambda ids: attn_grad_call(call, ids, normed, mix, grad_joined, branch), ids
        )
        send = attn_grad(0)
        two.pair(1)
        keep = attn_grad(1)
        three.first(chain.after(send))
        one.tail_down()
        three.pair(0, keep)
        two.tail_down()
        one.tail_down()
        two.tail_down()
        one.tail_up()
        three.pair(1)
        two.tail_down()
        one.tail_up()
        three.tail_down()
        one.pair_up(1)
        two.tail_up()
        three.tail_down()
        token_grad, small_c = chain.run(
            lambda grad: last_call(slots, grad, joined_weight, tok, gmid, first_gain),
            grad_joined,
        )
        small = jnp.concatenate([small_a, small_b, small_c[:4]], axis=0)
        three.tail_down(small)
        two.tail_up()
        three.tail_up()
        two.pair_up(1)
        three.tail_up()
        one.pair_up(0)
        mlp = finish(0, 0, None)
        three.pair_up(1)
        two.pair_up(0)
        mlp = finish(0, 1, mlp)
        mlp = finish(1, 0, mlp)
        mlp = finish(1, 1, mlp)
        three.pair_up(0)
        attn = chain.run(
            lambda a: finish_attn_call(0, ids, a, three.own[1], None), three.own[0]
        )
        small = finish_small_call(three.rows, three.all)
        joined_grad, merge_grad = finish_attn_call(1, ids, three.all, three.got[1], attn)
        down_grad, up_grad = mlp
        return (
            result.reshape(tokens.shape),
            token_grad.reshape(tokens.shape),
            small[5],
            small[6],
            joined_grad,
            small[7],
            merge_grad,
            small[4],
            small[2],
            small[3],
            up_grad,
            small[0],
            down_grad,
            small[1],
        )

    spread = P(("dp", "group"), None, None)
    return jax.shard_map(
        shards,
        mesh=mesh,
        in_specs=(spread, spread, P(("dp", "group"))) + (P(),) * 12,
        out_specs=(spread, spread) + (P(),) * 12,
        check_vma=False,
    )
```

```python
import math

import jax
import jax.numpy as jnp
from jax import lax
from jax.experimental import pallas as pl
from jax.experimental.pallas import tpu as pltpu
from jax.sharding import PartitionSpec as P

D = 768
HEADS = 12
HEAD_DIM = 64
FF = 3072
PAIRS = HEADS // 2
LANES = 2 * HEAD_DIM
EPS = 1e-06
NEG = -1e30
BF = jnp.bfloat16
F32 = jnp.float32
FACTOR = HEAD_DIM ** (-0.5)
BLOCKS = 16
BROWS = D // BLOCKS
SCALE = 10


def dot(a, b):
    return jnp.dot(a, b, preferred_element_type=F32)


def dot_t(a, b):
    return lax.dot_general(a, b, (((1,), (1,)), ((), ())), preferred_element_type=F32)


def t_dot(a, b):
    return lax.dot_general(a, b, (((0,), (0,)), ((), ())), preferred_element_type=F32)


def stats(x):
    centred = x - jnp.mean(x, axis=-1, keepdims=True)
    rstd = lax.rsqrt(jnp.mean(centred * centred, axis=-1, keepdims=True) + EPS)
    return centred * rstd, rstd


def pin(value):
    return pltpu.with_memory_space_constraint(value, pltpu.HBM)


HERE = pl.BlockSpec(memory_space=pltpu.VMEM)


def held(rows, shape, dtype):
    if rows <= 640:
        return pltpu.VMEM(shape, dtype)
    return jax.ShapeDtypeStruct(shape, dtype)


def vmem(limit):
    return pltpu.CompilerParams(vmem_limit_bytes=limit * 1024 * 1024)


def params(rows=640):
    return vmem(20 if rows <= 640 else 48)


def cost(us):
    return pl.CostEstimate(flops=int(us * SCALE * 1e9), bytes_accessed=1000, transcendentals=0)


def full(shape):
    return pl.BlockSpec(shape, lambda *_: (0,) * len(shape))


def head_masks(rows):
    lane = lax.broadcasted_iota(jnp.int32, (rows, LANES), 1)
    return lane < HEAD_DIM


def stack_heads(pair, low):
    zero = jnp.zeros_like(pair)
    return jnp.concatenate([jnp.where(low, pair, zero), jnp.where(low, zero, pair)], axis=0)


def first_body(
    slots,
    counts_ref,
    tok_hbm,
    cot_hbm,
    wj_hbm,
    wm_hbm,
    g1_ref,
    s1_ref,
    jb_ref,
    mb_ref,
    g2_ref,
    s2_ref,
    normed_ref,
    joined_ref,
    probs_ref,
    mix_ref,
    middle_ref,
    second_ref,
    gout_ref,
    tok_ref,
    cot_ref,
    wj_ref,
    wm_ref,
    sem,
):
    step = pl.program_id(0)
    rows = tok_ref.shape[0]
    items = rows // slots
    span = pl.ds(pl.multiple_of(step * rows, 16), rows)
    tok_copy = pltpu.make_async_copy(tok_hbm.at[span], tok_ref, sem.at[0])
    cot_copy = pltpu.make_async_copy(cot_hbm.at[span], cot_ref, sem.at[1])
    wm_copy = pltpu.make_async_copy(wm_hbm, wm_ref, sem.at[2])
    wj_copies = [
        pltpu.make_async_copy(
            wj_hbm.at[:, pl.ds(third * D, D)], wj_ref.at[third], sem.at[3 + third]
        )
        for third in range(3)
    ]
    tok_copy.start()

    @pl.when(step == 0)
    def _():
        for copy in wj_copies:
            copy.start()

    cot_copy.start()

    @pl.when(step == 0)
    def _():
        wm_copy.start()

    tok_copy.wait()
    xhat, _ = stats(tok_ref[...].astype(F32))
    normed = (xhat * g1_ref[...] + s1_ref[...]).astype(BF)
    normed_ref[...] = normed
    for third in range(3):
        cols = slice(third * D, (third + 1) * D)

        @pl.when(step == 0)
        def _():
            wj_copies[third].wait()

        part = dot(normed, wj_ref[third])
        if third == 0:
            part = part + jb_ref[0:1, :]
        if third == 2:
            part = part + jb_ref[1:2, :]
        joined_ref[:, cols] = part.astype(BF)
    cot_copy.wait()
    low = head_masks(slots)
    key_slot = lax.broadcasted_iota(jnp.int32, (slots, 2 * slots), 0)
    row_slot = lax.broadcasted_iota(jnp.int32, (slots, D), 0)

    def one(item, carry):
        count = counts_ref[step * items + item]
        here = pl.ds(pl.multiple_of(item * slots, 16), slots)
        seen = row_slot < count
        cot = cot_ref[here, :]
        gout_ref[here, :] = jnp.where(seen, cot, jnp.zeros_like(cot))
        allowed = key_slot < count
        for pair in range(PAIRS):
            cols = slice(pair * LANES, (pair + 1) * LANES)
            q = stack_heads(joined_ref[here, cols] * BF(FACTOR), low)
            k = joined_ref[here, D + pair * LANES : D + (pair + 1) * LANES]
            v = joined_ref[here, 2 * D + pair * LANES : 2 * D + (pair + 1) * LANES]
            scores = jnp.where(allowed, dot_t(k, q), NEG)
            raised = jnp.exp(scores - jnp.max(scores, axis=0, keepdims=True))
            soft = (raised * (1.0 / jnp.sum(raised, axis=0, keepdims=True))).astype(BF)
            probs_ref[item, pair] = soft
            mixed = t_dot(soft, v)
            mix_ref[here, cols] = jnp.where(low, mixed[:slots], mixed[slots:]).astype(BF)
        return carry

    lax.fori_loop(0, items, one, 0)

    @pl.when(step == 0)
    def _():
        wm_copy.wait()

    for part in range(2):
        here = slice(part * rows // 2, (part + 1) * rows // 2)
        there = pl.ds(pl.multiple_of(step * rows + part * rows // 2, 16), rows // 2)
        middle = tok_ref[here, :].astype(F32) + dot(mix_ref[here, :], wm_ref[...]) + mb_ref[...]
        middle_ref[here, :] = middle
        xhat, _ = stats(middle)
        second_ref[here, :] = (xhat * g2_ref[...] + s2_ref[...]).astype(BF)


def first_call(slots, counts, tok, cot, wj, wm, g1, s1, jb, mb, g2, s2):
    total = tok.shape[0]
    hbm = pl.BlockSpec(memory_space=pltpu.HBM)
    out = lambda width, dt: held(total, (total, width), dt)
    return pl.pallas_call(
        lambda *refs: first_body(slots, *refs),
        grid_spec=pltpu.PrefetchScalarGridSpec(
            num_scalar_prefetch=1,
            grid=(1,),
            in_specs=[hbm] * 4 + [full(a.shape) for a in (g1, s1, jb, mb, g2, s2)],
            out_specs=[HERE] * 7,
            scratch_shapes=[
                pltpu.VMEM((total, D), BF),
                pltpu.VMEM((total, D), BF),
                pltpu.VMEM((3, D, D), BF),
                pltpu.VMEM((D, D), BF),
                pltpu.SemaphoreType.DMA((6,)),
            ],
        ),
        out_shape=[
            out(D, BF),
            out(3 * D, BF),
            held(total, (total // slots, PAIRS, slots, 2 * slots), BF),
            out(D, BF),
            out(D, F32),
            out(D, BF),
            out(D, BF),
        ],
        compiler_params=vmem(20 if total <= 640 else 56),
        cost_estimate=cost(15),
        name="attn_fwd",
    )(*[pin(a) for a in (counts, tok, cot, wj, wm, g1, s1, jb, mb, g2, s2)])


def put_blocks(ref, which, mask, value):
    for k in range(BLOCKS):
        ref[which, k ^ mask] = value[k * BROWS : (k + 1) * BROWS, :].astype(BF)


def quarter_body(parts, ids_ref, sec_ref, gout_ref, up_ref, ub_ref, down_ref, *outs):
    grad_ref, act_ref, gh_ref = outs
    rows = sec_ref.shape[0] // parts
    for part in range(parts):
        here = slice(part * rows, (part + 1) * rows)
        hidden = dot(sec_ref[here, :], up_ref[...]) + ub_ref[...]
        grad_act = dot_t(gout_ref[here, :], down_ref[...])
        cdf = 0.5 + 0.5 * lax.erf(hidden * (0.5**0.5))
        act_ref[here, :] = (hidden * cdf).astype(BF)
        slope = cdf + hidden * (jnp.exp(-0.5 * hidden * hidden) * ((2 * math.pi) ** -0.5))
        gh_ref[here, :] = (grad_act * slope).astype(BF)
    put_blocks(grad_ref, 0, ids_ref[0], t_dot(act_ref[...], gout_ref[...]))
    put_blocks(grad_ref, 1, ids_ref[1], t_dot(sec_ref[...], gh_ref[...]))


def quarter_call(call, ids, second, gout, up, ub, down):
    total = second.shape[0]
    return pl.pallas_call(
        lambda *refs: quarter_body(2, *refs),
        grid_spec=pltpu.PrefetchScalarGridSpec(
            num_scalar_prefetch=1,
            grid=(1,),
            in_specs=[
                HERE,
                HERE,
                pl.BlockSpec((D, D), lambda i, ids: (0, ids[4 + call])),
                pl.BlockSpec((1, D), lambda i, ids: (0, ids[4 + call])),
                pl.BlockSpec((D, D), lambda i, ids: (ids[4 + call], 0)),
            ],
            out_specs=[HERE] * 3,
        ),
        out_shape=[
            held(total, (2, BLOCKS, BROWS, D), BF),
            held(total, (total, D), BF),
            held(total, (total, D), BF),
        ],
        compiler_params=params(total),
        cost_estimate=cost(4.3),
        name=f"mlp_{call}",
    )(ids, second, gout, up, ub, down)


def collect_body(chunk, ids_ref, *refs):
    acts, ghs = refs[:2], refs[2:4]
    down_ref, up_ref = refs[4:6]
    kept = refs[6:-3]
    outer_ref, g_ref, small_ref = refs[-3:]
    step = pl.program_id(0)
    for at in range(2):

        @pl.when(step == at)
        def _():
            outer = dot(acts[at][...], down_ref[...])
            g = dot_t(ghs[at][...], up_ref[...])
            if at:
                outer = outer + outer_ref[...]
                g = g + g_ref[...]
            elif chunk:
                outer = outer + kept[0][...]
                g = g + kept[1][...]
                small_ref[...] = kept[2][...]
            outer_ref[...] = outer
            g_ref[...] = g
            small_ref[pl.ds(ids_ref[4 + 2 * chunk + at], 1), :] = jnp.sum(
                ghs[at][...].astype(F32), axis=0, keepdims=True
            )


def collect_call(chunk, ids, acts, ghs, down, up, kept):
    total = acts[0].shape[0]
    return pl.pallas_call(
        lambda *refs: collect_body(chunk, *refs),
        grid_spec=pltpu.PrefetchScalarGridSpec(
            num_scalar_prefetch=1,
            grid=(2,),
            in_specs=[HERE] * 4
            + [
                pl.BlockSpec((D, D), lambda i, ids: (ids[4 + 2 * chunk + i], 0)),
                pl.BlockSpec((D, D), lambda i, ids: (0, ids[4 + 2 * chunk + i])),
            ]
            + [HERE] * (3 if chunk else 0),
            out_specs=[HERE] * 3,
        ),
        out_shape=[
            held(total, (total, D), F32),
            held(total, (total, D), F32),
            held(total, (4, D), F32),
        ],
        compiler_params=vmem(16 if total <= 640 else 56),
        cost_estimate=cost(4.3),
        name=f"mlp_collect_{chunk}",
    )(ids, *acts, *ghs, down, up, *(kept or ()))


def middle_body(
    slots,
    counts_ref,
    outer_ref,
    g_ref,
    mid_ref,
    gout_ref,
    db_ref,
    g2_ref,
    wm_ref,
    result_ref,
    gmid_ref,
    branch_ref,
    gmix_ref,
    small_ref,
):
    items = mid_ref.shape[0] // slots
    row_slot = lax.broadcasted_iota(jnp.int32, (slots, D), 0)

    def one(item, sums):
        here = pl.ds(pl.multiple_of(item * slots, 16), slots)
        seen = row_slot < counts_ref[item]
        middle = mid_ref[here, :]
        total = middle + outer_ref[here, :] + db_ref[...]
        result_ref[here, :] = jnp.where(seen, total, 0.0).astype(BF)
        gout = gout_ref[here, :].astype(F32)
        xhat, rstd = stats(middle)
        g = g_ref[here, :]
        e = g * g2_ref[...]
        mean_e = jnp.mean(e, axis=-1, keepdims=True)
        mean_x = jnp.mean(e * xhat, axis=-1, keepdims=True)
        grad = gout + rstd * (e - mean_e - xhat * mean_x)
        gmid_ref[here, :] = grad
        branch = grad.astype(BF)
        branch_ref[here, :] = branch
        row = lambda a: jnp.sum(a, axis=0, keepdims=True)
        return (
            sums[0] + row(gout),
            sums[1] + row(g * xhat),
            sums[2] + row(g),
            sums[3] + row(branch.astype(F32)),
        )

    zero = jnp.zeros((1, D), F32)
    sums = lax.fori_loop(0, items, one, (zero,) * 4)
    for k in range(4):
        small_ref[k : k + 1, :] = sums[k]
    gmix_ref[...] = dot_t(branch_ref[...], wm_ref[...]).astype(BF)


def middle_call(slots, counts, outer, g, mid, gout, db, g2, wm):
    total = mid.shape[0]
    hbm = jax.ShapeDtypeStruct((total, D), BF)
    return pl.pallas_call(
        lambda *refs: middle_body(slots, *refs),
        grid_spec=pltpu.PrefetchScalarGridSpec(
            num_scalar_prefetch=1,
            grid=(1,),
            in_specs=[HERE] * 4 + [full(db.shape), full(g2.shape), full((D, D))],
            out_specs=[full((total, D))] + [HERE] * 4,
        ),
        out_shape=[
            hbm,
            held(total, (total, D), F32),
            held(total, (total, D), BF),
            held(total, (total, D), BF),
            held(total, (4, D), F32),
        ],
        compiler_params=params(total),
        cost_estimate=cost(3.6),
        name="mlp_back",
    )(counts, outer, g, mid, gout, db, g2, wm)


def attn_back_body(slots, first, joined_ref, probs_ref, gmix_ref, grad_ref):
    low = head_masks(slots)
    items = joined_ref.shape[0] // slots // 2

    def one(at, carry):
        item = first * items + at
        here = pl.ds(pl.multiple_of(item * slots, 16), slots)
        for pair in range(PAIRS):
            cols = slice(pair * LANES, (pair + 1) * LANES)
            key_cols = slice(D + pair * LANES, D + (pair + 1) * LANES)
            value_cols = slice(2 * D + pair * LANES, 2 * D + (pair + 1) * LANES)
            q = stack_heads(joined_ref[here, cols] * BF(FACTOR), low)
            out = stack_heads(gmix_ref[here, cols], low)
            low_soft = probs_ref[item, pair]
            soft = low_soft.astype(F32)
            grad_probs = dot_t(joined_ref[here, value_cols], out)
            mean = jnp.sum(soft * grad_probs, axis=0, keepdims=True)
            scores = (soft * (grad_probs - mean)).astype(BF)
            gq = t_dot(scores, joined_ref[here, key_cols] * BF(FACTOR))
            grad_ref[here, cols] = jnp.where(low, gq[:slots], gq[slots:]).astype(BF)
            grad_ref[here, key_cols] = dot(scores, q).astype(BF)
            grad_ref[here, value_cols] = dot(low_soft, out).astype(BF)
        return carry

    lax.fori_loop(0, items, one, 0)


def attn_back_call(call, slots, joined, probs, gmix, kept):
    total = joined.shape[0]
    args = [joined, probs, gmix]
    aliases = {}
    if kept is not None:
        args.append(kept)
        aliases = {3: 0}
    return pl.pallas_call(
        lambda *refs: attn_back_body(slots, call, *refs[:3], refs[-1]),
        grid=(1,),
        in_specs=[HERE] * len(args),
        out_specs=HERE,
        out_shape=held(total, (total, 3 * D), BF),
        input_output_aliases=aliases,
        compiler_params=vmem(8 if total <= 640 else 48),
        cost_estimate=cost(5.5),
        name=f"attn_bwd_{call}",
    )(*args)


def attn_grad_body(ids_ref, normed_ref, mix_ref, grad_ref, branch_ref, qk_ref, vm_ref):
    def put(ref, which, value):
        mask = ids_ref[which] >> 1
        for k in range(BLOCKS // 2):
            ref[which, k ^ mask] = value[k * BROWS : (k + 1) * BROWS, :].astype(BF)

    normed = normed_ref[...]
    put(qk_ref, 0, t_dot(normed, grad_ref[:, :D]))
    put(qk_ref, 1, t_dot(normed, grad_ref[:, D : 2 * D]))
    put(vm_ref, 0, t_dot(normed, grad_ref[:, 2 * D :]))
    put(vm_ref, 1, t_dot(mix_ref[...], branch_ref[...]))


def attn_grad_call(call, ids, normed, mix, grad, branch):
    total = normed.shape[0]
    half = pl.BlockSpec((total, D // 2), lambda i, ids: (0, ids[8 + call]))
    shape = (2, BLOCKS // 2, BROWS, D)
    return pl.pallas_call(
        attn_grad_body,
        grid_spec=pltpu.PrefetchScalarGridSpec(
            num_scalar_prefetch=1,
            grid=(1,),
            in_specs=[half, half, HERE, HERE],
            out_specs=[HERE] * 2,
        ),
        out_shape=[held(total, shape, BF)] * 2,
        compiler_params=params(total),
        cost_estimate=cost(2.6),
        name=f"attn_grad_{call}",
    )(ids, normed, mix, grad, branch)


def last_body(slots, grad_ref, wj_ref, tok_ref, gmid_ref, g1_ref, out_ref, small_ref, g_ref):
    rows = tok_ref.shape[0]
    items = rows // slots
    g_ref[...] = dot_t(grad_ref[...], wj_ref[...])

    def one(item, sums):
        here = pl.ds(pl.multiple_of(item * slots, 16), slots)
        xhat, rstd = stats(tok_ref[here, :].astype(F32))
        g = g_ref[here, :]
        e = g * g1_ref[...]
        mean_e = jnp.mean(e, axis=-1, keepdims=True)
        mean_x = jnp.mean(e * xhat, axis=-1, keepdims=True)
        out_ref[here, :] = (gmid_ref[here, :] + rstd * (e - mean_e - xhat * mean_x)).astype(BF)
        row = lambda a: jnp.sum(a, axis=0, keepdims=True)
        return (
            sums[0] + row(grad_ref[here, :D].astype(F32)),
            sums[1] + row(grad_ref[here, 2 * D :].astype(F32)),
            sums[2] + row(g * xhat),
            sums[3] + row(g),
        )

    zero = jnp.zeros((1, D), F32)
    sums = lax.fori_loop(0, items, one, (zero,) * 4)
    for k in range(4):
        small_ref[k : k + 1, :] = sums[k]
    small_ref[4:8, :] = jnp.zeros((4, D), F32)


def last_call(slots, grad, wj, tok, gmid, g1):
    total = tok.shape[0]
    return pl.pallas_call(
        lambda *refs: last_body(slots, *refs),
        grid=(1,),
        in_specs=[HERE, full(wj.shape), full(tok.shape), HERE, full(g1.shape)],
        out_specs=[full((total, D)), full((8, D))],
        out_shape=[
            jax.ShapeDtypeStruct((total, D), BF),
            jax.ShapeDtypeStruct((8, D), F32),
        ],
        scratch_shapes=[pltpu.VMEM((total, D), F32)],
        compiler_params=params(total),
        cost_estimate=cost(0.001),
        name="first_back",
    )(grad, wj, tok, gmid, g1)


def finish_mlp_body(groups, ids_ref, a_ref, b_ref, *rest):
    for ab, in_ref in enumerate((a_ref, b_ref)):
        mask = ids_ref[ab] & (groups - 1)
        for k in range(groups):
            rest[ab - 2][k * BROWS : (k + 1) * BROWS, :] = in_ref[k ^ mask].astype(F32)


def finish_mlp_call(chunk, which, ids, a, b, kept):
    groups = 4
    steps = BLOCKS // groups

    def place(ab):
        def index(i, ids):
            at = (ids[ab] // groups) ^ i
            quarter = 2 * chunk + (ids[3] ^ which)
            return (quarter * steps + at, 0) if ab == 0 else (at, quarter)

        return index

    in_specs = [pl.BlockSpec((groups, BROWS, D), lambda i, ids: (i, 0, 0))] * 2
    args = [ids, a, b]
    aliases = {}
    if kept is not None:
        in_specs += [pl.BlockSpec(memory_space=pl.ANY)] * 2
        args += list(kept)
        aliases = {3: 0, 4: 1}
    return pl.pallas_call(
        lambda *refs: finish_mlp_body(groups, *refs),
        grid_spec=pltpu.PrefetchScalarGridSpec(
            num_scalar_prefetch=1,
            grid=(steps,),
            in_specs=in_specs,
            out_specs=[pl.BlockSpec((groups * BROWS, D), place(ab)) for ab in range(2)],
        ),
        out_shape=[jax.ShapeDtypeStruct(shape, F32) for shape in ((FF, D), (D, FF))],
        input_output_aliases=aliases,
        compiler_params=params(),
        cost_estimate=cost(0.001),
        name=f"finish_mlp_{chunk}_{which}",
    )(*args)


def finish_attn_body(chunk, ids_ref, a_ref, b_ref, *rest):
    for ab, in_ref in enumerate((a_ref, b_ref)):
        mask = ids_ref[ab] >> 1
        for k in range(BLOCKS // 2):
            block = in_ref[k ^ mask].astype(F32)
            rows = slice(k * BROWS, (k + 1) * BROWS)
            if chunk == 2:
                rest[-1][rows, ab * D : (ab + 1) * D] = block
            else:
                rest[ab - 2][rows, :] = block


def finish_attn_call(chunk, which, ids, a, b, joined, merge):
    half = (D // 2, D)
    top = lambda ids: ids[3] ^ which
    out_specs = [pl.BlockSpec((D // 2, 2 * D), lambda i, ids: (top(ids), 0))]
    shapes = [(D, 3 * D)]
    if chunk == 3:
        out_specs = [
            pl.BlockSpec(half, lambda i, ids: (top(ids), 2)),
            pl.BlockSpec(half, lambda i, ids: (top(ids), 0)),
        ]
        shapes.append((D, D))
    kept = [joined, merge][: len(shapes)]
    aliases = {}
    args = [ids, a, b]
    for at, value in enumerate(kept):
        if value is not None:
            aliases[len(args)] = at
            args.append(value)
    return pl.pallas_call(
        lambda *refs: finish_attn_body(chunk, *refs),
        grid_spec=pltpu.PrefetchScalarGridSpec(
            num_scalar_prefetch=1,
            grid=(1,),
            in_specs=[full(a.shape), full(b.shape)]
            + [pl.BlockSpec(memory_space=pl.ANY)] * (len(args) - 3),
            out_specs=out_specs,
        ),
        out_shape=[jax.ShapeDtypeStruct(s, F32) for s in shapes],
        input_output_aliases=aliases,
        compiler_params=params(),
        cost_estimate=cost(0.001),
        name=f"finish_attn_{chunk}_{which}",
    )(*args)


def finish_small_body(mine_ref, got_ref, *outs):
    mine = mine_ref[...].astype(F32)
    got = got_ref[0].astype(F32)
    total = mine[0:12, :] + mine[12:24, :] + (got[0:12, :] + got[12:24, :])
    for k in range(4):
        outs[0][pl.ds(k * D, D)] = total[k]
    for out, k in zip(outs[1:7], (4, 5, 6, 7, 10, 11)):
        out[...] = total[k]
    outs[7][...] = total[8:10, :]


def finish_small_call(mine, got):
    vector = lambda n: jax.ShapeDtypeStruct((n,), F32)
    shapes = [vector(FF)] + [vector(D)] * 6 + [jax.ShapeDtypeStruct((2, D), F32)]
    return pl.pallas_call(
        finish_small_body,
        grid=(1,),
        in_specs=[
            full(mine.shape),
            pl.BlockSpec((1, BROWS, D), lambda i: (got.shape[0] - 1, 0, 0)),
        ],
        out_specs=[full(s.shape) for s in shapes],
        out_shape=shapes,
        compiler_params=params(),
        cost_estimate=cost(0.001),
        name="finish_small",
    )(mine, got)


def stage_lists(sizes):
    bits = {axis: [(axis, b) for b in range(size.bit_length() - 1)] for axis, size in sizes.items()}
    dp, group = bits["dp"], bits["group"]
    if len(dp) == 2 and len(group) == 3:
        order = group + dp
    else:
        order = [dp[0], group[0], group[-1]] + dp[1:] + group[1:-1]
    return order[0], order[1:3], order[3:]


def add(a, b):
    return (a.astype(F32) + b.astype(F32)).astype(BF)


def bit_of(stage):
    return (lax.axis_index(stage[0]) >> stage[1]) & 1


def tie(*values):
    return lax.optimization_barrier(values)


class Chain:
    def __init__(self):
        self.last = None

    def after(self, value):
        if self.last is None:
            return value
        value, _ = tie(value, self.last)
        return value

    def run(self, step, value):
        out = step(self.after(value))
        self.last = jax.tree.leaves(out)[0]
        return out


class Chunk:
    def __init__(self, sums, chain):
        self.sums = sums
        self.chain = chain
        self.small = None

    def first(self, send):
        self.got = self.sums.swap(send, self.sums.first)

    def pair(self, at, keep=None):
        if keep is not None:
            self.keep = keep
        got = self.chain.after(self.got)
        both = [self.sums.halve(self.keep[ab], got[ab]) for ab in range(2)]
        self.keep = [b[0] for b in both]
        out = [b[1] for b in both]
        self.chain.last = out
        self.got = [self.sums.swap(out[ab], self.sums.stage(ab, at)) for ab in range(2)]

    def tail(self, at, small=None):
        rest = self.sums.rest
        got = self.chain.after(self.got)
        if at == 0:
            mine = jnp.stack([add(self.keep[ab], got[ab]) for ab in range(2)])
            n = mine.shape[1] // 2
            self.keep, out = mine[:, :n], mine[:, n:]
            self.chain.last = out
            self.got = self.sums.swap(out, rest[0])
        elif at == 1:
            mine = add(self.keep, got)
            for stage in rest[1:-1]:
                mine, out = self.sums.split_rows(stage, mine)
                mine = add(mine, self.sums.swap(out, stage))
            self.mine = self.chain.last = mine
            self.small = small
            self.up(mine, rest[-1])
        elif at == 2:
            self.mine = add(self.mine, got)
            self.small_sum()
            for stage in rest[-2:0:-1]:
                self.up(self.mine, stage)
                self.small_sum()
                self.mine = self.sums.join_rows(stage, self.mine, self.got)
            self.chain.last = self.mine
            self.up(self.mine, rest[0])
        else:
            self.mine = jnp.concatenate([self.mine, got], axis=1)
            self.chain.last = self.mine
            self.small_sum()
            self.own = [self.mine[0], self.mine[1]]
            self.ups([self.sums.stage(ab, 1) for ab in range(2)])

    def up(self, value, stage):
        if self.small is None:
            self.got = self.sums.swap(value, stage)
            return
        self.rows = split_small(self.small)
        pad = jnp.zeros((BROWS - self.rows.shape[0], D), BF)
        block = jnp.concatenate([self.rows, pad], axis=0)[None]
        load = value.reshape((-1,) + value.shape[-2:])
        if value.shape[-2] != BROWS:
            load = load.reshape(-1, D)
            load = jnp.concatenate([load, jnp.zeros((-load.shape[0] % BROWS, D), BF)])
            load = load.reshape(-1, BROWS, D)
        self.all = self.sums.swap(jnp.concatenate([load, block], axis=0), stage)
        self.got = self.all[:-1].reshape(-1, D)[: value.size // D].reshape(value.shape)

    def small_sum(self):
        if self.small is not None:
            other = self.all[-1, : self.rows.shape[0]]
            self.small = join_small(self.rows) + join_small(other)

    def ups(self, stages):
        self.up(self.own[0], stages[0])
        self.got = [self.got, self.sums.swap(self.own[1], stages[1])]

    def pair_up(self, at):
        got = self.chain.after(self.got)
        self.own = [jnp.concatenate([self.own[ab], got[ab]]) for ab in range(2)]
        self.chain.last = self.own
        self.small_sum()
        if at:
            self.ups([self.sums.stage(ab, at - 1) for ab in range(2)])
        else:
            self.ups([self.sums.first] * 2)


class Sums:
    def __init__(self, sizes):
        self.sizes = sizes
        self.first, self.pair, self.rest = stage_lists(sizes)

    def swap(self, value, stage):
        axis, bit = stage
        return lax.ppermute(value, axis, [(i, i ^ (1 << bit)) for i in range(self.sizes[axis])])

    def stage(self, ab, at):
        return self.pair[at if ab == 0 else 1 - at]

    def halve(self, mine, got, axis=0):
        n = mine.shape[axis] // 2
        low = lax.slice_in_dim(mine, 0, n, axis=axis), lax.slice_in_dim(got, 0, n, axis=axis)
        high = lax.slice_in_dim(mine, n, 2 * n, axis=axis), lax.slice_in_dim(
            got, n, 2 * n, axis=axis
        )
        return add(*low), add(*high)

    def split_rows(self, stage, mine):
        n = mine.shape[2] // 2
        high = bit_of(stage) == 1
        low_rows, high_rows = mine[:, :, :n], mine[:, :, n:]
        return jnp.where(high, high_rows, low_rows), jnp.where(high, low_rows, high_rows)

    def join_rows(self, stage, mine, got):
        high = bit_of(stage) == 1
        return jnp.concatenate([jnp.where(high, got, mine), jnp.where(high, mine, got)], axis=2)


def split_small(value):
    high = lax.reduce_precision(value, 8, 7)
    return jnp.concatenate([high.astype(BF), (value - high).astype(BF)], axis=0)


def join_small(value):
    n = value.shape[0] // 2
    return value[:n].astype(F32) + value[n:].astype(F32)


def solution(mesh):
    sizes = dict(mesh.shape)
    sums = Sums(sizes)

    def shards(
        tokens,
        cotangent,
        counts,
        first_gain,
        first_shift,
        joined_weight,
        joined_bias,
        merge_weight,
        merge_bias,
        second_gain,
        second_shift,
        up_weight,
        up_bias,
        down_weight,
        down_bias,
    ):
        items, slots, features = tokens.shape
        total = items * slots
        row = lambda a: a.reshape(1, -1)
        tok = tokens.reshape(total, features)
        cot = cotangent.reshape(total, features)
        counts = counts.astype(jnp.int32)
        masks = []
        for two in (sums.pair, sums.pair[::-1]):
            mask = 0
            for stage in list(two) + list(sums.rest[:1]):
                mask = 2 * mask + bit_of(stage)
            masks.append(2 * mask)
        core = bit_of(sums.first)
        other = 1 - core
        ids = jnp.stack(
            [masks[0], masks[1], core, core, other, core, 2 + other, 2 + core, other, core]
        ).astype(jnp.int32)

        normed, joined, probs, mix, middle, second, gout = first_call(
            slots,
            counts,
            tok,
            cot,
            joined_weight,
            merge_weight,
            first_gain,
            first_shift,
            joined_bias,
            merge_bias,
            second_gain,
            second_shift,
        )
        chain = Chain()

        acts, ghs = {}, {}

        def quarter(call):
            def step(ids):
                return quarter_call(
                    call, ids, second, gout, up_weight, row(up_bias), down_weight
                )

            grad, act, gh = chain.run(step, ids)
            acts[call], ghs[call] = act, gh
            return grad

        def collect(chunk, kept):
            pick = (2 * chunk, 2 * chunk + 1)
            return chain.run(
                lambda ids: collect_call(
                    chunk,
                    ids,
                    [acts[call] for call in pick],
                    [ghs[call] for call in pick],
                    down_weight,
                    up_weight,
                    kept,
                ),
                ids,
            )

        done = {}

        def finish(chunk, which):
            part = chunks[chunk].got if which else chunks[chunk].own
            if chunk < 2:
                done["mlp"] = chain.run(
                    lambda a: finish_mlp_call(
                        chunk, which, ids, a, part[1], done.get("mlp")
                    ),
                    part[0],
                )
                return
            if chunk == 3 and which:
                part = chunks[3].all, part[1]
            out = chain.run(
                lambda a: finish_attn_call(
                    chunk, which, ids, a, part[1], done.get("joined"), done.get("merge")
                ),
                part[0],
            )
            done["joined"] = out[0]
            if chunk == 3:
                done["merge"] = out[1]

        chunks = [Chunk(sums, chain) for _ in range(4)]
        one, two, three, four = chunks
        one.first(quarter(0))
        keep1 = quarter(1)
        send2 = quarter(2)
        one.pair(0, keep1)
        kept = collect(0, None)
        keep2 = quarter(3)
        two.first(chain.after(send2))
        outer, g, small_a = collect(1, kept)
        one.pair(1)
        two.pair(0, keep2)
        result, gmid, branch, gmix, small_b = chain.run(
            lambda outer: middle_call(
                slots, counts, outer, g, middle, gout, down_bias, second_gain, merge_weight
            ),
            outer,
        )
        grad_joined = chain.run(
            lambda gmix: attn_back_call(0, slots, joined, probs, gmix, None), gmix
        )
        one.tail(0)
        grad_joined = chain.run(
            lambda gmix: attn_back_call(1, slots, joined, probs, gmix, grad_joined), gmix
        )
        send3, send4 = chain.run(
            lambda ids: attn_grad_call(0, ids, normed, mix, grad_joined, branch), ids
        )
        four.first(chain.after(send4))
        three.first(chain.after(send3))
        two.pair(1)
        one.tail(1)
        keep3, keep4 = chain.run(
            lambda ids: attn_grad_call(1, ids, normed, mix, grad_joined, branch), ids
        )
        three.pair(0, keep3)
        two.tail(0)
        four.pair(0, keep4)
        one.tail(2)
        two.tail(1)
        three.pair(1)
        four.pair(1)
        one.tail(3)
        three.tail(0)
        four.tail(0)
        three.tail(1)
        two.tail(2)
        one.pair_up(1)
        three.tail(2)
        token_grad, small_c = chain.run(
            lambda grad: last_call(slots, grad, joined_weight, tok, gmid, first_gain),
            grad_joined,
        )
        small = jnp.concatenate([small_a, small_b, small_c[:4]], axis=0)
        two.tail(3)
        three.tail(3)
        one.pair_up(0)
        four.tail(1, small)
        three.pair_up(1)
        two.pair_up(1)
        four.tail(2)
        three.pair_up(0)
        four.tail(3)
        finish(0, 0)
        finish(0, 1)
        finish(2, 0)
        four.pair_up(1)
        two.pair_up(0)
        finish(1, 0)
        finish(2, 1)
        four.pair_up(0)
        finish(3, 0)
        finish(1, 1)
        small = finish_small_call(four.rows, four.all)
        finish(3, 1)
        joined_grad, merge_grad = done["joined"], done["merge"]
        down_grad, up_grad = done["mlp"]
        return (
            result.reshape(tokens.shape),
            token_grad.reshape(tokens.shape),
            small[5],
            small[6],
            joined_grad,
            small[7],
            merge_grad,
            small[4],
            small[2],
            small[3],
            up_grad,
            small[0],
            down_grad,
            small[1],
        )

    spread = P(("dp", "group"), None, None)
    return jax.shard_map(
        shards,
        mesh=mesh,
        in_specs=(spread, spread, P(("dp", "group"))) + (P(),) * 12,
        out_specs=(spread, spread) + (P(),) * 12,
        check_vma=False,
    )
```

```python
import math

import jax
import jax.numpy as jnp
from jax import lax
from jax.experimental import pallas as pl
from jax.experimental.pallas import tpu as pltpu
from jax.sharding import PartitionSpec as P

D = 768
HEADS = 12
HEAD_DIM = 64
FF = 3072
PAIRS = HEADS // 2
LANES = 2 * HEAD_DIM
EPS = 1e-06
NEG = -1e30
BF = jnp.bfloat16
F32 = jnp.float32
FACTOR = HEAD_DIM ** (-0.5)
BLOCKS = 16
BROWS = D // BLOCKS
SCALE = 10


def dot(a, b):
    return jnp.dot(a, b, preferred_element_type=F32)


def dot_t(a, b):
    return lax.dot_general(a, b, (((1,), (1,)), ((), ())), preferred_element_type=F32)


def t_dot(a, b):
    return lax.dot_general(a, b, (((0,), (0,)), ((), ())), preferred_element_type=F32)


def stats(x):
    centred = x - jnp.mean(x, axis=-1, keepdims=True)
    rstd = lax.rsqrt(jnp.mean(centred * centred, axis=-1, keepdims=True) + EPS)
    return centred * rstd, rstd


def pin(value):
    return pltpu.with_memory_space_constraint(value, pltpu.HBM)


HERE = pl.BlockSpec(memory_space=pltpu.VMEM)


def held(rows, shape, dtype):
    if rows <= 640:
        return pltpu.VMEM(shape, dtype)
    return jax.ShapeDtypeStruct(shape, dtype)


def vmem(limit):
    return pltpu.CompilerParams(vmem_limit_bytes=limit * 1024 * 1024)


def params(rows=640):
    return vmem(20 if rows <= 640 else 48)


def cost(us):
    return pl.CostEstimate(flops=int(us * SCALE * 1e9), bytes_accessed=1000, transcendentals=0)


def full(shape):
    return pl.BlockSpec(shape, lambda *_: (0,) * len(shape))


def head_masks(rows):
    lane = lax.broadcasted_iota(jnp.int32, (rows, LANES), 1)
    return lane < HEAD_DIM


def stack_heads(pair, low):
    zero = jnp.zeros_like(pair)
    return jnp.concatenate([jnp.where(low, pair, zero), jnp.where(low, zero, pair)], axis=0)


def first_body(
    slots,
    counts_ref,
    tok_hbm,
    cot_hbm,
    wj_hbm,
    wm_hbm,
    g1_ref,
    s1_ref,
    jb_ref,
    mb_ref,
    g2_ref,
    s2_ref,
    normed_ref,
    joined_ref,
    probs_ref,
    mix_ref,
    middle_ref,
    second_ref,
    gout_ref,
    tok_ref,
    cot_ref,
    wj_ref,
    wm_ref,
    sem,
):
    step = pl.program_id(0)
    rows = tok_ref.shape[0]
    items = rows // slots
    span = pl.ds(pl.multiple_of(step * rows, 16), rows)
    tok_copy = pltpu.make_async_copy(tok_hbm.at[span], tok_ref, sem.at[0])
    cot_copy = pltpu.make_async_copy(cot_hbm.at[span], cot_ref, sem.at[1])
    wm_copy = pltpu.make_async_copy(wm_hbm, wm_ref, sem.at[2])
    wj_copies = [
        pltpu.make_async_copy(
            wj_hbm.at[:, pl.ds(third * D, D)], wj_ref.at[third], sem.at[3 + third]
        )
        for third in range(3)
    ]
    tok_copy.start()

    @pl.when(step == 0)
    def _():
        for copy in wj_copies:
            copy.start()

    cot_copy.start()

    @pl.when(step == 0)
    def _():
        wm_copy.start()

    tok_copy.wait()
    xhat, _ = stats(tok_ref[...].astype(F32))
    normed = (xhat * g1_ref[...] + s1_ref[...]).astype(BF)
    normed_ref[...] = normed
    for third in range(3):
        cols = slice(third * D, (third + 1) * D)

        @pl.when(step == 0)
        def _():
            wj_copies[third].wait()

        bias = {0: jb_ref[0:1, :], 2: jb_ref[1:2, :]}.get(third, 0.0)

        def project(part, carry):
            here = pl.ds(pl.multiple_of(part * (rows // 2), 16), rows // 2)
            joined_ref[here, cols] = (dot(normed_ref[here, :], wj_ref[third]) + bias).astype(BF)
            return carry

        lax.fori_loop(0, 2, project, 0)
    cot_copy.wait()
    low = head_masks(slots)
    key_slot = lax.broadcasted_iota(jnp.int32, (slots, 2 * slots), 0)
    row_slot = lax.broadcasted_iota(jnp.int32, (slots, D), 0)

    def one(item, carry):
        count = counts_ref[step * items + item]
        here = pl.ds(pl.multiple_of(item * slots, 16), slots)
        seen = row_slot < count
        cot = cot_ref[here, :]
        gout_ref[here, :] = jnp.where(seen, cot, jnp.zeros_like(cot))
        allowed = key_slot < count
        for pair in range(PAIRS):
            cols = slice(pair * LANES, (pair + 1) * LANES)
            q = stack_heads(joined_ref[here, cols] * BF(FACTOR), low)
            k = joined_ref[here, D + pair * LANES : D + (pair + 1) * LANES]
            v = joined_ref[here, 2 * D + pair * LANES : 2 * D + (pair + 1) * LANES]
            scores = jnp.where(allowed, dot_t(k, q), NEG)
            raised = jnp.exp(scores - jnp.max(scores, axis=0, keepdims=True))
            soft = (raised * (1.0 / jnp.sum(raised, axis=0, keepdims=True))).astype(BF)
            probs_ref[item, pair] = soft
            mixed = t_dot(soft, v)
            mix_ref[here, cols] = jnp.where(low, mixed[:slots], mixed[slots:]).astype(BF)
        return carry

    lax.fori_loop(0, items, one, 0)

    @pl.when(step == 0)
    def _():
        wm_copy.wait()

    def finish(part, carry):
        here = pl.ds(pl.multiple_of(part * (rows // 2), 16), rows // 2)
        middle = tok_ref[here, :].astype(F32) + dot(mix_ref[here, :], wm_ref[...]) + mb_ref[...]
        middle_ref[here, :] = middle
        xhat, _ = stats(middle)
        second_ref[here, :] = (xhat * g2_ref[...] + s2_ref[...]).astype(BF)
        return carry

    lax.fori_loop(0, 2, finish, 0)


def first_call(slots, counts, tok, cot, wj, wm, g1, s1, jb, mb, g2, s2):
    total = tok.shape[0]
    hbm = pl.BlockSpec(memory_space=pltpu.HBM)
    out = lambda width, dt: held(total, (total, width), dt)
    return pl.pallas_call(
        lambda *refs: first_body(slots, *refs),
        grid_spec=pltpu.PrefetchScalarGridSpec(
            num_scalar_prefetch=1,
            grid=(1,),
            in_specs=[hbm] * 4 + [full(a.shape) for a in (g1, s1, jb, mb, g2, s2)],
            out_specs=[HERE] * 7,
            scratch_shapes=[
                pltpu.VMEM((total, D), BF),
                pltpu.VMEM((total, D), BF),
                pltpu.VMEM((3, D, D), BF),
                pltpu.VMEM((D, D), BF),
                pltpu.SemaphoreType.DMA((6,)),
            ],
        ),
        out_shape=[
            out(D, BF),
            out(3 * D, BF),
            held(total, (total // slots, PAIRS, slots, 2 * slots), BF),
            out(D, BF),
            out(D, F32),
            out(D, BF),
            out(D, BF),
        ],
        compiler_params=vmem(20 if total <= 640 else 56),
        cost_estimate=cost(15),
        name="attn_fwd",
    )(*[pin(a) for a in (counts, tok, cot, wj, wm, g1, s1, jb, mb, g2, s2)])


def put_blocks(ref, which, mask, value):
    for k in range(BLOCKS):
        ref[which, k ^ mask] = value[k * BROWS : (k + 1) * BROWS, :].astype(BF)


def quarter_body(parts, ids_ref, sec_ref, gout_ref, up_ref, ub_ref, down_ref, *outs):
    grad_ref, act_ref, gh_ref = outs
    rows = sec_ref.shape[0] // parts

    def one(part, carry):
        here = pl.ds(pl.multiple_of(part * rows, 16), rows)
        hidden = dot(sec_ref[here, :], up_ref[...]) + ub_ref[...]
        grad_act = dot_t(gout_ref[here, :], down_ref[...])
        cdf = 0.5 + 0.5 * lax.erf(hidden * (0.5**0.5))
        act_ref[here, :] = (hidden * cdf).astype(BF)
        slope = cdf + hidden * (jnp.exp(-0.5 * hidden * hidden) * ((2 * math.pi) ** -0.5))
        gh_ref[here, :] = (grad_act * slope).astype(BF)
        return carry

    lax.fori_loop(0, parts, one, 0)
    put_blocks(grad_ref, 0, ids_ref[0], t_dot(act_ref[...], gout_ref[...]))
    put_blocks(grad_ref, 1, ids_ref[1], t_dot(sec_ref[...], gh_ref[...]))


def quarter_call(call, ids, second, gout, up, ub, down):
    total = second.shape[0]
    return pl.pallas_call(
        lambda *refs: quarter_body(2, *refs),
        grid_spec=pltpu.PrefetchScalarGridSpec(
            num_scalar_prefetch=1,
            grid=(1,),
            in_specs=[
                HERE,
                HERE,
                pl.BlockSpec((D, D), lambda i, ids: (0, ids[4 + call])),
                pl.BlockSpec((1, D), lambda i, ids: (0, ids[4 + call])),
                pl.BlockSpec((D, D), lambda i, ids: (ids[4 + call], 0)),
            ],
            out_specs=[HERE] * 3,
        ),
        out_shape=[
            held(total, (2, BLOCKS, BROWS, D), BF),
            held(total, (total, D), BF),
            held(total, (total, D), BF),
        ],
        compiler_params=params(total),
        cost_estimate=cost(4.3),
        name=f"mlp_{call}",
    )(ids, second, gout, up, ub, down)


def collect_body(chunk, ids_ref, *refs):
    acts, ghs = refs[:2], refs[2:4]
    down_ref, up_ref = refs[4:6]
    kept = refs[6:-3]
    outer_ref, g_ref, small_ref = refs[-3:]
    step = pl.program_id(0)
    for at in range(2):

        @pl.when(step == at)
        def _():
            if chunk and not at:
                small_ref[...] = kept[2][...]
            rows = outer_ref.shape[0] // 2

            def part(k, carry):
                here = pl.ds(pl.multiple_of(k * rows, 16), rows)
                outer = dot(acts[at][here, :], down_ref[...])
                g = dot_t(ghs[at][here, :], up_ref[...])
                if at:
                    outer = outer + outer_ref[here, :]
                    g = g + g_ref[here, :]
                elif chunk:
                    outer = outer + kept[0][here, :]
                    g = g + kept[1][here, :]
                outer_ref[here, :] = outer
                g_ref[here, :] = g
                return carry

            lax.fori_loop(0, 2, part, 0)
            small_ref[pl.ds(ids_ref[4 + 2 * chunk + at], 1), :] = jnp.sum(
                ghs[at][...].astype(F32), axis=0, keepdims=True
            )


def collect_call(chunk, ids, acts, ghs, down, up, kept):
    total = acts[0].shape[0]
    return pl.pallas_call(
        lambda *refs: collect_body(chunk, *refs),
        grid_spec=pltpu.PrefetchScalarGridSpec(
            num_scalar_prefetch=1,
            grid=(2,),
            in_specs=[HERE] * 4
            + [
                pl.BlockSpec((D, D), lambda i, ids: (ids[4 + 2 * chunk + i], 0)),
                pl.BlockSpec((D, D), lambda i, ids: (0, ids[4 + 2 * chunk + i])),
            ]
            + [HERE] * (3 if chunk else 0),
            out_specs=[HERE] * 3,
        ),
        out_shape=[
            held(total, (total, D), F32),
            held(total, (total, D), F32),
            held(total, (4, D), F32),
        ],
        compiler_params=vmem(16 if total <= 640 else 56),
        cost_estimate=cost(4.3),
        name=f"mlp_collect_{chunk}",
    )(ids, *acts, *ghs, down, up, *(kept or ()))


def middle_body(
    slots,
    counts_ref,
    outer_ref,
    g_ref,
    mid_ref,
    gout_ref,
    db_ref,
    g2_ref,
    wm_ref,
    result_ref,
    gmid_ref,
    branch_ref,
    gmix_ref,
    small_ref,
):
    items = mid_ref.shape[0] // slots
    row_slot = lax.broadcasted_iota(jnp.int32, (slots, D), 0)

    def one(item, sums):
        here = pl.ds(pl.multiple_of(item * slots, 16), slots)
        seen = row_slot < counts_ref[item]
        middle = mid_ref[here, :]
        total = middle + outer_ref[here, :] + db_ref[...]
        result_ref[here, :] = jnp.where(seen, total, 0.0).astype(BF)
        gout = gout_ref[here, :].astype(F32)
        xhat, rstd = stats(middle)
        g = g_ref[here, :]
        e = g * g2_ref[...]
        mean_e = jnp.mean(e, axis=-1, keepdims=True)
        mean_x = jnp.mean(e * xhat, axis=-1, keepdims=True)
        grad = gout + rstd * (e - mean_e - xhat * mean_x)
        gmid_ref[here, :] = grad
        branch = grad.astype(BF)
        branch_ref[here, :] = branch
        row = lambda a: jnp.sum(a, axis=0, keepdims=True)
        return (
            sums[0] + row(gout),
            sums[1] + row(g * xhat),
            sums[2] + row(g),
            sums[3] + row(branch.astype(F32)),
        )

    zero = jnp.zeros((1, D), F32)
    sums = lax.fori_loop(0, items, one, (zero,) * 4)
    for k in range(4):
        small_ref[k : k + 1, :] = sums[k]
    gmix_ref[...] = dot_t(branch_ref[...], wm_ref[...]).astype(BF)


def middle_call(slots, counts, outer, g, mid, gout, db, g2, wm):
    total = mid.shape[0]
    hbm = jax.ShapeDtypeStruct((total, D), BF)
    return pl.pallas_call(
        lambda *refs: middle_body(slots, *refs),
        grid_spec=pltpu.PrefetchScalarGridSpec(
            num_scalar_prefetch=1,
            grid=(1,),
            in_specs=[HERE] * 4 + [full(db.shape), full(g2.shape), full((D, D))],
            out_specs=[full((total, D))] + [HERE] * 4,
        ),
        out_shape=[
            hbm,
            held(total, (total, D), F32),
            held(total, (total, D), BF),
            held(total, (total, D), BF),
            held(total, (4, D), F32),
        ],
        compiler_params=params(total),
        cost_estimate=cost(3.6),
        name="mlp_back",
    )(counts, outer, g, mid, gout, db, g2, wm)


def attn_back_body(slots, first, joined_ref, probs_ref, gmix_ref, grad_ref):
    low = head_masks(slots)
    items = joined_ref.shape[0] // slots // 2
    group = 3

    def one(at, carry):
        item = first * items + at // (PAIRS // group)
        here = pl.ds(pl.multiple_of(item * slots, 16), slots)
        for step in range(group):
            pair = at % (PAIRS // group) * group + step
            start = pair * LANES
            cols = pl.ds(pl.multiple_of(start, LANES), LANES)
            key_cols = pl.ds(pl.multiple_of(D + start, LANES), LANES)
            value_cols = pl.ds(pl.multiple_of(2 * D + start, LANES), LANES)
            q = stack_heads(joined_ref[here, cols] * BF(FACTOR), low)
            out = stack_heads(gmix_ref[here, cols], low)
            low_soft = probs_ref[item, pair]
            soft = low_soft.astype(F32)
            grad_probs = dot_t(joined_ref[here, value_cols], out)
            mean = jnp.sum(soft * grad_probs, axis=0, keepdims=True)
            scores = (soft * (grad_probs - mean)).astype(BF)
            gq = t_dot(scores, joined_ref[here, key_cols] * BF(FACTOR))
            grad_ref[here, cols] = jnp.where(low, gq[:slots], gq[slots:]).astype(BF)
            grad_ref[here, key_cols] = dot(scores, q).astype(BF)
            grad_ref[here, value_cols] = dot(low_soft, out).astype(BF)
        return carry

    lax.fori_loop(0, items * (PAIRS // group), one, 0)


def attn_back_call(call, slots, joined, probs, gmix, kept):
    total = joined.shape[0]
    args = [joined, probs, gmix]
    aliases = {}
    if kept is not None:
        args.append(kept)
        aliases = {3: 0}
    return pl.pallas_call(
        lambda *refs: attn_back_body(slots, call, *refs[:3], refs[-1]),
        grid=(1,),
        in_specs=[HERE] * len(args),
        out_specs=HERE,
        out_shape=held(total, (total, 3 * D), BF),
        input_output_aliases=aliases,
        compiler_params=vmem(8 if total <= 640 else 48),
        cost_estimate=cost(5.5),
        name=f"attn_bwd_{call}",
    )(*args)


def attn_grad_body(ids_ref, normed_ref, mix_ref, grad_ref, branch_ref, qk_ref, vm_ref):
    def put(ref, which, value):
        mask = ids_ref[which] >> 1
        for k in range(BLOCKS // 2):
            ref[which, k ^ mask] = value[k * BROWS : (k + 1) * BROWS, :].astype(BF)

    normed = normed_ref[...]
    put(qk_ref, 0, t_dot(normed, grad_ref[:, :D]))
    put(qk_ref, 1, t_dot(normed, grad_ref[:, D : 2 * D]))
    put(vm_ref, 0, t_dot(normed, grad_ref[:, 2 * D :]))
    put(vm_ref, 1, t_dot(mix_ref[...], branch_ref[...]))


def attn_grad_call(call, ids, normed, mix, grad, branch):
    total = normed.shape[0]
    half = pl.BlockSpec((total, D // 2), lambda i, ids: (0, ids[8 + call]))
    shape = (2, BLOCKS // 2, BROWS, D)
    return pl.pallas_call(
        attn_grad_body,
        grid_spec=pltpu.PrefetchScalarGridSpec(
            num_scalar_prefetch=1,
            grid=(1,),
            in_specs=[half, half, HERE, HERE],
            out_specs=[HERE] * 2,
        ),
        out_shape=[held(total, shape, BF)] * 2,
        compiler_params=params(total),
        cost_estimate=cost(2.6),
        name=f"attn_grad_{call}",
    )(ids, normed, mix, grad, branch)


def last_body(slots, grad_ref, wj_ref, tok_ref, gmid_ref, g1_ref, out_ref, small_ref, g_ref):
    rows = tok_ref.shape[0]
    items = rows // slots
    half = rows // 2

    def back(part, carry):
        here = pl.ds(pl.multiple_of(part * half, 16), half)
        g_ref[here, :] = dot_t(grad_ref[here, :], wj_ref[...])
        return carry

    lax.fori_loop(0, 2, back, 0)

    def one(item, sums):
        here = pl.ds(pl.multiple_of(item * slots, 16), slots)
        xhat, rstd = stats(tok_ref[here, :].astype(F32))
        g = g_ref[here, :]
        e = g * g1_ref[...]
        mean_e = jnp.mean(e, axis=-1, keepdims=True)
        mean_x = jnp.mean(e * xhat, axis=-1, keepdims=True)
        out_ref[here, :] = (gmid_ref[here, :] + rstd * (e - mean_e - xhat * mean_x)).astype(BF)
        row = lambda a: jnp.sum(a, axis=0, keepdims=True)
        return (
            sums[0] + row(grad_ref[here, :D].astype(F32)),
            sums[1] + row(grad_ref[here, 2 * D :].astype(F32)),
            sums[2] + row(g * xhat),
            sums[3] + row(g),
        )

    zero = jnp.zeros((1, D), F32)
    sums = lax.fori_loop(0, items, one, (zero,) * 4)
    for k in range(4):
        small_ref[k : k + 1, :] = sums[k]
    small_ref[4:8, :] = jnp.zeros((4, D), F32)


def last_call(slots, grad, wj, tok, gmid, g1):
    total = tok.shape[0]
    return pl.pallas_call(
        lambda *refs: last_body(slots, *refs),
        grid=(1,),
        in_specs=[HERE, full(wj.shape), full(tok.shape), HERE, full(g1.shape)],
        out_specs=[full((total, D)), full((8, D))],
        out_shape=[
            jax.ShapeDtypeStruct((total, D), BF),
            jax.ShapeDtypeStruct((8, D), F32),
        ],
        scratch_shapes=[pltpu.VMEM((total, D), F32)],
        compiler_params=params(total),
        cost_estimate=cost(0.001),
        name="first_back",
    )(grad, wj, tok, gmid, g1)


def finish_mlp_body(groups, ids_ref, a_ref, b_ref, *rest):
    for ab, in_ref in enumerate((a_ref, b_ref)):
        mask = ids_ref[ab] & (groups - 1)
        for k in range(groups):
            rest[ab - 2][k * BROWS : (k + 1) * BROWS, :] = in_ref[k ^ mask].astype(F32)


def finish_mlp_call(chunk, which, ids, a, b, kept):
    groups = 4
    steps = BLOCKS // groups

    def place(ab):
        def index(i, ids):
            at = (ids[ab] // groups) ^ i
            quarter = 2 * chunk + (ids[3] ^ which)
            return (quarter * steps + at, 0) if ab == 0 else (at, quarter)

        return index

    in_specs = [pl.BlockSpec((groups, BROWS, D), lambda i, ids: (i, 0, 0))] * 2
    args = [ids, a, b]
    aliases = {}
    if kept is not None:
        in_specs += [pl.BlockSpec(memory_space=pl.ANY)] * 2
        args += list(kept)
        aliases = {3: 0, 4: 1}
    return pl.pallas_call(
        lambda *refs: finish_mlp_body(groups, *refs),
        grid_spec=pltpu.PrefetchScalarGridSpec(
            num_scalar_prefetch=1,
            grid=(steps,),
            in_specs=in_specs,
            out_specs=[pl.BlockSpec((groups * BROWS, D), place(ab)) for ab in range(2)],
        ),
        out_shape=[jax.ShapeDtypeStruct(shape, F32) for shape in ((FF, D), (D, FF))],
        input_output_aliases=aliases,
        compiler_params=params(),
        cost_estimate=cost(0.001),
        name=f"finish_mlp_{chunk}_{which}",
    )(*args)


def finish_attn_body(chunk, ids_ref, a_ref, b_ref, *rest):
    for ab, in_ref in enumerate((a_ref, b_ref)):
        mask = ids_ref[ab] >> 1
        for k in range(BLOCKS // 2):
            block = in_ref[k ^ mask].astype(F32)
            rows = slice(k * BROWS, (k + 1) * BROWS)
            if chunk == 2:
                rest[-1][rows, ab * D : (ab + 1) * D] = block
            else:
                rest[ab - 2][rows, :] = block


def finish_attn_call(chunk, which, ids, a, b, joined, merge):
    half = (D // 2, D)
    top = lambda ids: ids[3] ^ which
    out_specs = [pl.BlockSpec((D // 2, 2 * D), lambda i, ids: (top(ids), 0))]
    shapes = [(D, 3 * D)]
    if chunk == 3:
        out_specs = [
            pl.BlockSpec(half, lambda i, ids: (top(ids), 2)),
            pl.BlockSpec(half, lambda i, ids: (top(ids), 0)),
        ]
        shapes.append((D, D))
    kept = [joined, merge][: len(shapes)]
    aliases = {}
    args = [ids, a, b]
    for at, value in enumerate(kept):
        if value is not None:
            aliases[len(args)] = at
            args.append(value)
    return pl.pallas_call(
        lambda *refs: finish_attn_body(chunk, *refs),
        grid_spec=pltpu.PrefetchScalarGridSpec(
            num_scalar_prefetch=1,
            grid=(1,),
            in_specs=[full(a.shape), full(b.shape)]
            + [pl.BlockSpec(memory_space=pl.ANY)] * (len(args) - 3),
            out_specs=out_specs,
        ),
        out_shape=[jax.ShapeDtypeStruct(s, F32) for s in shapes],
        input_output_aliases=aliases,
        compiler_params=params(),
        cost_estimate=cost(0.001),
        name=f"finish_attn_{chunk}_{which}",
    )(*args)


def finish_small_body(mine_ref, got_ref, *outs):
    mine = mine_ref[...].astype(F32)
    got = got_ref[0].astype(F32)
    total = mine[0:12, :] + mine[12:24, :] + (got[0:12, :] + got[12:24, :])
    for k in range(4):
        outs[0][pl.ds(k * D, D)] = total[k]
    for out, k in zip(outs[1:7], (4, 5, 6, 7, 10, 11)):
        out[...] = total[k]
    outs[7][...] = total[8:10, :]


def finish_small_call(mine, got):
    vector = lambda n: jax.ShapeDtypeStruct((n,), F32)
    shapes = [vector(FF)] + [vector(D)] * 6 + [jax.ShapeDtypeStruct((2, D), F32)]
    return pl.pallas_call(
        finish_small_body,
        grid=(1,),
        in_specs=[
            full(mine.shape),
            pl.BlockSpec((1, BROWS, D), lambda i: (got.shape[0] - 1, 0, 0)),
        ],
        out_specs=[full(s.shape) for s in shapes],
        out_shape=shapes,
        compiler_params=params(),
        cost_estimate=cost(0.001),
        name="finish_small",
    )(mine, got)


def stage_lists(sizes):
    bits = {axis: [(axis, b) for b in range(size.bit_length() - 1)] for axis, size in sizes.items()}
    dp, group = bits["dp"], bits["group"]
    if len(dp) == 2 and len(group) == 3:
        order = group + dp
    else:
        order = [dp[0], group[0], group[-1]] + dp[1:] + group[1:-1]
    return order[0], order[1:3], order[3:]


def add(a, b):
    return (a.astype(F32) + b.astype(F32)).astype(BF)


def bit_of(stage):
    return (lax.axis_index(stage[0]) >> stage[1]) & 1


def tie(*values):
    return lax.optimization_barrier(values)


class Chain:
    def __init__(self):
        self.last = None

    def after(self, value):
        if self.last is None:
            return value
        value, _ = tie(value, self.last)
        return value

    def run(self, step, value):
        out = step(self.after(value))
        self.last = jax.tree.leaves(out)[0]
        return out


class Chunk:
    def __init__(self, sums, chain):
        self.sums = sums
        self.chain = chain
        self.small = None

    def first(self, send):
        self.got = self.sums.swap(send, self.sums.first)

    def pair(self, at, keep=None):
        if keep is not None:
            self.keep = keep
        got = self.chain.after(self.got)
        both = [self.sums.halve(self.keep[ab], got[ab]) for ab in range(2)]
        self.keep = [b[0] for b in both]
        out = [b[1] for b in both]
        self.chain.last = out
        self.got = [self.sums.swap(out[ab], self.sums.stage(ab, at)) for ab in range(2)]

    def tail(self, at, small=None):
        rest = self.sums.rest
        got = self.chain.after(self.got)
        if at == 0:
            mine = jnp.stack([add(self.keep[ab], got[ab]) for ab in range(2)])
            n = mine.shape[1] // 2
            self.keep, out = mine[:, :n], mine[:, n:]
            self.chain.last = out
            self.got = self.sums.swap(out, rest[0])
        elif at == 1:
            mine = add(self.keep, got)
            for stage in rest[1:-1]:
                mine, out = self.sums.split_rows(stage, mine)
                mine = add(mine, self.sums.swap(out, stage))
            self.mine = self.chain.last = mine
            self.small = small
            self.up(mine, rest[-1])
        elif at == 2:
            self.mine = add(self.mine, got)
            self.small_sum()
            for stage in rest[-2:0:-1]:
                self.up(self.mine, stage)
                self.small_sum()
                self.mine = self.sums.join_rows(stage, self.mine, self.got)
            self.chain.last = self.mine
            self.up(self.mine, rest[0])
        else:
            self.mine = jnp.concatenate([self.mine, got], axis=1)
            self.chain.last = self.mine
            self.small_sum()
            self.own = [self.mine[0], self.mine[1]]
            self.ups([self.sums.stage(ab, 1) for ab in range(2)])

    def up(self, value, stage):
        if self.small is None:
            self.got = self.sums.swap(value, stage)
            return
        self.rows = split_small(self.small)
        pad = jnp.zeros((BROWS - self.rows.shape[0], D), BF)
        block = jnp.concatenate([self.rows, pad], axis=0)[None]
        load = value.reshape((-1,) + value.shape[-2:])
        if value.shape[-2] != BROWS:
            load = load.reshape(-1, D)
            load = jnp.concatenate([load, jnp.zeros((-load.shape[0] % BROWS, D), BF)])
            load = load.reshape(-1, BROWS, D)
        self.all = self.sums.swap(jnp.concatenate([load, block], axis=0), stage)
        self.got = self.all[:-1].reshape(-1, D)[: value.size // D].reshape(value.shape)

    def small_sum(self):
        if self.small is not None:
            other = self.all[-1, : self.rows.shape[0]]
            self.small = join_small(self.rows) + join_small(other)

    def ups(self, stages):
        self.up(self.own[0], stages[0])
        self.got = [self.got, self.sums.swap(self.own[1], stages[1])]

    def pair_up(self, at):
        got = self.chain.after(self.got)
        self.own = [jnp.concatenate([self.own[ab], got[ab]]) for ab in range(2)]
        self.chain.last = self.own
        self.small_sum()
        if at:
            self.ups([self.sums.stage(ab, at - 1) for ab in range(2)])
        else:
            self.ups([self.sums.first] * 2)


class Sums:
    def __init__(self, sizes):
        self.sizes = sizes
        self.first, self.pair, self.rest = stage_lists(sizes)

    def swap(self, value, stage):
        axis, bit = stage
        return lax.ppermute(value, axis, [(i, i ^ (1 << bit)) for i in range(self.sizes[axis])])

    def stage(self, ab, at):
        return self.pair[at if ab == 0 else 1 - at]

    def halve(self, mine, got, axis=0):
        n = mine.shape[axis] // 2
        low = lax.slice_in_dim(mine, 0, n, axis=axis), lax.slice_in_dim(got, 0, n, axis=axis)
        high = lax.slice_in_dim(mine, n, 2 * n, axis=axis), lax.slice_in_dim(
            got, n, 2 * n, axis=axis
        )
        return add(*low), add(*high)

    def split_rows(self, stage, mine):
        n = mine.shape[2] // 2
        high = bit_of(stage) == 1
        low_rows, high_rows = mine[:, :, :n], mine[:, :, n:]
        return jnp.where(high, high_rows, low_rows), jnp.where(high, low_rows, high_rows)

    def join_rows(self, stage, mine, got):
        high = bit_of(stage) == 1
        return jnp.concatenate([jnp.where(high, got, mine), jnp.where(high, mine, got)], axis=2)


def split_small(value):
    high = lax.reduce_precision(value, 8, 7)
    return jnp.concatenate([high.astype(BF), (value - high).astype(BF)], axis=0)


def join_small(value):
    n = value.shape[0] // 2
    return value[:n].astype(F32) + value[n:].astype(F32)


def solution(mesh):
    sizes = dict(mesh.shape)
    sums = Sums(sizes)

    def shards(
        tokens,
        cotangent,
        counts,
        first_gain,
        first_shift,
        joined_weight,
        joined_bias,
        merge_weight,
        merge_bias,
        second_gain,
        second_shift,
        up_weight,
        up_bias,
        down_weight,
        down_bias,
    ):
        items, slots, features = tokens.shape
        total = items * slots
        row = lambda a: a.reshape(1, -1)
        tok = tokens.reshape(total, features)
        cot = cotangent.reshape(total, features)
        counts = counts.astype(jnp.int32)
        masks = []
        for two in (sums.pair, sums.pair[::-1]):
            mask = 0
            for stage in list(two) + list(sums.rest[:1]):
                mask = 2 * mask + bit_of(stage)
            masks.append(2 * mask)
        core = bit_of(sums.first)
        other = 1 - core
        ids = jnp.stack(
            [masks[0], masks[1], core, core, other, core, 2 + other, 2 + core, other, core]
        ).astype(jnp.int32)

        normed, joined, probs, mix, middle, second, gout = first_call(
            slots,
            counts,
            tok,
            cot,
            joined_weight,
            merge_weight,
            first_gain,
            first_shift,
            joined_bias,
            merge_bias,
            second_gain,
            second_shift,
        )
        chain = Chain()

        acts, ghs = {}, {}

        def quarter(call):
            def step(ids):
                return quarter_call(
                    call, ids, second, gout, up_weight, row(up_bias), down_weight
                )

            grad, act, gh = chain.run(step, ids)
            acts[call], ghs[call] = act, gh
            return grad

        def collect(chunk, kept):
            pick = (2 * chunk, 2 * chunk + 1)
            return chain.run(
                lambda ids: collect_call(
                    chunk,
                    ids,
                    [acts[call] for call in pick],
                    [ghs[call] for call in pick],
                    down_weight,
                    up_weight,
                    kept,
                ),
                ids,
            )

        done = {}

        def finish(chunk, which):
            part = chunks[chunk].got if which else chunks[chunk].own
            if chunk < 2:
                done["mlp"] = chain.run(
                    lambda a: finish_mlp_call(
                        chunk, which, ids, a, part[1], done.get("mlp")
                    ),
                    part[0],
                )
                return
            if chunk == 3 and which:
                part = chunks[3].all, part[1]
            out = chain.run(
                lambda a: finish_attn_call(
                    chunk, which, ids, a, part[1], done.get("joined"), done.get("merge")
                ),
                part[0],
            )
            done["joined"] = out[0]
            if chunk == 3:
                done["merge"] = out[1]

        chunks = [Chunk(sums, chain) for _ in range(4)]
        one, two, three, four = chunks
        one.first(quarter(0))
        keep1 = quarter(1)
        send2 = quarter(2)
        one.pair(0, keep1)
        kept = collect(0, None)
        keep2 = quarter(3)
        two.first(chain.after(send2))
        outer, g, small_a = collect(1, kept)
        one.pair(1)
        two.pair(0, keep2)
        result, gmid, branch, gmix, small_b = chain.run(
            lambda outer: middle_call(
                slots, counts, outer, g, middle, gout, down_bias, second_gain, merge_weight
            ),
            outer,
        )
        grad_joined = chain.run(
            lambda gmix: attn_back_call(0, slots, joined, probs, gmix, None), gmix
        )
        one.tail(0)
        grad_joined = chain.run(
            lambda gmix: attn_back_call(1, slots, joined, probs, gmix, grad_joined), gmix
        )
        send3, send4 = chain.run(
            lambda ids: attn_grad_call(0, ids, normed, mix, grad_joined, branch), ids
        )
        four.first(chain.after(send4))
        two.pair(1)
        three.first(chain.after(send3))
        one.tail(1)
        keep3, keep4 = chain.run(
            lambda ids: attn_grad_call(1, ids, normed, mix, grad_joined, branch), ids
        )
        three.pair(0, keep3)
        two.tail(0)
        four.pair(0, keep4)
        one.tail(2)
        two.tail(1)
        three.pair(1)
        four.pair(1)
        one.tail(3)
        three.tail(0)
        four.tail(0)
        two.tail(2)
        three.tail(1)
        three.tail(2)
        token_grad, small_c = chain.run(
            lambda grad: last_call(slots, grad, joined_weight, tok, gmid, first_gain),
            grad_joined,
        )
        small = jnp.concatenate([small_a, small_b, small_c[:4]], axis=0)
        two.tail(3)
        one.pair_up(1)
        three.tail(3)
        one.pair_up(0)
        four.tail(1, small)
        finish(0, 0)
        three.pair_up(1)
        two.pair_up(1)
        four.tail(2)
        four.tail(3)
        three.pair_up(0)
        finish(0, 1)
        finish(2, 0)
        four.pair_up(1)
        two.pair_up(0)
        finish(1, 0)
        finish(2, 1)
        four.pair_up(0)
        finish(3, 0)
        small = finish_small_call(four.rows, four.all)
        finish(3, 1)
        finish(1, 1)
        joined_grad, merge_grad = done["joined"], done["merge"]
        down_grad, up_grad = done["mlp"]
        return (
            result.reshape(tokens.shape),
            token_grad.reshape(tokens.shape),
            small[5],
            small[6],
            joined_grad,
            small[7],
            merge_grad,
            small[4],
            small[2],
            small[3],
            up_grad,
            small[0],
            down_grad,
            small[1],
        )

    spread = P(("dp", "group"), None, None)
    return jax.shard_map(
        shards,
        mesh=mesh,
        in_specs=(spread, spread, P(("dp", "group"))) + (P(),) * 12,
        out_specs=(spread, spread) + (P(),) * 12,
        check_vma=False,
    )
```

```python
import math

import jax
import jax.numpy as jnp
from jax import lax
from jax.experimental import pallas as pl
from jax.experimental.pallas import tpu as pltpu
from jax.sharding import PartitionSpec as P

D = 768
HEADS = 12
HEAD_DIM = 64
FF = 3072
PAIRS = HEADS // 2
LANES = 2 * HEAD_DIM
EPS = 1e-06
NEG = -1e30
BF = jnp.bfloat16
F32 = jnp.float32
FACTOR = HEAD_DIM ** (-0.5)
BLOCKS = 16
BROWS = D // BLOCKS
SCALE = 10


def dot(a, b):
    return jnp.dot(a, b, preferred_element_type=F32)


def dot_t(a, b):
    return lax.dot_general(a, b, (((1,), (1,)), ((), ())), preferred_element_type=F32)


def t_dot(a, b):
    return lax.dot_general(a, b, (((0,), (0,)), ((), ())), preferred_element_type=F32)


def stats(x):
    centred = x - jnp.mean(x, axis=-1, keepdims=True)
    rstd = lax.rsqrt(jnp.mean(centred * centred, axis=-1, keepdims=True) + EPS)
    return centred * rstd, rstd


def pin(value):
    return pltpu.with_memory_space_constraint(value, pltpu.HBM)


HERE = pl.BlockSpec(memory_space=pltpu.VMEM)


def held(rows, shape, dtype):
    if rows <= 640:
        return pltpu.VMEM(shape, dtype)
    return jax.ShapeDtypeStruct(shape, dtype)


def vmem(limit):
    return pltpu.CompilerParams(vmem_limit_bytes=limit * 1024 * 1024)


def params(rows=640):
    return vmem(20 if rows <= 640 else 48)


def cost(us):
    return pl.CostEstimate(flops=int(us * SCALE * 1e9), bytes_accessed=1000, transcendentals=0)


def full(shape):
    return pl.BlockSpec(shape, lambda *_: (0,) * len(shape))


def head_masks(rows):
    lane = lax.broadcasted_iota(jnp.int32, (rows, LANES), 1)
    return lane < HEAD_DIM


def stack_heads(pair, low):
    zero = jnp.zeros_like(pair)
    return jnp.concatenate([jnp.where(low, pair, zero), jnp.where(low, zero, pair)], axis=0)


def first_body(
    slots,
    counts_ref,
    tok_hbm,
    cot_hbm,
    wj_hbm,
    wm_hbm,
    g1_ref,
    s1_ref,
    jb_ref,
    mb_ref,
    g2_ref,
    s2_ref,
    normed_ref,
    joined_ref,
    probs_ref,
    mix_ref,
    middle_ref,
    second_ref,
    gout_ref,
    tok_ref,
    cot_ref,
    wj_ref,
    wm_ref,
    sem,
):
    step = pl.program_id(0)
    rows = tok_ref.shape[0]
    items = rows // slots
    span = pl.ds(pl.multiple_of(step * rows, 16), rows)
    tok_copy = pltpu.make_async_copy(tok_hbm.at[span], tok_ref, sem.at[0])
    cot_copy = pltpu.make_async_copy(cot_hbm.at[span], cot_ref, sem.at[1])
    wm_copy = pltpu.make_async_copy(wm_hbm, wm_ref, sem.at[2])
    wj_copies = [
        pltpu.make_async_copy(
            wj_hbm.at[:, pl.ds(third * D, D)], wj_ref.at[third], sem.at[3 + third]
        )
        for third in range(3)
    ]
    tok_copy.start()

    @pl.when(step == 0)
    def _():
        for copy in wj_copies:
            copy.start()

    cot_copy.start()

    @pl.when(step == 0)
    def _():
        wm_copy.start()

    tok_copy.wait()
    xhat, _ = stats(tok_ref[...].astype(F32))
    normed = (xhat * g1_ref[...] + s1_ref[...]).astype(BF)
    normed_ref[...] = normed
    for third in range(3):
        cols = slice(third * D, (third + 1) * D)

        @pl.when(step == 0)
        def _():
            wj_copies[third].wait()

        bias = {0: jb_ref[0:1, :], 2: jb_ref[1:2, :]}.get(third, 0.0)

        def project(part, carry):
            here = pl.ds(pl.multiple_of(part * (rows // 2), 16), rows // 2)
            joined_ref[here, cols] = (dot(normed_ref[here, :], wj_ref[third]) + bias).astype(BF)
            return carry

        lax.fori_loop(0, 2, project, 0)
    cot_copy.wait()
    low = head_masks(slots)
    key_slot = lax.broadcasted_iota(jnp.int32, (slots, 2 * slots), 0)
    row_slot = lax.broadcasted_iota(jnp.int32, (slots, D), 0)

    def one(item, carry):
        count = counts_ref[step * items + item]
        here = pl.ds(pl.multiple_of(item * slots, 16), slots)
        seen = row_slot < count
        cot = cot_ref[here, :]
        gout_ref[here, :] = jnp.where(seen, cot, jnp.zeros_like(cot))
        allowed = key_slot < count
        for pair in range(PAIRS):
            cols = slice(pair * LANES, (pair + 1) * LANES)
            q = stack_heads(joined_ref[here, cols] * BF(FACTOR), low)
            k = joined_ref[here, D + pair * LANES : D + (pair + 1) * LANES]
            v = joined_ref[here, 2 * D + pair * LANES : 2 * D + (pair + 1) * LANES]
            scores = jnp.where(allowed, dot_t(k, q), NEG)
            raised = jnp.exp(scores - jnp.max(scores, axis=0, keepdims=True))
            soft = (raised * (1.0 / jnp.sum(raised, axis=0, keepdims=True))).astype(BF)
            probs_ref[item, pair] = soft
            mixed = t_dot(soft, v)
            mix_ref[here, cols] = jnp.where(low, mixed[:slots], mixed[slots:]).astype(BF)
        return carry

    lax.fori_loop(0, items, one, 0)

    @pl.when(step == 0)
    def _():
        wm_copy.wait()

    def finish(part, carry):
        here = pl.ds(pl.multiple_of(part * (rows // 2), 16), rows // 2)
        middle = tok_ref[here, :].astype(F32) + dot(mix_ref[here, :], wm_ref[...]) + mb_ref[...]
        middle_ref[here, :] = middle
        xhat, _ = stats(middle)
        second_ref[here, :] = (xhat * g2_ref[...] + s2_ref[...]).astype(BF)
        return carry

    lax.fori_loop(0, 2, finish, 0)


def first_call(slots, counts, tok, cot, wj, wm, g1, s1, jb, mb, g2, s2):
    total = tok.shape[0]
    hbm = pl.BlockSpec(memory_space=pltpu.HBM)
    out = lambda width, dt: held(total, (total, width), dt)
    return pl.pallas_call(
        lambda *refs: first_body(slots, *refs),
        grid_spec=pltpu.PrefetchScalarGridSpec(
            num_scalar_prefetch=1,
            grid=(1,),
            in_specs=[hbm] * 4 + [full(a.shape) for a in (g1, s1, jb, mb, g2, s2)],
            out_specs=[HERE] * 7,
            scratch_shapes=[
                pltpu.VMEM((total, D), BF),
                pltpu.VMEM((total, D), BF),
                pltpu.VMEM((3, D, D), BF),
                pltpu.VMEM((D, D), BF),
                pltpu.SemaphoreType.DMA((6,)),
            ],
        ),
        out_shape=[
            out(D, BF),
            out(3 * D, BF),
            held(total, (total // slots, PAIRS, slots, 2 * slots), BF),
            out(D, BF),
            out(D, F32),
            out(D, BF),
            out(D, BF),
        ],
        compiler_params=vmem(20 if total <= 640 else 56),
        cost_estimate=cost(15),
        name="attn_fwd",
    )(*[pin(a) for a in (counts, tok, cot, wj, wm, g1, s1, jb, mb, g2, s2)])


def put_blocks(ref, which, mask, value):
    for k in range(BLOCKS):
        ref[which, k ^ mask] = value[k * BROWS : (k + 1) * BROWS, :].astype(BF)


def quarter_body(parts, ids_ref, sec_ref, gout_ref, up_ref, ub_ref, down_ref, *outs):
    grad_ref, act_ref, gh_ref = outs
    rows = sec_ref.shape[0] // parts

    def one(part, carry):
        here = pl.ds(pl.multiple_of(part * rows, 16), rows)
        hidden = dot(sec_ref[here, :], up_ref[...]) + ub_ref[...]
        grad_act = dot_t(gout_ref[here, :], down_ref[...])
        cdf = 0.5 + 0.5 * lax.erf(hidden * (0.5**0.5))
        act_ref[here, :] = (hidden * cdf).astype(BF)
        slope = cdf + hidden * (jnp.exp(-0.5 * hidden * hidden) * ((2 * math.pi) ** -0.5))
        gh_ref[here, :] = (grad_act * slope).astype(BF)
        return carry

    lax.fori_loop(0, parts, one, 0)
    put_blocks(grad_ref, 0, ids_ref[0], t_dot(act_ref[...], gout_ref[...]))
    put_blocks(grad_ref, 1, ids_ref[1], t_dot(sec_ref[...], gh_ref[...]))


def quarter_call(call, ids, second, gout, up, ub, down):
    total = second.shape[0]
    return pl.pallas_call(
        lambda *refs: quarter_body(2, *refs),
        grid_spec=pltpu.PrefetchScalarGridSpec(
            num_scalar_prefetch=1,
            grid=(1,),
            in_specs=[
                HERE,
                HERE,
                pl.BlockSpec((D, D), lambda i, ids: (0, ids[4 + call])),
                pl.BlockSpec((1, D), lambda i, ids: (0, ids[4 + call])),
                pl.BlockSpec((D, D), lambda i, ids: (ids[4 + call], 0)),
            ],
            out_specs=[HERE] * 3,
        ),
        out_shape=[
            held(total, (2, BLOCKS, BROWS, D), BF),
            held(total, (total, D), BF),
            held(total, (total, D), BF),
        ],
        compiler_params=params(total),
        cost_estimate=cost(4.3),
        name=f"mlp_{call}",
    )(ids, second, gout, up, ub, down)


def collect_body(chunk, ids_ref, *refs):
    acts, ghs = refs[:2], refs[2:4]
    down_ref, up_ref = refs[4:6]
    kept = refs[6:-3]
    outer_ref, g_ref, small_ref = refs[-3:]
    step = pl.program_id(0)
    for at in range(2):

        @pl.when(step == at)
        def _():
            if chunk and not at:
                small_ref[...] = kept[2][...]
            rows = outer_ref.shape[0] // 2

            def part(k, carry):
                here = pl.ds(pl.multiple_of(k * rows, 16), rows)
                outer = dot(acts[at][here, :], down_ref[...])
                g = dot_t(ghs[at][here, :], up_ref[...])
                if at:
                    outer = outer + outer_ref[here, :]
                    g = g + g_ref[here, :]
                elif chunk:
                    outer = outer + kept[0][here, :]
                    g = g + kept[1][here, :]
                outer_ref[here, :] = outer
                g_ref[here, :] = g
                return carry

            lax.fori_loop(0, 2, part, 0)
            small_ref[pl.ds(ids_ref[4 + 2 * chunk + at], 1), :] = jnp.sum(
                ghs[at][...].astype(F32), axis=0, keepdims=True
            )


def collect_call(chunk, ids, acts, ghs, down, up, kept):
    total = acts[0].shape[0]
    return pl.pallas_call(
        lambda *refs: collect_body(chunk, *refs),
        grid_spec=pltpu.PrefetchScalarGridSpec(
            num_scalar_prefetch=1,
            grid=(2,),
            in_specs=[HERE] * 4
            + [
                pl.BlockSpec((D, D), lambda i, ids: (ids[4 + 2 * chunk + i], 0)),
                pl.BlockSpec((D, D), lambda i, ids: (0, ids[4 + 2 * chunk + i])),
            ]
            + [HERE] * (3 if chunk else 0),
            out_specs=[HERE] * 3,
        ),
        out_shape=[
            held(total, (total, D), F32),
            held(total, (total, D), F32),
            held(total, (4, D), F32),
        ],
        compiler_params=vmem(16 if total <= 640 else 56),
        cost_estimate=cost(4.3),
        name=f"mlp_collect_{chunk}",
    )(ids, *acts, *ghs, down, up, *(kept or ()))


def middle_body(
    slots,
    counts_ref,
    outer_ref,
    g_ref,
    mid_ref,
    gout_ref,
    db_ref,
    g2_ref,
    wm_ref,
    result_ref,
    gmid_ref,
    branch_ref,
    gmix_ref,
    small_ref,
):
    items = mid_ref.shape[0] // slots
    row_slot = lax.broadcasted_iota(jnp.int32, (slots, D), 0)

    def one(item, sums):
        here = pl.ds(pl.multiple_of(item * slots, 16), slots)
        seen = row_slot < counts_ref[item]
        middle = mid_ref[here, :]
        total = middle + outer_ref[here, :] + db_ref[...]
        result_ref[here, :] = jnp.where(seen, total, 0.0).astype(BF)
        gout = gout_ref[here, :].astype(F32)
        xhat, rstd = stats(middle)
        g = g_ref[here, :]
        e = g * g2_ref[...]
        mean_e = jnp.mean(e, axis=-1, keepdims=True)
        mean_x = jnp.mean(e * xhat, axis=-1, keepdims=True)
        grad = gout + rstd * (e - mean_e - xhat * mean_x)
        gmid_ref[here, :] = grad
        branch = grad.astype(BF)
        branch_ref[here, :] = branch
        row = lambda a: jnp.sum(a, axis=0, keepdims=True)
        return (
            sums[0] + row(gout),
            sums[1] + row(g * xhat),
            sums[2] + row(g),
            sums[3] + row(branch.astype(F32)),
        )

    zero = jnp.zeros((1, D), F32)
    sums = lax.fori_loop(0, items, one, (zero,) * 4)
    for k in range(4):
        small_ref[k : k + 1, :] = sums[k]
    gmix_ref[...] = dot_t(branch_ref[...], wm_ref[...]).astype(BF)


def middle_call(slots, counts, outer, g, mid, gout, db, g2, wm):
    total = mid.shape[0]
    hbm = jax.ShapeDtypeStruct((total, D), BF)
    return pl.pallas_call(
        lambda *refs: middle_body(slots, *refs),
        grid_spec=pltpu.PrefetchScalarGridSpec(
            num_scalar_prefetch=1,
            grid=(1,),
            in_specs=[HERE] * 4 + [full(db.shape), full(g2.shape), full((D, D))],
            out_specs=[full((total, D))] + [HERE] * 4,
        ),
        out_shape=[
            hbm,
            held(total, (total, D), F32),
            held(total, (total, D), BF),
            held(total, (total, D), BF),
            held(total, (4, D), F32),
        ],
        compiler_params=params(total),
        cost_estimate=cost(3.6),
        name="mlp_back",
    )(counts, outer, g, mid, gout, db, g2, wm)


def attn_back_body(slots, first, joined_ref, probs_ref, gmix_ref, grad_ref):
    low = head_masks(slots)
    items = joined_ref.shape[0] // slots // 2
    group = 3

    def one(at, carry):
        item = first * items + at // (PAIRS // group)
        here = pl.ds(pl.multiple_of(item * slots, 16), slots)
        for step in range(group):
            pair = at % (PAIRS // group) * group + step
            start = pair * LANES
            cols = pl.ds(pl.multiple_of(start, LANES), LANES)
            key_cols = pl.ds(pl.multiple_of(D + start, LANES), LANES)
            value_cols = pl.ds(pl.multiple_of(2 * D + start, LANES), LANES)
            q = stack_heads(joined_ref[here, cols] * BF(FACTOR), low)
            out = stack_heads(gmix_ref[here, cols], low)
            low_soft = probs_ref[item, pair]
            soft = low_soft.astype(F32)
            grad_probs = dot_t(joined_ref[here, value_cols], out)
            mean = jnp.sum(soft * grad_probs, axis=0, keepdims=True)
            scores = (soft * (grad_probs - mean)).astype(BF)
            gq = t_dot(scores, joined_ref[here, key_cols] * BF(FACTOR))
            grad_ref[here, cols] = jnp.where(low, gq[:slots], gq[slots:]).astype(BF)
            grad_ref[here, key_cols] = dot(scores, q).astype(BF)
            grad_ref[here, value_cols] = dot(low_soft, out).astype(BF)
        return carry

    lax.fori_loop(0, items * (PAIRS // group), one, 0)


def attn_back_call(call, slots, joined, probs, gmix, kept):
    total = joined.shape[0]
    args = [joined, probs, gmix]
    aliases = {}
    if kept is not None:
        args.append(kept)
        aliases = {3: 0}
    return pl.pallas_call(
        lambda *refs: attn_back_body(slots, call, *refs[:3], refs[-1]),
        grid=(1,),
        in_specs=[HERE] * len(args),
        out_specs=HERE,
        out_shape=held(total, (total, 3 * D), BF),
        input_output_aliases=aliases,
        compiler_params=vmem(8 if total <= 640 else 48),
        cost_estimate=cost(5.5),
        name=f"attn_bwd_{call}",
    )(*args)


def attn_grad_body(ids_ref, normed_ref, mix_ref, grad_ref, branch_ref, qk_ref, vm_ref):
    def put(ref, which, value):
        mask = ids_ref[which] >> 1
        for k in range(BLOCKS // 2):
            ref[which, k ^ mask] = value[k * BROWS : (k + 1) * BROWS, :].astype(BF)

    normed = normed_ref[...]
    put(qk_ref, 0, t_dot(normed, grad_ref[:, :D]))
    put(qk_ref, 1, t_dot(normed, grad_ref[:, D : 2 * D]))
    put(vm_ref, 0, t_dot(normed, grad_ref[:, 2 * D :]))
    put(vm_ref, 1, t_dot(mix_ref[...], branch_ref[...]))


def attn_grad_call(call, ids, normed, mix, grad, branch):
    total = normed.shape[0]
    half = pl.BlockSpec((total, D // 2), lambda i, ids: (0, ids[8 + call]))
    shape = (2, BLOCKS // 2, BROWS, D)
    return pl.pallas_call(
        attn_grad_body,
        grid_spec=pltpu.PrefetchScalarGridSpec(
            num_scalar_prefetch=1,
            grid=(1,),
            in_specs=[half, half, HERE, HERE],
            out_specs=[HERE] * 2,
        ),
        out_shape=[held(total, shape, BF)] * 2,
        compiler_params=params(total),
        cost_estimate=cost(2.6),
        name=f"attn_grad_{call}",
    )(ids, normed, mix, grad, branch)


def last_body(slots, grad_ref, wj_ref, tok_ref, gmid_ref, g1_ref, out_ref, small_ref, g_ref):
    rows = tok_ref.shape[0]
    items = rows // slots
    half = rows // 2

    def back(part, carry):
        here = pl.ds(pl.multiple_of(part * half, 16), half)
        g_ref[here, :] = dot_t(grad_ref[here, :], wj_ref[...])
        return carry

    lax.fori_loop(0, 2, back, 0)

    def one(item, sums):
        here = pl.ds(pl.multiple_of(item * slots, 16), slots)
        xhat, rstd = stats(tok_ref[here, :].astype(F32))
        g = g_ref[here, :]
        e = g * g1_ref[...]
        mean_e = jnp.mean(e, axis=-1, keepdims=True)
        mean_x = jnp.mean(e * xhat, axis=-1, keepdims=True)
        out_ref[here, :] = (gmid_ref[here, :] + rstd * (e - mean_e - xhat * mean_x)).astype(BF)
        row = lambda a: jnp.sum(a, axis=0, keepdims=True)
        return (
            sums[0] + row(grad_ref[here, :D].astype(F32)),
            sums[1] + row(grad_ref[here, 2 * D :].astype(F32)),
            sums[2] + row(g * xhat),
            sums[3] + row(g),
        )

    zero = jnp.zeros((1, D), F32)
    sums = lax.fori_loop(0, items, one, (zero,) * 4)
    for k in range(4):
        small_ref[k : k + 1, :] = sums[k]
    small_ref[4:8, :] = jnp.zeros((4, D), F32)


def last_call(slots, grad, wj, tok, gmid, g1):
    total = tok.shape[0]
    return pl.pallas_call(
        lambda *refs: last_body(slots, *refs),
        grid=(1,),
        in_specs=[HERE, full(wj.shape), full(tok.shape), HERE, full(g1.shape)],
        out_specs=[full((total, D)), full((8, D))],
        out_shape=[
            jax.ShapeDtypeStruct((total, D), BF),
            jax.ShapeDtypeStruct((8, D), F32),
        ],
        scratch_shapes=[pltpu.VMEM((total, D), F32)],
        compiler_params=params(total),
        cost_estimate=cost(0.001),
        name="first_back",
    )(grad, wj, tok, gmid, g1)


def finish_mlp_body(groups, ids_ref, a_ref, b_ref, *rest):
    for ab, in_ref in enumerate((a_ref, b_ref)):
        mask = ids_ref[ab] & (groups - 1)
        for k in range(groups):
            rest[ab - 2][k * BROWS : (k + 1) * BROWS, :] = in_ref[k ^ mask].astype(F32)


def finish_mlp_call(chunk, which, ids, a, b, kept):
    groups = 4
    steps = BLOCKS // groups

    def place(ab):
        def index(i, ids):
            at = (ids[ab] // groups) ^ i
            quarter = 2 * chunk + (ids[3] ^ which)
            return (quarter * steps + at, 0) if ab == 0 else (at, quarter)

        return index

    in_specs = [pl.BlockSpec((groups, BROWS, D), lambda i, ids: (i, 0, 0))] * 2
    args = [ids, a, b]
    aliases = {}
    if kept is not None:
        in_specs += [pl.BlockSpec(memory_space=pl.ANY)] * 2
        args += list(kept)
        aliases = {3: 0, 4: 1}
    return pl.pallas_call(
        lambda *refs: finish_mlp_body(groups, *refs),
        grid_spec=pltpu.PrefetchScalarGridSpec(
            num_scalar_prefetch=1,
            grid=(steps,),
            in_specs=in_specs,
            out_specs=[pl.BlockSpec((groups * BROWS, D), place(ab)) for ab in range(2)],
        ),
        out_shape=[jax.ShapeDtypeStruct(shape, F32) for shape in ((FF, D), (D, FF))],
        input_output_aliases=aliases,
        compiler_params=params(),
        cost_estimate=cost(0.001),
        name=f"finish_mlp_{chunk}_{which}",
    )(*args)


def finish_attn_body(chunk, ids_ref, a_ref, b_ref, *rest):
    for ab, in_ref in enumerate((a_ref, b_ref)):
        mask = ids_ref[ab] >> 1
        for k in range(BLOCKS // 2):
            block = in_ref[k ^ mask].astype(F32)
            rows = slice(k * BROWS, (k + 1) * BROWS)
            if chunk == 2:
                rest[-1][rows, ab * D : (ab + 1) * D] = block
            else:
                rest[ab - 2][rows, :] = block


def finish_attn_call(chunk, which, ids, a, b, joined, merge):
    half = (D // 2, D)
    top = lambda ids: ids[3] ^ which
    out_specs = [pl.BlockSpec((D // 2, 2 * D), lambda i, ids: (top(ids), 0))]
    shapes = [(D, 3 * D)]
    if chunk == 3:
        out_specs = [
            pl.BlockSpec(half, lambda i, ids: (top(ids), 2)),
            pl.BlockSpec(half, lambda i, ids: (top(ids), 0)),
        ]
        shapes.append((D, D))
    kept = [joined, merge][: len(shapes)]
    aliases = {}
    args = [ids, a, b]
    for at, value in enumerate(kept):
        if value is not None:
            aliases[len(args)] = at
            args.append(value)
    return pl.pallas_call(
        lambda *refs: finish_attn_body(chunk, *refs),
        grid_spec=pltpu.PrefetchScalarGridSpec(
            num_scalar_prefetch=1,
            grid=(1,),
            in_specs=[full(a.shape), full(b.shape)]
            + [pl.BlockSpec(memory_space=pl.ANY)] * (len(args) - 3),
            out_specs=out_specs,
        ),
        out_shape=[jax.ShapeDtypeStruct(s, F32) for s in shapes],
        input_output_aliases=aliases,
        compiler_params=params(),
        cost_estimate=cost(0.001),
        name=f"finish_attn_{chunk}_{which}",
    )(*args)


def finish_small_body(mine_ref, got_ref, *outs):
    mine = mine_ref[...].astype(F32)
    got = got_ref[0].astype(F32)
    total = mine[0:12, :] + mine[12:24, :] + (got[0:12, :] + got[12:24, :])
    for k in range(4):
        outs[0][pl.ds(k * D, D)] = total[k]
    for out, k in zip(outs[1:7], (4, 5, 6, 7, 10, 11)):
        out[...] = total[k]
    outs[7][...] = total[8:10, :]


def finish_small_call(mine, got):
    vector = lambda n: jax.ShapeDtypeStruct((n,), F32)
    shapes = [vector(FF)] + [vector(D)] * 6 + [jax.ShapeDtypeStruct((2, D), F32)]
    return pl.pallas_call(
        finish_small_body,
        grid=(1,),
        in_specs=[
            full(mine.shape),
            pl.BlockSpec((1, BROWS, D), lambda i: (got.shape[0] - 1, 0, 0)),
        ],
        out_specs=[full(s.shape) for s in shapes],
        out_shape=shapes,
        compiler_params=params(),
        cost_estimate=cost(0.001),
        name="finish_small",
    )(mine, got)


def stage_lists(sizes):
    bits = {axis: [(axis, b) for b in range(size.bit_length() - 1)] for axis, size in sizes.items()}
    dp, group = bits["dp"], bits["group"]
    if len(dp) == 2 and len(group) == 3:
        order = group + dp
    else:
        order = [dp[0], group[0], group[-1]] + dp[1:] + group[1:-1]
    return order[0], order[1:3], order[3:]


def add(a, b):
    return (a.astype(F32) + b.astype(F32)).astype(BF)


def bit_of(stage):
    return (lax.axis_index(stage[0]) >> stage[1]) & 1


def tie(*values):
    return lax.optimization_barrier(values)


class Chain:
    def __init__(self):
        self.last = None

    def after(self, value):
        if self.last is None:
            return value
        value, _ = tie(value, self.last)
        return value

    def run(self, step, value):
        out = step(self.after(value))
        self.last = jax.tree.leaves(out)[0]
        return out


class Chunk:
    def __init__(self, sums, chain):
        self.sums = sums
        self.chain = chain
        self.small = None

    def first(self, send):
        self.got = self.sums.swap(send, self.sums.first)

    def pair(self, at, keep=None):
        if keep is not None:
            self.keep = keep
        got = self.chain.after(self.got)
        both = [self.sums.halve(self.keep[ab], got[ab]) for ab in range(2)]
        self.keep = [b[0] for b in both]
        out = [b[1] for b in both]
        self.chain.last = out
        self.got = [self.sums.swap(out[ab], self.sums.stage(ab, at)) for ab in range(2)]

    def tail(self, at, small=None):
        rest = self.sums.rest
        got = self.chain.after(self.got)
        if at == 0:
            mine = jnp.stack([add(self.keep[ab], got[ab]) for ab in range(2)])
            n = mine.shape[1] // 2
            self.keep, out = mine[:, :n], mine[:, n:]
            self.chain.last = out
            self.got = self.sums.swap(out, rest[0])
        elif at == 1:
            mine = add(self.keep, got)
            for stage in rest[1:-1]:
                mine, out = self.sums.split_rows(stage, mine)
                mine = add(mine, self.sums.swap(out, stage))
            self.mine = self.chain.last = mine
            self.small = small
            self.up(mine, rest[-1])
        elif at == 2:
            self.mine = add(self.mine, got)
            self.small_sum()
            for stage in rest[-2:0:-1]:
                self.up(self.mine, stage)
                self.small_sum()
                self.mine = self.sums.join_rows(stage, self.mine, self.got)
            self.chain.last = self.mine
            self.up(self.mine, rest[0])
        else:
            self.mine = jnp.concatenate([self.mine, got], axis=1)
            self.chain.last = self.mine
            self.small_sum()
            self.own = [self.mine[0], self.mine[1]]
            self.ups([self.sums.stage(ab, 1) for ab in range(2)])

    def up(self, value, stage):
        if self.small is None:
            self.got = self.sums.swap(value, stage)
            return
        self.rows = split_small(self.small)
        pad = jnp.zeros((BROWS - self.rows.shape[0], D), BF)
        block = jnp.concatenate([self.rows, pad], axis=0)[None]
        load = value.reshape((-1,) + value.shape[-2:])
        if value.shape[-2] != BROWS:
            load = load.reshape(-1, D)
            load = jnp.concatenate([load, jnp.zeros((-load.shape[0] % BROWS, D), BF)])
            load = load.reshape(-1, BROWS, D)
        self.all = self.sums.swap(jnp.concatenate([load, block], axis=0), stage)
        self.got = self.all[:-1].reshape(-1, D)[: value.size // D].reshape(value.shape)

    def small_sum(self):
        if self.small is not None:
            other = self.all[-1, : self.rows.shape[0]]
            self.small = join_small(self.rows) + join_small(other)

    def ups(self, stages):
        self.up(self.own[0], stages[0])
        self.got = [self.got, self.sums.swap(self.own[1], stages[1])]

    def pair_up(self, at):
        got = self.chain.after(self.got)
        self.own = [jnp.concatenate([self.own[ab], got[ab]]) for ab in range(2)]
        self.chain.last = self.own
        self.small_sum()
        if at:
            self.ups([self.sums.stage(ab, at - 1) for ab in range(2)])
        else:
            self.ups([self.sums.first] * 2)


class Sums:
    def __init__(self, sizes):
        self.sizes = sizes
        self.first, self.pair, self.rest = stage_lists(sizes)

    def swap(self, value, stage):
        axis, bit = stage
        return lax.ppermute(value, axis, [(i, i ^ (1 << bit)) for i in range(self.sizes[axis])])

    def stage(self, ab, at):
        return self.pair[at if ab == 0 else 1 - at]

    def halve(self, mine, got, axis=0):
        n = mine.shape[axis] // 2
        low = lax.slice_in_dim(mine, 0, n, axis=axis), lax.slice_in_dim(got, 0, n, axis=axis)
        high = lax.slice_in_dim(mine, n, 2 * n, axis=axis), lax.slice_in_dim(
            got, n, 2 * n, axis=axis
        )
        return add(*low), add(*high)

    def split_rows(self, stage, mine):
        n = mine.shape[2] // 2
        high = bit_of(stage) == 1
        low_rows, high_rows = mine[:, :, :n], mine[:, :, n:]
        return jnp.where(high, high_rows, low_rows), jnp.where(high, low_rows, high_rows)

    def join_rows(self, stage, mine, got):
        high = bit_of(stage) == 1
        return jnp.concatenate([jnp.where(high, got, mine), jnp.where(high, mine, got)], axis=2)


def split_small(value):
    high = lax.reduce_precision(value, 8, 7)
    return jnp.concatenate([high.astype(BF), (value - high).astype(BF)], axis=0)


def join_small(value):
    n = value.shape[0] // 2
    return value[:n].astype(F32) + value[n:].astype(F32)


def solution(mesh):
    sizes = dict(mesh.shape)
    sums = Sums(sizes)

    def shards(
        tokens,
        cotangent,
        counts,
        first_gain,
        first_shift,
        joined_weight,
        joined_bias,
        merge_weight,
        merge_bias,
        second_gain,
        second_shift,
        up_weight,
        up_bias,
        down_weight,
        down_bias,
    ):
        items, slots, features = tokens.shape
        total = items * slots
        row = lambda a: a.reshape(1, -1)
        tok = tokens.reshape(total, features)
        cot = cotangent.reshape(total, features)
        counts = counts.astype(jnp.int32)
        masks = []
        for two in (sums.pair, sums.pair[::-1]):
            mask = 0
            for stage in list(two) + list(sums.rest[:1]):
                mask = 2 * mask + bit_of(stage)
            masks.append(2 * mask)
        core = bit_of(sums.first)
        other = 1 - core
        ids = jnp.stack(
            [masks[0], masks[1], core, core, other, core, 2 + other, 2 + core, other, core]
        ).astype(jnp.int32)

        normed, joined, probs, mix, middle, second, gout = first_call(
            slots,
            counts,
            tok,
            cot,
            joined_weight,
            merge_weight,
            first_gain,
            first_shift,
            joined_bias,
            merge_bias,
            second_gain,
            second_shift,
        )
        chain = Chain()

        acts, ghs = {}, {}

        def quarter(call):
            def step(ids):
                return quarter_call(
                    call, ids, second, gout, up_weight, row(up_bias), down_weight
                )

            grad, act, gh = chain.run(step, ids)
            acts[call], ghs[call] = act, gh
            return grad

        def collect(chunk, kept):
            pick = (2 * chunk, 2 * chunk + 1)
            return chain.run(
                lambda ids: collect_call(
                    chunk,
                    ids,
                    [acts[call] for call in pick],
                    [ghs[call] for call in pick],
                    down_weight,
                    up_weight,
                    kept,
                ),
                ids,
            )

        done = {}

        def finish(chunk, which):
            part = chunks[chunk].got if which else chunks[chunk].own
            if chunk < 2:
                done["mlp"] = chain.run(
                    lambda a: finish_mlp_call(
                        chunk, which, ids, a, part[1], done.get("mlp")
                    ),
                    part[0],
                )
                return
            if chunk == 3 and which:
                part = chunks[3].all, part[1]
            out = chain.run(
                lambda a: finish_attn_call(
                    chunk, which, ids, a, part[1], done.get("joined"), done.get("merge")
                ),
                part[0],
            )
            done["joined"] = out[0]
            if chunk == 3:
                done["merge"] = out[1]

        chunks = [Chunk(sums, chain) for _ in range(4)]
        one, two, three, four = chunks
        one.first(quarter(0))
        keep1 = quarter(1)
        send2 = quarter(2)
        one.pair(0, keep1)
        kept = collect(0, None)
        keep2 = quarter(3)
        two.first(chain.after(send2))
        outer, g, small_a = collect(1, kept)
        one.pair(1)
        two.pair(0, keep2)
        result, gmid, branch, gmix, small_b = chain.run(
            lambda outer: middle_call(
                slots, counts, outer, g, middle, gout, down_bias, second_gain, merge_weight
            ),
            outer,
        )
        grad_joined = chain.run(
            lambda gmix: attn_back_call(0, slots, joined, probs, gmix, None), gmix
        )
        one.tail(0)
        grad_joined = chain.run(
            lambda gmix: attn_back_call(1, slots, joined, probs, gmix, grad_joined), gmix
        )
        send3, send4 = chain.run(
            lambda ids: attn_grad_call(0, ids, normed, mix, grad_joined, branch), ids
        )
        four.first(chain.after(send4))
        two.pair(1)
        three.first(chain.after(send3))
        one.tail(1)
        keep3, keep4 = chain.run(
            lambda ids: attn_grad_call(1, ids, normed, mix, grad_joined, branch), ids
        )
        three.pair(0, keep3)
        two.tail(0)
        four.pair(0, keep4)
        one.tail(2)
        two.tail(1)
        three.pair(1)
        four.pair(1)
        one.tail(3)
        three.tail(0)
        four.tail(0)
        two.tail(2)
        three.tail(1)
        three.tail(2)
        token_grad, small_c = chain.run(
            lambda grad: last_call(slots, grad, joined_weight, tok, gmid, first_gain),
            grad_joined,
        )
        small = jnp.concatenate([small_a, small_b, small_c[:4]], axis=0)
        three.tail(3)
        one.pair_up(1)
        one.pair_up(0)
        four.tail(1, small)
        two.tail(3)
        finish(0, 0)
        three.pair_up(1)
        two.pair_up(1)
        four.tail(2)
        four.tail(3)
        three.pair_up(0)
        finish(0, 1)
        four.pair_up(1)
        two.pair_up(0)
        finish(1, 0)
        finish(2, 0)
        finish(2, 1)
        four.pair_up(0)
        finish(3, 0)
        small = finish_small_call(four.rows, four.all)
        finish(3, 1)
        finish(1, 1)
        joined_grad, merge_grad = done["joined"], done["merge"]
        down_grad, up_grad = done["mlp"]
        return (
            result.reshape(tokens.shape),
            token_grad.reshape(tokens.shape),
            small[5],
            small[6],
            joined_grad,
            small[7],
            merge_grad,
            small[4],
            small[2],
            small[3],
            up_grad,
            small[0],
            down_grad,
            small[1],
        )

    spread = P(("dp", "group"), None, None)
    return jax.shard_map(
        shards,
        mesh=mesh,
        in_specs=(spread, spread, P(("dp", "group"))) + (P(),) * 12,
        out_specs=(spread, spread) + (P(),) * 12,
        check_vma=False,
    )
```

```python
import math

import jax
import jax.numpy as jnp
from jax import lax
from jax.experimental import pallas as pl
from jax.experimental.pallas import tpu as pltpu
from jax.sharding import PartitionSpec as P

D = 768
HEADS = 12
HEAD_DIM = 64
FF = 3072
PAIRS = HEADS // 2
LANES = 2 * HEAD_DIM
EPS = 1e-06
NEG = -1e30
BF = jnp.bfloat16
F32 = jnp.float32
FACTOR = HEAD_DIM ** (-0.5)
BLOCKS = 16
BROWS = D // BLOCKS
SCALE = 10


def dot(a, b):
    return jnp.dot(a, b, preferred_element_type=F32)


def dot_t(a, b):
    return lax.dot_general(a, b, (((1,), (1,)), ((), ())), preferred_element_type=F32)


def t_dot(a, b):
    return lax.dot_general(a, b, (((0,), (0,)), ((), ())), preferred_element_type=F32)


def stats(x):
    centred = x - jnp.mean(x, axis=-1, keepdims=True)
    rstd = lax.rsqrt(jnp.mean(centred * centred, axis=-1, keepdims=True) + EPS)
    return centred * rstd, rstd


def pin(value):
    return pltpu.with_memory_space_constraint(value, pltpu.HBM)


HERE = pl.BlockSpec(memory_space=pltpu.VMEM)


def held(rows, shape, dtype):
    if rows <= 640:
        return pltpu.VMEM(shape, dtype)
    return jax.ShapeDtypeStruct(shape, dtype)


def vmem(limit):
    return pltpu.CompilerParams(vmem_limit_bytes=limit * 1024 * 1024)


def params(rows=640):
    return vmem(20 if rows <= 640 else 48)


def cost(us):
    return pl.CostEstimate(flops=int(us * SCALE * 1e9), bytes_accessed=1000, transcendentals=0)


def full(shape):
    return pl.BlockSpec(shape, lambda *_: (0,) * len(shape))


def head_masks(rows):
    lane = lax.broadcasted_iota(jnp.int32, (rows, LANES), 1)
    return lane < HEAD_DIM


def stack_heads(pair, low):
    zero = jnp.zeros_like(pair)
    return jnp.concatenate([jnp.where(low, pair, zero), jnp.where(low, zero, pair)], axis=0)


def first_body(
    slots,
    counts_ref,
    tok_hbm,
    cot_hbm,
    wj_hbm,
    wm_hbm,
    g1_ref,
    s1_ref,
    jb_ref,
    mb_ref,
    g2_ref,
    s2_ref,
    normed_ref,
    joined_ref,
    probs_ref,
    mix_ref,
    middle_ref,
    second_ref,
    gout_ref,
    tok_ref,
    cot_ref,
    wj_ref,
    wm_ref,
    sem,
):
    step = pl.program_id(0)
    rows = tok_ref.shape[0]
    items = rows // slots
    span = pl.ds(pl.multiple_of(step * rows, 16), rows)
    tok_copy = pltpu.make_async_copy(tok_hbm.at[span], tok_ref, sem.at[0])
    cot_copy = pltpu.make_async_copy(cot_hbm.at[span], cot_ref, sem.at[1])
    wm_copy = pltpu.make_async_copy(wm_hbm, wm_ref, sem.at[2])
    wj_copies = [
        pltpu.make_async_copy(
            wj_hbm.at[:, pl.ds(third * D, D)], wj_ref.at[third], sem.at[3 + third]
        )
        for third in range(3)
    ]
    tok_copy.start()

    @pl.when(step == 0)
    def _():
        for copy in wj_copies:
            copy.start()

    cot_copy.start()

    @pl.when(step == 0)
    def _():
        wm_copy.start()

    tok_copy.wait()
    xhat, _ = stats(tok_ref[...].astype(F32))
    normed = (xhat * g1_ref[...] + s1_ref[...]).astype(BF)
    normed_ref[...] = normed
    for third in range(3):
        cols = slice(third * D, (third + 1) * D)

        @pl.when(step == 0)
        def _():
            wj_copies[third].wait()

        bias = {0: jb_ref[0:1, :], 2: jb_ref[1:2, :]}.get(third, 0.0)

        def project(part, carry):
            here = pl.ds(pl.multiple_of(part * (rows // 2), 16), rows // 2)
            joined_ref[here, cols] = (dot(normed_ref[here, :], wj_ref[third]) + bias).astype(BF)
            return carry

        lax.fori_loop(0, 2, project, 0)
    cot_copy.wait()
    low = head_masks(slots)
    key_slot = lax.broadcasted_iota(jnp.int32, (slots, 2 * slots), 0)
    row_slot = lax.broadcasted_iota(jnp.int32, (slots, D), 0)

    def one(item, carry):
        count = counts_ref[step * items + item]
        here = pl.ds(pl.multiple_of(item * slots, 16), slots)
        seen = row_slot < count
        cot = cot_ref[here, :]
        gout_ref[here, :] = jnp.where(seen, cot, jnp.zeros_like(cot))
        allowed = key_slot < count
        for pair in range(PAIRS):
            cols = slice(pair * LANES, (pair + 1) * LANES)
            q = stack_heads(joined_ref[here, cols] * BF(FACTOR), low)
            k = joined_ref[here, D + pair * LANES : D + (pair + 1) * LANES]
            v = joined_ref[here, 2 * D + pair * LANES : 2 * D + (pair + 1) * LANES]
            scores = jnp.where(allowed, dot_t(k, q), NEG)
            raised = jnp.exp(scores - jnp.max(scores, axis=0, keepdims=True))
            soft = (raised * (1.0 / jnp.sum(raised, axis=0, keepdims=True))).astype(BF)
            probs_ref[item, pair] = soft
            mixed = t_dot(soft, v)
            mix_ref[here, cols] = jnp.where(low, mixed[:slots], mixed[slots:]).astype(BF)
        return carry

    lax.fori_loop(0, items, one, 0)

    @pl.when(step == 0)
    def _():
        wm_copy.wait()

    def finish(part, carry):
        here = pl.ds(pl.multiple_of(part * (rows // 2), 16), rows // 2)
        middle = tok_ref[here, :].astype(F32) + dot(mix_ref[here, :], wm_ref[...]) + mb_ref[...]
        middle_ref[here, :] = middle
        xhat, _ = stats(middle)
        second_ref[here, :] = (xhat * g2_ref[...] + s2_ref[...]).astype(BF)
        return carry

    lax.fori_loop(0, 2, finish, 0)


def first_call(slots, counts, tok, cot, wj, wm, g1, s1, jb, mb, g2, s2):
    total = tok.shape[0]
    hbm = pl.BlockSpec(memory_space=pltpu.HBM)
    out = lambda width, dt: held(total, (total, width), dt)
    return pl.pallas_call(
        lambda *refs: first_body(slots, *refs),
        grid_spec=pltpu.PrefetchScalarGridSpec(
            num_scalar_prefetch=1,
            grid=(1,),
            in_specs=[hbm] * 4 + [full(a.shape) for a in (g1, s1, jb, mb, g2, s2)],
            out_specs=[HERE] * 7,
            scratch_shapes=[
                pltpu.VMEM((total, D), BF),
                pltpu.VMEM((total, D), BF),
                pltpu.VMEM((3, D, D), BF),
                pltpu.VMEM((D, D), BF),
                pltpu.SemaphoreType.DMA((6,)),
            ],
        ),
        out_shape=[
            out(D, BF),
            out(3 * D, BF),
            held(total, (total // slots, PAIRS, slots, 2 * slots), BF),
            out(D, BF),
            out(D, F32),
            out(D, BF),
            out(D, BF),
        ],
        compiler_params=vmem(20 if total <= 640 else 56),
        cost_estimate=cost(15),
        name="attn_fwd",
    )(*[pin(a) for a in (counts, tok, cot, wj, wm, g1, s1, jb, mb, g2, s2)])


def put_blocks(ref, which, mask, value):
    for k in range(BLOCKS):
        ref[which, k ^ mask] = value[k * BROWS : (k + 1) * BROWS, :].astype(BF)


def quarter_body(parts, ids_ref, sec_ref, gout_ref, up_ref, ub_ref, down_ref, *outs):
    grad_ref, act_ref, gh_ref = outs
    rows = sec_ref.shape[0] // parts

    def one(part, carry):
        here = pl.ds(pl.multiple_of(part * rows, 16), rows)
        hidden = dot(sec_ref[here, :], up_ref[...]) + ub_ref[...]
        grad_act = dot_t(gout_ref[here, :], down_ref[...])
        cdf = 0.5 + 0.5 * lax.erf(hidden * (0.5**0.5))
        act_ref[here, :] = (hidden * cdf).astype(BF)
        slope = cdf + hidden * (jnp.exp(-0.5 * hidden * hidden) * ((2 * math.pi) ** -0.5))
        gh_ref[here, :] = (grad_act * slope).astype(BF)
        return carry

    lax.fori_loop(0, parts, one, 0)
    put_blocks(grad_ref, 0, ids_ref[0], t_dot(act_ref[...], gout_ref[...]))
    put_blocks(grad_ref, 1, ids_ref[1], t_dot(sec_ref[...], gh_ref[...]))


def quarter_call(call, ids, second, gout, up, ub, down):
    total = second.shape[0]
    return pl.pallas_call(
        lambda *refs: quarter_body(2, *refs),
        grid_spec=pltpu.PrefetchScalarGridSpec(
            num_scalar_prefetch=1,
            grid=(1,),
            in_specs=[
                HERE,
                HERE,
                pl.BlockSpec((D, D), lambda i, ids: (0, ids[4 + call])),
                pl.BlockSpec((1, D), lambda i, ids: (0, ids[4 + call])),
                pl.BlockSpec((D, D), lambda i, ids: (ids[4 + call], 0)),
            ],
            out_specs=[HERE] * 3,
        ),
        out_shape=[
            held(total, (2, BLOCKS, BROWS, D), BF),
            held(total, (total, D), BF),
            held(total, (total, D), BF),
        ],
        compiler_params=params(total),
        cost_estimate=cost(4.3),
        name=f"mlp_{call}",
    )(ids, second, gout, up, ub, down)


def collect_body(chunk, ids_ref, *refs):
    acts, ghs = refs[:2], refs[2:4]
    down_ref, up_ref = refs[4:6]
    kept = refs[6:-3]
    outer_ref, g_ref, small_ref = refs[-3:]
    step = pl.program_id(0)
    for at in range(2):

        @pl.when(step == at)
        def _():
            if chunk and not at:
                small_ref[...] = kept[2][...]
            rows = outer_ref.shape[0] // 2

            def part(k, carry):
                here = pl.ds(pl.multiple_of(k * rows, 16), rows)
                outer = dot(acts[at][here, :], down_ref[...])
                g = dot_t(ghs[at][here, :], up_ref[...])
                if at:
                    outer = outer + outer_ref[here, :]
                    g = g + g_ref[here, :]
                elif chunk:
                    outer = outer + kept[0][here, :]
                    g = g + kept[1][here, :]
                outer_ref[here, :] = outer
                g_ref[here, :] = g
                return carry

            lax.fori_loop(0, 2, part, 0)
            small_ref[pl.ds(ids_ref[4 + 2 * chunk + at], 1), :] = jnp.sum(
                ghs[at][...].astype(F32), axis=0, keepdims=True
            )


def collect_call(chunk, ids, acts, ghs, down, up, kept):
    total = acts[0].shape[0]
    return pl.pallas_call(
        lambda *refs: collect_body(chunk, *refs),
        grid_spec=pltpu.PrefetchScalarGridSpec(
            num_scalar_prefetch=1,
            grid=(2,),
            in_specs=[HERE] * 4
            + [
                pl.BlockSpec((D, D), lambda i, ids: (ids[4 + 2 * chunk + i], 0)),
                pl.BlockSpec((D, D), lambda i, ids: (0, ids[4 + 2 * chunk + i])),
            ]
            + [HERE] * (3 if chunk else 0),
            out_specs=[HERE] * 3,
        ),
        out_shape=[
            held(total, (total, D), F32),
            held(total, (total, D), F32),
            held(total, (4, D), F32),
        ],
        compiler_params=vmem(16 if total <= 640 else 56),
        cost_estimate=cost(4.3),
        name=f"mlp_collect_{chunk}",
    )(ids, *acts, *ghs, down, up, *(kept or ()))


def middle_body(
    slots,
    counts_ref,
    outer_ref,
    g_ref,
    mid_ref,
    gout_ref,
    db_ref,
    g2_ref,
    wm_ref,
    result_ref,
    gmid_ref,
    branch_ref,
    gmix_ref,
    small_ref,
):
    items = mid_ref.shape[0] // slots
    row_slot = lax.broadcasted_iota(jnp.int32, (slots, D), 0)

    def one(item, sums):
        here = pl.ds(pl.multiple_of(item * slots, 16), slots)
        seen = row_slot < counts_ref[item]
        middle = mid_ref[here, :]
        total = middle + outer_ref[here, :] + db_ref[...]
        result_ref[here, :] = jnp.where(seen, total, 0.0).astype(BF)
        gout = gout_ref[here, :].astype(F32)
        xhat, rstd = stats(middle)
        g = g_ref[here, :]
        e = g * g2_ref[...]
        mean_e = jnp.mean(e, axis=-1, keepdims=True)
        mean_x = jnp.mean(e * xhat, axis=-1, keepdims=True)
        grad = gout + rstd * (e - mean_e - xhat * mean_x)
        gmid_ref[here, :] = grad
        branch = grad.astype(BF)
        branch_ref[here, :] = branch
        row = lambda a: jnp.sum(a, axis=0, keepdims=True)
        return (
            sums[0] + row(gout),
            sums[1] + row(g * xhat),
            sums[2] + row(g),
            sums[3] + row(branch.astype(F32)),
        )

    zero = jnp.zeros((1, D), F32)
    sums = lax.fori_loop(0, items, one, (zero,) * 4)
    for k in range(4):
        small_ref[k : k + 1, :] = sums[k]
    gmix_ref[...] = dot_t(branch_ref[...], wm_ref[...]).astype(BF)


def middle_call(slots, counts, outer, g, mid, gout, db, g2, wm):
    total = mid.shape[0]
    hbm = jax.ShapeDtypeStruct((total, D), BF)
    return pl.pallas_call(
        lambda *refs: middle_body(slots, *refs),
        grid_spec=pltpu.PrefetchScalarGridSpec(
            num_scalar_prefetch=1,
            grid=(1,),
            in_specs=[HERE] * 4 + [full(db.shape), full(g2.shape), full((D, D))],
            out_specs=[full((total, D))] + [HERE] * 4,
        ),
        out_shape=[
            hbm,
            held(total, (total, D), F32),
            held(total, (total, D), BF),
            held(total, (total, D), BF),
            held(total, (4, D), F32),
        ],
        compiler_params=params(total),
        cost_estimate=cost(3.6),
        name="mlp_back",
    )(counts, outer, g, mid, gout, db, g2, wm)


def attn_back_body(slots, first, joined_ref, probs_ref, gmix_ref, grad_ref):
    low = head_masks(slots)
    items = joined_ref.shape[0] // slots // 2
    group = 3

    def one(at, carry):
        item = first * items + at // (PAIRS // group)
        here = pl.ds(pl.multiple_of(item * slots, 16), slots)
        for step in range(group):
            pair = at % (PAIRS // group) * group + step
            start = pair * LANES
            cols = pl.ds(pl.multiple_of(start, LANES), LANES)
            key_cols = pl.ds(pl.multiple_of(D + start, LANES), LANES)
            value_cols = pl.ds(pl.multiple_of(2 * D + start, LANES), LANES)
            q = stack_heads(joined_ref[here, cols] * BF(FACTOR), low)
            out = stack_heads(gmix_ref[here, cols], low)
            low_soft = probs_ref[item, pair]
            soft = low_soft.astype(F32)
            grad_probs = dot_t(joined_ref[here, value_cols], out)
            mean = jnp.sum(soft * grad_probs, axis=0, keepdims=True)
            scores = (soft * (grad_probs - mean)).astype(BF)
            gq = t_dot(scores, joined_ref[here, key_cols] * BF(FACTOR))
            grad_ref[here, cols] = jnp.where(low, gq[:slots], gq[slots:]).astype(BF)
            grad_ref[here, key_cols] = dot(scores, q).astype(BF)
            grad_ref[here, value_cols] = dot(low_soft, out).astype(BF)
        return carry

    lax.fori_loop(0, items * (PAIRS // group), one, 0)


def attn_back_call(call, slots, joined, probs, gmix, kept):
    total = joined.shape[0]
    args = [joined, probs, gmix]
    aliases = {}
    if kept is not None:
        args.append(kept)
        aliases = {3: 0}
    return pl.pallas_call(
        lambda *refs: attn_back_body(slots, call, *refs[:3], refs[-1]),
        grid=(1,),
        in_specs=[HERE] * len(args),
        out_specs=HERE,
        out_shape=held(total, (total, 3 * D), BF),
        input_output_aliases=aliases,
        compiler_params=vmem(8 if total <= 640 else 48),
        cost_estimate=cost(5.5),
        name=f"attn_bwd_{call}",
    )(*args)


def attn_grad_body(ids_ref, normed_ref, mix_ref, grad_ref, branch_ref, qk_ref, vm_ref):
    def put(ref, which, value):
        mask = ids_ref[which] >> 1
        for k in range(BLOCKS // 2):
            ref[which, k ^ mask] = value[k * BROWS : (k + 1) * BROWS, :].astype(BF)

    normed = normed_ref[...]
    put(qk_ref, 0, t_dot(normed, grad_ref[:, :D]))
    put(qk_ref, 1, t_dot(normed, grad_ref[:, D : 2 * D]))
    put(vm_ref, 0, t_dot(normed, grad_ref[:, 2 * D :]))
    put(vm_ref, 1, t_dot(mix_ref[...], branch_ref[...]))


def attn_grad_call(call, ids, normed, mix, grad, branch):
    total = normed.shape[0]
    half = pl.BlockSpec((total, D // 2), lambda i, ids: (0, ids[8 + call]))
    shape = (2, BLOCKS // 2, BROWS, D)
    return pl.pallas_call(
        attn_grad_body,
        grid_spec=pltpu.PrefetchScalarGridSpec(
            num_scalar_prefetch=1,
            grid=(1,),
            in_specs=[half, half, HERE, HERE],
            out_specs=[HERE] * 2,
        ),
        out_shape=[held(total, shape, BF)] * 2,
        compiler_params=params(total),
        cost_estimate=cost(2.6),
        name=f"attn_grad_{call}",
    )(ids, normed, mix, grad, branch)


def last_body(slots, grad_ref, wj_ref, tok_ref, gmid_ref, g1_ref, out_ref, small_ref, g_ref):
    rows = tok_ref.shape[0]
    items = rows // slots
    half = rows // 2

    def back(part, carry):
        here = pl.ds(pl.multiple_of(part * half, 16), half)
        g_ref[here, :] = dot_t(grad_ref[here, :], wj_ref[...])
        return carry

    lax.fori_loop(0, 2, back, 0)

    def one(item, sums):
        here = pl.ds(pl.multiple_of(item * slots, 16), slots)
        xhat, rstd = stats(tok_ref[here, :].astype(F32))
        g = g_ref[here, :]
        e = g * g1_ref[...]
        mean_e = jnp.mean(e, axis=-1, keepdims=True)
        mean_x = jnp.mean(e * xhat, axis=-1, keepdims=True)
        out_ref[here, :] = (gmid_ref[here, :] + rstd * (e - mean_e - xhat * mean_x)).astype(BF)
        row = lambda a: jnp.sum(a, axis=0, keepdims=True)
        return (
            sums[0] + row(grad_ref[here, :D].astype(F32)),
            sums[1] + row(grad_ref[here, 2 * D :].astype(F32)),
            sums[2] + row(g * xhat),
            sums[3] + row(g),
        )

    zero = jnp.zeros((1, D), F32)
    sums = lax.fori_loop(0, items, one, (zero,) * 4)
    for k in range(4):
        small_ref[k : k + 1, :] = sums[k]
    small_ref[4:8, :] = jnp.zeros((4, D), F32)


def last_call(slots, grad, wj, tok, gmid, g1):
    total = tok.shape[0]
    return pl.pallas_call(
        lambda *refs: last_body(slots, *refs),
        grid=(1,),
        in_specs=[HERE, full(wj.shape), full(tok.shape), HERE, full(g1.shape)],
        out_specs=[full((total, D)), full((8, D))],
        out_shape=[
            jax.ShapeDtypeStruct((total, D), BF),
            jax.ShapeDtypeStruct((8, D), F32),
        ],
        scratch_shapes=[pltpu.VMEM((total, D), F32)],
        compiler_params=params(total),
        cost_estimate=cost(0.001),
        name="first_back",
    )(grad, wj, tok, gmid, g1)


def finish_mlp_body(groups, ids_ref, a_ref, b_ref, *rest):
    for ab, in_ref in enumerate((a_ref, b_ref)):
        mask = ids_ref[ab] & (groups - 1)
        for k in range(groups):
            rest[ab - 2][k * BROWS : (k + 1) * BROWS, :] = in_ref[k ^ mask].astype(F32)


def finish_mlp_call(chunk, which, ids, a, b, kept):
    groups = 4
    steps = BLOCKS // groups

    def place(ab):
        def index(i, ids):
            at = (ids[ab] // groups) ^ i
            quarter = 2 * chunk + (ids[3] ^ which)
            return (quarter * steps + at, 0) if ab == 0 else (at, quarter)

        return index

    in_specs = [pl.BlockSpec((groups, BROWS, D), lambda i, ids: (i, 0, 0))] * 2
    args = [ids, a, b]
    aliases = {}
    if kept is not None:
        in_specs += [pl.BlockSpec(memory_space=pl.ANY)] * 2
        args += list(kept)
        aliases = {3: 0, 4: 1}
    return pl.pallas_call(
        lambda *refs: finish_mlp_body(groups, *refs),
        grid_spec=pltpu.PrefetchScalarGridSpec(
            num_scalar_prefetch=1,
            grid=(steps,),
            in_specs=in_specs,
            out_specs=[pl.BlockSpec((groups * BROWS, D), place(ab)) for ab in range(2)],
        ),
        out_shape=[jax.ShapeDtypeStruct(shape, F32) for shape in ((FF, D), (D, FF))],
        input_output_aliases=aliases,
        compiler_params=params(),
        cost_estimate=cost(0.001),
        name=f"finish_mlp_{chunk}_{which}",
    )(*args)


def finish_attn_body(chunk, ids_ref, a_ref, b_ref, *rest):
    for ab, in_ref in enumerate((a_ref, b_ref)):
        mask = ids_ref[ab] >> 1
        for k in range(BLOCKS // 2):
            block = in_ref[k ^ mask].astype(F32)
            rows = slice(k * BROWS, (k + 1) * BROWS)
            if chunk == 2:
                rest[-1][rows, ab * D : (ab + 1) * D] = block
            else:
                rest[ab - 2][rows, :] = block


def finish_attn_call(chunk, which, ids, a, b, joined, merge):
    half = (D // 2, D)
    top = lambda ids: ids[3] ^ which
    out_specs = [pl.BlockSpec((D // 2, 2 * D), lambda i, ids: (top(ids), 0))]
    shapes = [(D, 3 * D)]
    if chunk == 3:
        out_specs = [
            pl.BlockSpec(half, lambda i, ids: (top(ids), 2)),
            pl.BlockSpec(half, lambda i, ids: (top(ids), 0)),
        ]
        shapes.append((D, D))
    kept = [joined, merge][: len(shapes)]
    aliases = {}
    args = [ids, a, b]
    for at, value in enumerate(kept):
        if value is not None:
            aliases[len(args)] = at
            args.append(value)
    return pl.pallas_call(
        lambda *refs: finish_attn_body(chunk, *refs),
        grid_spec=pltpu.PrefetchScalarGridSpec(
            num_scalar_prefetch=1,
            grid=(1,),
            in_specs=[full(a.shape), full(b.shape)]
            + [pl.BlockSpec(memory_space=pl.ANY)] * (len(args) - 3),
            out_specs=out_specs,
        ),
        out_shape=[jax.ShapeDtypeStruct(s, F32) for s in shapes],
        input_output_aliases=aliases,
        compiler_params=params(),
        cost_estimate=cost(0.001),
        name=f"finish_attn_{chunk}_{which}",
    )(*args)


def finish_small_body(mine_ref, got_ref, *outs):
    mine = mine_ref[...].astype(F32)
    got = got_ref[0].astype(F32)
    total = mine[0:12, :] + mine[12:24, :] + (got[0:12, :] + got[12:24, :])
    for k in range(4):
        outs[0][pl.ds(k * D, D)] = total[k]
    for out, k in zip(outs[1:7], (4, 5, 6, 7, 10, 11)):
        out[...] = total[k]
    outs[7][...] = total[8:10, :]


def finish_small_call(mine, got):
    vector = lambda n: jax.ShapeDtypeStruct((n,), F32)
    shapes = [vector(FF)] + [vector(D)] * 6 + [jax.ShapeDtypeStruct((2, D), F32)]
    return pl.pallas_call(
        finish_small_body,
        grid=(1,),
        in_specs=[
            full(mine.shape),
            pl.BlockSpec((1, BROWS, D), lambda i: (got.shape[0] - 1, 0, 0)),
        ],
        out_specs=[full(s.shape) for s in shapes],
        out_shape=shapes,
        compiler_params=params(),
        cost_estimate=cost(0.001),
        name="finish_small",
    )(mine, got)


def stage_lists(sizes):
    bits = {axis: [(axis, b) for b in range(size.bit_length() - 1)] for axis, size in sizes.items()}
    dp, group = bits["dp"], bits["group"]
    if len(dp) == 2 and len(group) == 3:
        order = group + dp
    else:
        order = [dp[0], group[0], group[-1]] + dp[1:] + group[1:-1]
    return order[0], order[1:3], order[3:]


def add(a, b):
    return (a.astype(F32) + b.astype(F32)).astype(BF)


def bit_of(stage):
    return (lax.axis_index(stage[0]) >> stage[1]) & 1


def tie(*values):
    return lax.optimization_barrier(values)


class Chain:
    def __init__(self):
        self.last = None

    def after(self, value):
        if self.last is None:
            return value
        value, _ = tie(value, self.last)
        return value

    def run(self, step, value):
        out = step(self.after(value))
        self.last = jax.tree.leaves(out)[0]
        return out


class Chunk:
    def __init__(self, sums, chain):
        self.sums = sums
        self.chain = chain
        self.small = None

    def first(self, send):
        self.got = self.sums.swap(send, self.sums.first)

    def pair(self, at, keep=None):
        if keep is not None:
            self.keep = keep
        got = self.chain.after(self.got)
        both = [self.sums.halve(self.keep[ab], got[ab]) for ab in range(2)]
        self.keep = [b[0] for b in both]
        out = [b[1] for b in both]
        self.chain.last = out
        self.got = [self.sums.swap(out[ab], self.sums.stage(ab, at)) for ab in range(2)]

    def tail(self, at, small=None):
        rest = self.sums.rest
        got = self.chain.after(self.got)
        if at == 0:
            mine = jnp.stack([add(self.keep[ab], got[ab]) for ab in range(2)])
            n = mine.shape[1] // 2
            self.keep, out = mine[:, :n], mine[:, n:]
            self.chain.last = out
            self.got = self.sums.swap(out, rest[0])
        elif at == 1:
            mine = add(self.keep, got)
            for stage in rest[1:-1]:
                mine, out = self.sums.split_rows(stage, mine)
                mine = add(mine, self.sums.swap(out, stage))
            self.mine = self.chain.last = mine
            self.small = small
            self.up(mine, rest[-1])
        elif at == 2:
            self.mine = add(self.mine, got)
            self.small_sum()
            for stage in rest[-2:0:-1]:
                self.up(self.mine, stage)
                self.small_sum()
                self.mine = self.sums.join_rows(stage, self.mine, self.got)
            self.chain.last = self.mine
            self.up(self.mine, rest[0])
        else:
            self.mine = jnp.concatenate([self.mine, got], axis=1)
            self.chain.last = self.mine
            self.small_sum()
            self.own = [self.mine[0], self.mine[1]]
            self.ups([self.sums.stage(ab, 1) for ab in range(2)])

    def up(self, value, stage):
        if self.small is None:
            self.got = self.sums.swap(value, stage)
            return
        self.rows = split_small(self.small)
        pad = jnp.zeros((BROWS - self.rows.shape[0], D), BF)
        block = jnp.concatenate([self.rows, pad], axis=0)[None]
        load = value.reshape((-1,) + value.shape[-2:])
        if value.shape[-2] != BROWS:
            load = load.reshape(-1, D)
            load = jnp.concatenate([load, jnp.zeros((-load.shape[0] % BROWS, D), BF)])
            load = load.reshape(-1, BROWS, D)
        self.all = self.sums.swap(jnp.concatenate([load, block], axis=0), stage)
        self.got = self.all[:-1].reshape(-1, D)[: value.size // D].reshape(value.shape)

    def small_sum(self):
        if self.small is not None:
            other = self.all[-1, : self.rows.shape[0]]
            self.small = join_small(self.rows) + join_small(other)

    def ups(self, stages):
        self.up(self.own[0], stages[0])
        self.got = [self.got, self.sums.swap(self.own[1], stages[1])]

    def pair_up(self, at):
        got = self.chain.after(self.got)
        self.own = [jnp.concatenate([self.own[ab], got[ab]]) for ab in range(2)]
        self.chain.last = self.own
        self.small_sum()
        if at:
            self.ups([self.sums.stage(ab, at - 1) for ab in range(2)])
        else:
            self.ups([self.sums.first] * 2)


class Sums:
    def __init__(self, sizes):
        self.sizes = sizes
        self.first, self.pair, self.rest = stage_lists(sizes)

    def swap(self, value, stage):
        axis, bit = stage
        return lax.ppermute(value, axis, [(i, i ^ (1 << bit)) for i in range(self.sizes[axis])])

    def stage(self, ab, at):
        return self.pair[at if ab == 0 else 1 - at]

    def halve(self, mine, got, axis=0):
        n = mine.shape[axis] // 2
        low = lax.slice_in_dim(mine, 0, n, axis=axis), lax.slice_in_dim(got, 0, n, axis=axis)
        high = lax.slice_in_dim(mine, n, 2 * n, axis=axis), lax.slice_in_dim(
            got, n, 2 * n, axis=axis
        )
        return add(*low), add(*high)

    def split_rows(self, stage, mine):
        n = mine.shape[2] // 2
        high = bit_of(stage) == 1
        low_rows, high_rows = mine[:, :, :n], mine[:, :, n:]
        return jnp.where(high, high_rows, low_rows), jnp.where(high, low_rows, high_rows)

    def join_rows(self, stage, mine, got):
        high = bit_of(stage) == 1
        return jnp.concatenate([jnp.where(high, got, mine), jnp.where(high, mine, got)], axis=2)


def split_small(value):
    high = lax.reduce_precision(value, 8, 7)
    return jnp.concatenate([high.astype(BF), (value - high).astype(BF)], axis=0)


def join_small(value):
    n = value.shape[0] // 2
    return value[:n].astype(F32) + value[n:].astype(F32)


def solution(mesh):
    sizes = dict(mesh.shape)
    sums = Sums(sizes)

    def shards(
        tokens,
        cotangent,
        counts,
        first_gain,
        first_shift,
        joined_weight,
        joined_bias,
        merge_weight,
        merge_bias,
        second_gain,
        second_shift,
        up_weight,
        up_bias,
        down_weight,
        down_bias,
    ):
        items, slots, features = tokens.shape
        total = items * slots
        row = lambda a: a.reshape(1, -1)
        tok = tokens.reshape(total, features)
        cot = cotangent.reshape(total, features)
        counts = counts.astype(jnp.int32)
        masks = []
        for two in (sums.pair, sums.pair[::-1]):
            mask = 0
            for stage in list(two) + list(sums.rest[:1]):
                mask = 2 * mask + bit_of(stage)
            masks.append(2 * mask)
        core = bit_of(sums.first)
        other = 1 - core
        ids = jnp.stack(
            [masks[0], masks[1], core, core, other, core, 2 + other, 2 + core, other, core]
        ).astype(jnp.int32)

        normed, joined, probs, mix, middle, second, gout = first_call(
            slots,
            counts,
            tok,
            cot,
            joined_weight,
            merge_weight,
            first_gain,
            first_shift,
            joined_bias,
            merge_bias,
            second_gain,
            second_shift,
        )
        chain = Chain()

        acts, ghs = {}, {}

        def quarter(call):
            def step(ids):
                return quarter_call(
                    call, ids, second, gout, up_weight, row(up_bias), down_weight
                )

            grad, act, gh = chain.run(step, ids)
            acts[call], ghs[call] = act, gh
            return grad

        def collect(chunk, kept):
            pick = (2 * chunk, 2 * chunk + 1)
            return chain.run(
                lambda ids: collect_call(
                    chunk,
                    ids,
                    [acts[call] for call in pick],
                    [ghs[call] for call in pick],
                    down_weight,
                    up_weight,
                    kept,
                ),
                ids,
            )

        done = {}

        def finish(chunk, which):
            part = chunks[chunk].got if which else chunks[chunk].own
            if chunk < 2:
                done["mlp"] = chain.run(
                    lambda a: finish_mlp_call(
                        chunk, which, ids, a, part[1], done.get("mlp")
                    ),
                    part[0],
                )
                return
            if chunk == 3 and which:
                part = chunks[3].all, part[1]
            out = chain.run(
                lambda a: finish_attn_call(
                    chunk, which, ids, a, part[1], done.get("joined"), done.get("merge")
                ),
                part[0],
            )
            done["joined"] = out[0]
            if chunk == 3:
                done["merge"] = out[1]

        chunks = [Chunk(sums, chain) for _ in range(4)]
        one, two, three, four = chunks
        one.first(quarter(0))
        keep1 = quarter(1)
        send2 = quarter(2)
        one.pair(0, keep1)
        kept = collect(0, None)
        keep2 = quarter(3)
        two.first(chain.after(send2))
        outer, g, small_a = collect(1, kept)
        one.pair(1)
        two.pair(0, keep2)
        result, gmid, branch, gmix, small_b = chain.run(
            lambda outer: middle_call(
                slots, counts, outer, g, middle, gout, down_bias, second_gain, merge_weight
            ),
            outer,
        )
        grad_joined = chain.run(
            lambda gmix: attn_back_call(0, slots, joined, probs, gmix, None), gmix
        )
        one.tail(0)
        grad_joined = chain.run(
            lambda gmix: attn_back_call(1, slots, joined, probs, gmix, grad_joined), gmix
        )
        send3, send4 = chain.run(
            lambda ids: attn_grad_call(0, ids, normed, mix, grad_joined, branch), ids
        )
        four.first(chain.after(send4))
        three.first(chain.after(send3))
        two.pair(1)
        one.tail(1)
        keep3, keep4 = chain.run(
            lambda ids: attn_grad_call(1, ids, normed, mix, grad_joined, branch), ids
        )
        three.pair(0, keep3)
        two.tail(0)
        four.pair(0, keep4)
        one.tail(2)
        two.tail(1)
        four.pair(1)
        one.tail(3)
        three.pair(1)
        three.tail(0)
        four.tail(0)
        three.tail(1)
        two.tail(2)
        one.pair_up(1)
        three.tail(2)
        token_grad, small_c = chain.run(
            lambda grad: last_call(slots, grad, joined_weight, tok, gmid, first_gain),
            grad_joined,
        )
        small = jnp.concatenate([small_a, small_b, small_c[:4]], axis=0)
        two.tail(3)
        three.tail(3)
        one.pair_up(0)
        four.tail(1, small)
        three.pair_up(1)
        two.pair_up(1)
        three.pair_up(0)
        four.tail(2)
        four.tail(3)
        finish(0, 0)
        finish(0, 1)
        finish(2, 0)
        four.pair_up(1)
        two.pair_up(0)
        finish(1, 0)
        finish(2, 1)
        four.pair_up(0)
        finish(3, 0)
        small = finish_small_call(four.rows, four.all)
        finish(3, 1)
        finish(1, 1)
        joined_grad, merge_grad = done["joined"], done["merge"]
        down_grad, up_grad = done["mlp"]
        return (
            result.reshape(tokens.shape),
            token_grad.reshape(tokens.shape),
            small[5],
            small[6],
            joined_grad,
            small[7],
            merge_grad,
            small[4],
            small[2],
            small[3],
            up_grad,
            small[0],
            down_grad,
            small[1],
        )

    spread = P(("dp", "group"), None, None)
    return jax.shard_map(
        shards,
        mesh=mesh,
        in_specs=(spread, spread, P(("dp", "group"))) + (P(),) * 12,
        out_specs=(spread, spread) + (P(),) * 12,
        check_vma=False,
    )
```
